32 devices in a mesh: dp: 4 (over y, x), row: 2 (over core), col: 4 (over z).
Axes of the slice: x: 2, y: 2, z: 4, core: 2. Of those that a mesh axis runs over, the one named last changes fastest.
Arguments:
- inputs: bfloat16 [8192, 1536], P('dp', 'row'), may hold values from -6 to 6
- segments: int32 [4, 2048], P('dp'), may hold values from 0 to 5, never falling along the last dimension, each value on 1 to 1024 neighbouring positions
- cotangent: bfloat16 [8192, 1536], P('dp', 'row'), may hold values from -6 to 6
- norm_gain: float32 [1536], P('row'), may hold values from 0.1 to 1.9
- gate_proj: float32 [1536, 48, 64], P('dp', 'col', 'row'), may hold values from -0.15625 to 0.15625
- inner_proj: float32 [1536, 48, 64], P('dp', 'col', 'row'), may hold values from -0.15625 to 0.15625
- state_proj: float32 [1536, 256], P('dp'), may hold values from -0.15625 to 0.15625
- step_proj: float32 [1536, 48], P('dp', 'col'), may hold values from -0.15625 to 0.15625
- conv_inner: float32 [4, 48, 64], P(None, 'col', 'row'), may hold values from -0.5 to 0.5
- bias_inner: float32 [48, 64], P('col', 'row'), may hold values from -0.5 to 0.5
- conv_state: float32 [4, 256], replicated, may hold values from -0.5 to 0.5
- bias_state: float32 [256], replicated, may hold values from -0.5 to 0.5
- step_bias: float32 [48], P('col'), may hold values from -3 to -1
- decay_log: float32 [48], P('col'), may hold values from -2.3 to 1.4
- skip_gain: float32 [48], P('col'), may hold values from 0.25 to 1
- gate_norm: float32 [48, 64], P('col', 'row'), may hold values from 0.1 to 1.9
- out_proj: float32 [1536, 48, 64], P('dp', 'col', 'row'), may hold values from -0.109375 to 0.109375
Outputs:
- output: bfloat16 [8192, 1536], P('dp', 'row')
- grad_inputs: float32 [8192, 1536], P('dp', 'row')
- grad_norm_gain: float32 [1536], P('row')
- grad_gate_proj: float32 [1536, 48, 64], P('dp', 'col', 'row')
- grad_inner_proj: float32 [1536, 48, 64], P('dp', 'col', 'row')
- grad_state_proj: float32 [1536, 256], P('dp')
- grad_step_proj: float32 [1536, 48], P('dp', 'col')
- grad_conv_inner: float32 [4, 48, 64], P(None, 'col', 'row')
- grad_bias_inner: float32 [48, 64], P('col', 'row')
- grad_conv_state: float32 [4, 256], replicated
- grad_bias_state: float32 [256], replicated
- grad_step_bias: float32 [48], P('col')
- grad_decay_log: float32 [48], P('col')
- grad_skip_gain: float32 [48], P('col')
- grad_gate_norm: float32 [48, 64], P('col', 'row')
- grad_out_proj: float32 [1536, 48, 64], P('dp', 'col', 'row')
The draws below stay inside these ranges and needn't reach their ends.
Inputs may be any that keep to these rules, and one draw needn't show every extreme that they name: `segments`: in each sequence the numbers never fall; a document is a run of equal numbers of at most 1024 tokens, and one document has exactly 1024.
All inputs are finite; a program needn't handle non-finite values.
Results may differ from the reference program's by a relative error of at most 0.012.
The reference program's roundings to bfloat16 on the way (of `normed` and `normed_gate`) count: a program that leaves them out, or rounds other values in their place, can miss the bound.
Values may be sent and summed in bfloat16 or wider, within the bound.
A program may use at most 192 MiB of HBM per device.

```python
import math
import jax
import jax.numpy as jnp
import numpy as np
from jax import lax

D = 1536
H = 48
P_SIZE = 64
N = 128
CONV = 4
BLOCK_LEN = 256
SEQ_LEN = 2048
DOCS = 6
MOST = 1024
SEQS = 4
TOKENS = 8192


def steps_of(stream_key, extent, pieces, low, high):
    level, own = 1.0, jax.random.fold_in(stream_key, 6)
    for dim, shards_of in pieces:
        heights = jnp.exp(jax.random.uniform(jax.random.fold_in(own, dim), (shards_of,), jnp.float32, low / len(pieces), high / len(pieces)))
        level = level * jnp.repeat(heights, extent[dim] // shards_of).reshape([-1 if axis == dim else 1 for axis in range(len(extent))])
    return level


def length_profile(number_of, total, most, lean):
    portions = [(1 << 20) // math.isqrt(rank ** lean) + 1 for rank in range(2, number_of + 1)]
    surplus, given = total - most - (number_of - 1), [1] * (number_of - 1)
    while surplus > 0:
        movable = [i for i in range(number_of - 1) if given[i] < most]
        whole, budget = sum([portions[i] for i in movable]), surplus
        for i in movable:
            more = min(most - given[i], max(1, budget * portions[i] // whole), surplus)
            given[i] = given[i] + more
            surplus = surplus - more
    return np.array([most] + given)


def uneven(rng, number_of, total, most, lean):
    if number_of == 2:
        one = jax.random.randint(rng, (), max(1, total - most), min(most, total - 1) + 1)
        return jnp.stack([one, total - one])
    lengths = jnp.asarray(length_profile(number_of, total, most, lean), jnp.int32)
    couples = (number_of - 1) // 2
    source_of, taker = lengths[1:1 + 2 * couples:2], lengths[2:2 + 2 * couples:2]
    margin = jnp.minimum(source_of - 1, most - taker)
    moved = jax.random.randint(jax.random.fold_in(rng, 1), (couples,), 0, 1 << 20) % (margin + 1)
    lengths = lengths.at[1:1 + 2 * couples:2].set(source_of - moved).at[2:2 + 2 * couples:2].set(taker + moved)
    return lengths[jax.random.permutation(jax.random.fold_in(rng, 2), number_of)]


def noise(key, shape, scale, bound, cuts=(), kind=jnp.bfloat16):
    values = scale * jax.random.normal(key, shape, jnp.float32)
    if cuts:
        values = values * steps_of(key, shape, cuts, -0.22, 0.18)
    return jnp.clip(values, -bound, bound).astype(kind)


def setup_inputs(seed: int = 0) -> dict:
    key_of = jax.random.split(jax.random.key(seed), 18)
    inputs = noise(key_of[0], (TOKENS, D), 1.0, 6.0, ((0, 4), (1, 2)))
    segments = jax.vmap(lambda own: jnp.searchsorted(jnp.cumsum(uneven(own, DOCS, SEQ_LEN, MOST, 1)), jnp.arange(SEQ_LEN), side="right"))(jax.random.split(key_of[1], SEQS)).reshape((SEQS, SEQ_LEN)).astype(jnp.int32)
    cotangent = noise(key_of[2], (TOKENS, D), 1.0, 6.0, ((0, 4), (1, 2)))
    norm_gain = jnp.clip(1.0 + 0.18 * jax.random.normal(key_of[3], (D,), jnp.float32), 0.1, 1.9)
    gate_proj = noise(key_of[4], (D, H, P_SIZE), D ** -0.5, 0.15625, ((0, 4), (1, 4), (2, 2)), jnp.float32)
    inner_proj = noise(key_of[5], (D, H, P_SIZE), D ** -0.5, 0.15625, ((0, 4), (1, 4), (2, 2)), jnp.float32)
    state_proj = noise(key_of[6], (D, 2 * N), D ** -0.5, 0.15625, ((0, 4),), jnp.float32)
    step_proj = noise(key_of[7], (D, H), D ** -0.5, 0.15625, ((0, 4), (1, 4)), jnp.float32)
    conv_inner = jnp.clip(jax.random.uniform(key_of[8], (CONV, H, P_SIZE), jnp.float32, -0.5, 0.5) * steps_of(key_of[8], (CONV, H, P_SIZE), ((1, 4), (2, 2)), -0.4, 0.0), -0.5, 0.5)
    bias_inner = jnp.clip(jax.random.uniform(key_of[9], (H, P_SIZE), jnp.float32, -0.5, 0.5) * steps_of(key_of[9], (H, P_SIZE), ((0, 4), (1, 2)), -0.4, 0.0), -0.5, 0.5)
    conv_state = jnp.clip(jax.random.uniform(key_of[10], (CONV, 2 * N), jnp.float32, -0.5, 0.5), -0.5, 0.5)
    bias_state = jnp.clip(jax.random.uniform(key_of[11], (2 * N,), jnp.float32, -0.5, 0.5), -0.5, 0.5)
    step_bias = jnp.clip(-3.0 + 2.0 * jax.random.uniform(key_of[12], (H,), jnp.float32) ** steps_of(key_of[12], (H,), ((0, 4),), -0.2, 0.2), -3.0, -1.0)
    decay_log = jnp.clip(-2.3 + 3.6999999 * jax.random.uniform(key_of[13], (H,), jnp.float32) ** steps_of(key_of[13], (H,), ((0, 4),), -0.2, 0.2), -2.3, 1.4)
    skip_gain = jnp.clip(0.25 + 0.75 * jax.random.uniform(key_of[14], (H,), jnp.float32) ** steps_of(key_of[14], (H,), ((0, 4),), -0.2, 0.2), 0.25, 1.0)
    gate_norm = jnp.clip(1.0 + 0.18 * jax.random.normal(key_of[15], (H, P_SIZE), jnp.float32), 0.1, 1.9)
    out_proj = noise(key_of[16], (D, H, P_SIZE), (H * P_SIZE) ** -0.5, 0.109375, ((0, 4), (1, 4), (2, 2)), jnp.float32)
    return {"inputs": inputs, "segments": segments, "cotangent": cotangent, "norm_gain": norm_gain, "gate_proj": gate_proj, "inner_proj": inner_proj, "state_proj": state_proj, "step_proj": step_proj, "conv_inner": conv_inner, "bias_inner": bias_inner, "conv_state": conv_state, "bias_state": bias_state, "step_bias": step_bias, "decay_log": decay_log, "skip_gain": skip_gain, "gate_norm": gate_norm, "out_proj": out_proj}


EPSILON = 1e-05
HIGHEST = lax.Precision.HIGHEST

@jax.custom_vjp
def low(v):
    return lax.optimization_barrier(v.astype(jnp.bfloat16)).astype(jnp.float32)

@jax.custom_vjp
def low_back(v):
    return v

def low_keep(v):
    return (low(v), None)

def low_pass(kept, grad):
    return (grad,)

def back_keep(v):
    return (v, None)

def back_low(kept, grad):
    return (low(grad),)
low.defvjp(low_keep, low_pass)
low_back.defvjp(back_keep, back_low)

def matmul(left, right):
    return jnp.dot(left, right, precision=HIGHEST)

def conv_act(values, kernel, offset_bias, seg_ids):
    length = values.shape[0]
    width_k = kernel.shape[0]
    summed = offset_bias[None, :] + kernel[width_k - 1][None, :] * values
    for offset in range(1, width_k):
        shifted = jnp.pad(values, ((offset, 0), (0, 0)))[:length]
        earlier = jnp.pad(seg_ids, (offset, 0), constant_values=-1)[:length]
        within = (earlier == seg_ids).astype(jnp.float32)
        summed = summed + kernel[width_k - 1 - offset][None, :] * shifted * within[:, None]
    return jax.nn.silu(summed)

def ssm_gate(gate_pre, inner_act, state_act, step_size, decay_rate, skip_vals, seg_ids, head_count, block_len):
    length = gate_pre.shape[0]
    channels = inner_act.shape[1] // head_count
    state_dim = state_act.shape[1] // 2
    block_count = length // block_len
    inner_heads = inner_act.reshape(length, head_count, channels)
    log_decay = step_size * decay_rate[None, :]
    cumul = jnp.cumsum(log_decay.reshape(block_count, block_len, head_count), axis=1)
    seg_blocks = seg_ids.reshape(block_count, block_len)
    driven = (inner_heads * step_size[:, :, None]).reshape(block_count, block_len, head_count, channels)
    in_blocks = state_act[:, :state_dim].reshape(block_count, block_len, state_dim)
    out_blocks = state_act[:, state_dim:].reshape(block_count, block_len, state_dim)
    positions = jnp.arange(block_len)
    causal = positions[:, None] >= positions[None, :]

    def intra_block(item):
        cum_block, seg_block, in_block, out_block, driven_block = item
        inner_prod = jnp.dot(out_block, in_block.T, precision=HIGHEST)
        gaps = cum_block.T[:, :, None] - cum_block.T[:, None, :]
        allowed = (causal & (seg_block[:, None] == seg_block[None, :]))[None]
        decays = jnp.where(allowed, jnp.exp(jnp.where(allowed, gaps, 0.0)), 0.0)
        mixing = decays * inner_prod[None]
        return jnp.einsum('hts,shp->thp', mixing, driven_block, precision=HIGHEST)
    local_out = lax.map(jax.checkpoint(intra_block), (cumul, seg_blocks, in_blocks, out_blocks, driven))
    last_cum = cumul[:, -1, :]
    last_seg = seg_blocks[:, -1]
    tails = jnp.where(seg_blocks[:, :, None] == last_seg[:, None, None], jnp.exp(last_cum[:, None, :] - cumul), 0.0)
    contrib = jnp.einsum('kqhp,kqn->khpn', driven * tails[..., None], in_blocks, precision=HIGHEST)
    before_seg = jnp.concatenate([jnp.full((1,), -1, seg_ids.dtype), last_seg[:-1]])
    carried = (last_seg == before_seg).astype(jnp.float32)

    def advance(state, item):
        keep_flag, last_block, contrib_block = item
        renewed = keep_flag * jnp.exp(last_block)[:, None, None] * state + contrib_block
        return (renewed, state)
    initial = jnp.zeros((head_count, channels, state_dim), jnp.float32)
    final_state, entering = lax.scan(advance, initial, (carried, last_cum, contrib))
    reach = jnp.where(seg_blocks[:, :, None] == before_seg[:, None, None], jnp.exp(cumul), 0.0)
    from_state = jnp.einsum('kqn,khpn->kqhp', out_blocks, entering, precision=HIGHEST) * reach[..., None]
    mixed = (local_out + from_state).reshape(length, head_count, channels) + skip_vals[None, :, None] * inner_heads
    gated = mixed * jax.nn.silu(gate_pre.reshape(length, head_count, channels))
    return gated.reshape(length, head_count * channels)

def reference(inputs, segments, cotangent, norm_gain, gate_proj, inner_proj, state_proj, step_proj, conv_inner, bias_inner, conv_state, bias_state, step_bias, decay_log, skip_gain, gate_norm, out_proj):
    inner_width = H * P_SIZE

    def forward(rows_all, norm_vals, gate_vals, inner_vals, state_vals, step_vals, conv_in_vals, bias_in_vals, conv_st_vals, bias_st_vals, step_bias_vals, decay_vals, skip_vals, gate_norm_vals, out_vals):
        gate_w = low(gate_vals.reshape(D, inner_width))
        inner_w = low(inner_vals.reshape(D, inner_width))
        state_w = low(state_vals)
        step_w = low(step_vals)
        out_w = low(out_vals.reshape(D, inner_width))
        conv_flat = conv_in_vals.reshape(CONV, inner_width)
        bias_flat = bias_in_vals.reshape(inner_width)
        gain_flat = gate_norm_vals.reshape(inner_width)
        decay_rate = -jnp.exp(decay_vals)

        def one_seq(item):
            rows, seg_ids = item
            scaling = lax.rsqrt(lax.optimization_barrier(jnp.mean(rows * rows, axis=1)) + EPSILON)
            normed = low(rows * scaling[:, None] * norm_vals[None, :])
            gate_pre = low_back(matmul(normed, gate_w))
            inner_pre = low_back(matmul(normed, inner_w))
            state_pre = low_back(matmul(normed, state_w))
            step_pre = low_back(matmul(normed, step_w))
            inner_act = conv_act(inner_pre, conv_flat, bias_flat, seg_ids)
            state_act = conv_act(state_pre, conv_st_vals, bias_st_vals, seg_ids)
            step_size = jax.nn.softplus(step_pre + step_bias_vals[None, :])
            gated = ssm_gate(gate_pre, inner_act, state_act, step_size, decay_rate, skip_vals, seg_ids, H, BLOCK_LEN)
            gate_scale = lax.rsqrt(lax.optimization_barrier(jnp.mean(gated * gated, axis=1)) + EPSILON)
            normed_gate = low(gated * gate_scale[:, None] * gain_flat[None, :])
            return rows + matmul(normed_gate, out_w.T)
        return lax.map(jax.checkpoint(one_seq), (rows_all.reshape(SEQS, SEQ_LEN, D), segments))
    primal = (inputs.astype(jnp.float32), norm_gain, gate_proj, inner_proj, state_proj, step_proj, conv_inner, bias_inner, conv_state, bias_state, step_bias, decay_log, skip_gain, gate_norm, out_proj)
    result, backward = jax.vjp(forward, *primal)
    grads = backward(cotangent.astype(jnp.float32).reshape(SEQS, SEQ_LEN, D))
    return (result.reshape(TOKENS, D).astype(jnp.bfloat16), grads[0].reshape(TOKENS, D), grads[1], grads[2], grads[3], grads[4], grads[5], grads[6], grads[7], grads[8], grads[9], grads[10], grads[11], grads[12], grads[13], grads[14])
```

```python
import functools

import jax
import jax.numpy as jnp
from jax import lax
from jax.experimental import pallas as pl
from jax.experimental.pallas import tpu as pltpu
from jax.sharding import PartitionSpec as P

H = 48
P_SIZE = 64
BLOCK_LEN = 256
EPSILON = 1e-05
NEG = -1e30
STEP_ROWS = 16
F32 = jnp.float32
BF16 = jnp.bfloat16
HIGHEST = lax.Precision.HIGHEST


def dot_nn(left, right, precision=None):
    return lax.dot_general(
        left, right, (((1,), (0,)), ((), ())), preferred_element_type=F32, precision=precision
    )


def dot_nt(left, right, precision=None):
    return lax.dot_general(
        left, right, (((1,), (1,)), ((), ())), preferred_element_type=F32, precision=precision
    )


def dot_tn(left, right):
    return lax.dot_general(left, right, (((0,), (0,)), ((), ())), preferred_element_type=F32)


def sigmoid(values):
    return 0.5 * jnp.tanh(0.5 * values) + 0.5


def softplus(values):
    return jnp.maximum(values, 0.0) + jnp.log1p(jnp.exp(-jnp.abs(values)))


def lane_fold(values):
    total = values[:, :128]
    for at in range(128, values.shape[1], 128):
        total = total + values[:, at : at + 128]
    return total


def columns_of(rows):
    padded = jnp.concatenate([rows, jnp.zeros((128 - rows.shape[0], rows.shape[1]), F32)], axis=0)
    return padded.T


def block_rows(dims, step_pre, hrow, aux):
    q = step_pre.shape[1]
    step_arg = step_pre + hrow[:, 0:1]
    step = softplus(step_arg)
    log_decay = step * hrow[:, 1:2]
    source = lax.broadcasted_iota(jnp.int32, (q, q), 0)
    target = lax.broadcasted_iota(jnp.int32, (q, q), 1)
    upper = (source <= target).astype(F32)
    cumul = dot_nn(log_decay, upper, HIGHEST)
    last = cumul[:, q - 1 : q]
    cols = columns_of(jnp.concatenate([cumul, aux], axis=0))
    return step_arg, step, cumul, last, cols


def forward_kernel(
    dims,
    x_own,
    x_sib,
    c_own,
    c_sib,
    weights,
    gain_own,
    gain_sib,
    aux_ref,
    conv_ref,
    chan_ref,
    hrow_ref,
    normed_own,
    normed_sib,
    pre_out,
    arg_out,
    gate_out,
    step_out,
    mixed_out,
    dng_out,
    state_out,
    stats_out,
    out_own,
    out_sib,
    prev,
    state,
    act_scr,
):
    nh, pc, ns, width = dims
    inner = nh * pc
    conv_rows = inner + 2 * ns
    gate_at = conv_rows + STEP_ROWS
    out_at = gate_at + inner
    half = x_own.shape[1]
    q = x_own.shape[0]
    row_at = lax.axis_index("row")
    own_at = pl.multiple_of(row_at * half, 128)
    sib_at = pl.multiple_of((1 - row_at) * half, 128)

    @pl.when(pl.program_id(0) == 0)
    def _():
        prev[...] = jnp.zeros_like(prev)
        state[...] = jnp.zeros_like(state)

    xo = x_own[...].astype(F32)
    xs = x_sib[...].astype(F32)
    squares = jnp.sum(xo * xo, axis=1, keepdims=True) + jnp.sum(xs * xs, axis=1, keepdims=True)
    scaling = lax.rsqrt(squares / width + EPSILON)
    no = (xo * scaling * gain_own[...]).astype(BF16)
    nsib = (xs * scaling * gain_sib[...]).astype(BF16)
    normed_own[...] = no
    normed_sib[...] = nsib
    pre = dot_nt(weights[0:out_at, pl.ds(own_at, half)], no) + dot_nt(
        weights[0:out_at, pl.ds(sib_at, half)], nsib
    )
    values = pre[0:conv_rows]
    step_pre = pre[conv_rows:gate_at]
    gate = pre[gate_at:out_at]
    pre_out[...] = values
    step_out[...] = step_pre
    gate_out[...] = gate
    aux = aux_ref[...]
    conv = conv_ref[...]
    joined = jnp.concatenate([prev[...], values], axis=1)
    arg = conv[:, 4:5] + conv[:, 3:4] * values
    for offset in range(1, 4):
        arg = arg + conv[:, 3 - offset : 4 - offset] * (
            aux[offset - 1 : offset] * joined[:, 128 - offset : 128 - offset + q]
        )
    prev[...] = values[:, q - 128 :]
    arg_out[...] = arg
    act = arg * sigmoid(arg)
    act_scr[...] = act[0:inner]
    in_low = act[inner : inner + ns].astype(BF16)
    out_low = act[inner + ns :].astype(BF16)

    _, step, cumul, last, cols = block_rows(dims, step_pre, hrow_ref[...], aux)
    source = lax.broadcasted_iota(jnp.int32, (q, q), 0)
    target = lax.broadcasted_iota(jnp.int32, (q, q), 1)
    seg_col = cols[:, STEP_ROWS + 3 : STEP_ROWS + 4]
    bias = jnp.where((source <= target) & (seg_col == aux[3:4]), 0.0, NEG)
    pairs = dot_tn(in_low, out_low)
    entering = state[...]
    state_out[0] = entering
    from_state = dot_nn(entering.astype(BF16), out_low)
    reach = aux[4:5] * jnp.exp(cumul)
    tails = aux[5:6] * jnp.exp(last - cumul)
    keep = aux[6:7, 0:1] * jnp.exp(last)
    hq = q // 2
    gain = chan_ref[...]
    squares_row = jnp.zeros((1, q), F32)
    tail_parts = []
    for h in range(nh):
        lo = h * pc
        x_h = act_scr[lo : lo + pc]
        u_h = (x_h * step[h : h + 1]).astype(BF16)
        tail_parts.append((x_h * (step[h : h + 1] * tails[h : h + 1])).astype(BF16))
        col = cols[:, h : h + 1]
        row = cumul[h : h + 1]
        top = (jnp.exp((row - col[:hq]) + bias[:hq]) * pairs[:hq]).astype(BF16)
        low = (jnp.exp((row[:, hq:] - col[hq:]) + bias[hq:, hq:]) * pairs[hq:, hq:]).astype(BF16)
        y_top = dot_nn(u_h[:, :hq], top)
        y_low = dot_nn(u_h[:, hq:], low)
        y_h = jnp.concatenate([y_top[:, :hq], y_top[:, hq:] + y_low], axis=1)
        y_h = y_h + from_state[lo : lo + pc] * reach[h : h + 1]
        mixed_out[lo : lo + pc] = y_h + gain[lo : lo + pc, 1:2] * x_h
    contrib = dot_nt(jnp.concatenate(tail_parts, axis=0), in_low)
    for h in range(nh):
        lo = h * pc
        state[lo : lo + pc] = keep[h : h + 1] * entering[lo : lo + pc] + contrib[lo : lo + pc]
    gated = mixed_out[...] * (gate * sigmoid(gate))
    squares_row = jnp.sum(gated * gated, axis=0, keepdims=True)
    weighted = gated * gain[:, 0:1]
    low = weighted.astype(BF16)
    out_own[...] = dot_tn(low, weights[out_at:, pl.ds(own_at, half)]).astype(BF16)
    out_sib[...] = dot_tn(low, weights[out_at:, pl.ds(sib_at, half)]).astype(BF16)
    dng = dot_nt(weights[out_at:, pl.ds(own_at, half)], c_own[...]) + dot_nt(
        weights[out_at:, pl.ds(sib_at, half)], c_sib[...]
    )
    dng_out[...] = dng
    dot_row = jnp.sum(dng * weighted, axis=0, keepdims=True)
    stats_out[...] = jnp.concatenate([squares_row, dot_row, jnp.zeros((6, q), F32)], axis=0)


def backward_kernel(
    dims,
    normed_own,
    normed_sib,
    c_own,
    c_sib,
    weights,
    aux_ref,
    conv_ref,
    chan_ref,
    hrow_ref,
    pre_ref,
    arg_ref,
    gate_ref,
    step_ref,
    mixed_ref,
    dng_ref,
    state_ref,
    stats_ref,
    dn_own,
    dn_sib,
    grad_w,
    conv_grad,
    chan_grad,
    head_grad,
    after,
    d_state,
    acc_w,
    acc_conv,
    acc_chan,
    acc_head,
    du_scr,
    low_scr,
):
    nh, pc, ns, width = dims
    inner = nh * pc
    conv_rows = inner + 2 * ns
    gate_at = conv_rows + STEP_ROWS
    out_at = gate_at + inner
    half = c_own.shape[1]
    q = c_own.shape[0]
    inner_width = H * P_SIZE
    row_at = lax.axis_index("row")
    own_at = pl.multiple_of(row_at * half, 128)
    sib_at = pl.multiple_of((1 - row_at) * half, 128)

    @pl.when(pl.program_id(0) == 0)
    def _():
        after[...] = jnp.zeros_like(after)
        d_state[...] = jnp.zeros_like(d_state)
        acc_w[...] = jnp.zeros_like(acc_w)
        acc_conv[...] = jnp.zeros_like(acc_conv)
        acc_chan[...] = jnp.zeros_like(acc_chan)
        acc_head[...] = jnp.zeros_like(acc_head)

    aux = aux_ref[...]
    conv = conv_ref[...]
    chan = chan_ref[...]
    hrow = hrow_ref[...]
    stats = stats_ref[...]
    gate_scale = lax.rsqrt(stats[0:1] / inner_width + EPSILON)
    pull = gate_scale * gate_scale * gate_scale * stats[1:2] / inner_width
    gate = gate_ref[...]
    sig = sigmoid(gate)
    silu = gate * sig
    mixed = mixed_ref[...]
    gated = mixed * silu
    dng_scaled = dng_ref[...] * gate_scale
    d_gated = chan[:, 0:1] * dng_scaled - gated * pull
    acc_chan[0] += lane_fold(dng_scaled * gated)
    normed_gate = (gated * (gate_scale * chan[:, 0:1])).astype(BF16)
    acc_w[out_at:, pl.ds(own_at, half)] += dot_nn(normed_gate, c_own[...])
    acc_w[out_at:, pl.ds(sib_at, half)] += dot_nn(normed_gate, c_sib[...])
    grad_mixed = d_gated * silu
    low_scr[gate_at:out_at] = (d_gated * mixed * (sig * (1.0 + gate * (1.0 - sig)))).astype(BF16)

    arg = arg_ref[...]
    sig_arg = sigmoid(arg)
    act = arg * sig_arg
    act_slope = sig_arg * (1.0 + arg * (1.0 - sig_arg))
    x_all = act[0:inner]
    in_low = act[inner : inner + ns].astype(BF16)
    out_low = act[inner + ns :].astype(BF16)
    step_arg, step, cumul, last, cols = block_rows(dims, step_ref[...], hrow, aux)
    t_at = lax.broadcasted_iota(jnp.int32, (q, q), 0)
    s_at = lax.broadcasted_iota(jnp.int32, (q, q), 1)
    seg_col = cols[:, STEP_ROWS + 3 : STEP_ROWS + 4]
    bias = jnp.where((s_at <= t_at) & (seg_col == aux[3:4]), 0.0, NEG)
    pairs = dot_tn(out_low, in_low)
    reach = aux[4:5] * jnp.exp(cumul)
    tails = aux[5:6] * jnp.exp(last - cumul)
    keep = aux[6:7, 0:1] * jnp.exp(last)
    entering = state_ref[0]
    d_next = d_state[...]
    from_next = dot_nn(d_next.astype(BF16), in_low)
    hq = q // 2
    acc_chan[1] += lane_fold(grad_mixed * x_all)
    d_pairs_top = jnp.zeros((hq, hq), F32)
    d_pairs_low = jnp.zeros((hq, q), F32)
    reach_parts, tail_parts = [], []
    row_sums, col_sums, x_sums, tail_sums, carry_sums = [], [], [], [], []
    for h in range(nh):
        lo = h * pc
        x_h = x_all[lo : lo + pc]
        u_h = x_h * step[h : h + 1]
        u_low = u_h.astype(BF16)
        g_h = grad_mixed[lo : lo + pc]
        g_low = g_h.astype(BF16)
        col = cols[:, h : h + 1]
        row = cumul[h : h + 1]
        reach_parts.append((g_h * reach[h : h + 1]).astype(BF16))
        tail_parts.append((u_h * tails[h : h + 1]).astype(BF16))
        e_top = jnp.exp((col[:hq] - row[:, :hq]) + bias[:hq, :hq])
        e_low = jnp.exp((col[hq:] - row) + bias[hq:])
        m_top = (e_top * pairs[:hq, :hq]).astype(BF16)
        m_low = (e_low * pairs[hq:]).astype(BF16)
        dm_top = dot_tn(g_low[:, :hq], u_low[:, :hq])
        dm_low = dot_tn(g_low[:, hq:], u_low)
        d_pairs_top = d_pairs_top + dm_top * e_top
        d_pairs_low = d_pairs_low + dm_low * e_low
        du_top = dot_nn(g_low[:, :hq], m_top)
        du_low = dot_nn(g_low[:, hq:], m_low)
        du_local = jnp.concatenate([du_top + du_low[:, :hq], du_low[:, hq:]], axis=1)
        du_next = from_next[lo : lo + pc] * tails[h : h + 1]
        du = du_local + du_next
        du_scr[lo : lo + pc] = du * step[h : h + 1] + chan[lo : lo + pc, 1:2] * g_h
        u_round = u_low.astype(F32)
        y_h = mixed[lo : lo + pc] - chan[lo : lo + pc, 1:2] * x_h
        row_sums.append(jnp.sum(g_low.astype(F32) * y_h, axis=0, keepdims=True))
        next_sum = jnp.sum(u_round * du_next, axis=0, keepdims=True)
        col_sums.append(jnp.sum(u_round * du_local, axis=0, keepdims=True) + next_sum)
        tail_sums.append(next_sum)
        x_sums.append(jnp.sum(x_h * du, axis=0, keepdims=True))
        flow = jnp.sum(entering[lo : lo + pc] * d_next[lo : lo + pc], axis=0, keepdims=True)
        carry_sums.append(flow)
    pad_rows = [jnp.zeros((STEP_ROWS - nh, q), F32)]
    row_sum = jnp.concatenate(row_sums + pad_rows, axis=0)
    col_sum = jnp.concatenate(col_sums + pad_rows, axis=0)
    tail_sum = jnp.concatenate(tail_sums + pad_rows, axis=0)
    x_sum = jnp.concatenate(x_sums + pad_rows, axis=0)
    carry = jnp.concatenate(carry_sums + [jnp.zeros((STEP_ROWS - nh, ns), F32)], axis=0)
    d_last = jnp.sum(tail_sum, axis=1, keepdims=True) + keep * jnp.sum(
        carry, axis=1, keepdims=True
    )
    later = (t_at >= s_at).astype(F32)
    d_log = dot_nn(row_sum - col_sum, later, HIGHEST) + d_last
    d_step = x_sum + hrow[:, 1:2] * d_log
    d_step_arg = d_step * sigmoid(step_arg)
    acc_head[0] += lane_fold(d_step_arg)
    acc_head[1] += lane_fold(step * d_log)
    low_scr[conv_rows:gate_at] = d_step_arg.astype(BF16)

    g_reach = jnp.concatenate(reach_parts, axis=0)
    u_tail = jnp.concatenate(tail_parts, axis=0)
    d_top_low = d_pairs_top.astype(BF16)
    d_low_low = d_pairs_low.astype(BF16)
    d_out = dot_tn(entering.astype(BF16), g_reach)
    d_out = d_out + jnp.concatenate(
        [dot_nt(in_low[:, :hq], d_top_low), dot_nt(in_low, d_low_low)], axis=1
    )
    d_in = dot_tn(d_next.astype(BF16), u_tail) + dot_nn(out_low[:, hq:], d_low_low)
    d_in_top = dot_nn(out_low[:, :hq], d_top_low)
    d_in = jnp.concatenate([d_in[:, :hq] + d_in_top, d_in[:, hq:]], axis=1)
    d_enter = dot_nt(g_reach, out_low)
    for h in range(nh):
        lo = h * pc
        d_state[lo : lo + pc] = keep[h : h + 1] * d_next[lo : lo + pc] + d_enter[lo : lo + pc]

    err = jnp.concatenate([du_scr[...], d_in, d_out], axis=0) * act_slope
    values = pre_ref[...]
    d_pre = conv[:, 3:4] * err
    acc_conv[3] += lane_fold(err * values)
    acc_conv[4] += lane_fold(err)
    for offset in range(1, 4):
        masked = err * aux[offset - 1 : offset]
        joined = jnp.concatenate([masked, after[offset - 1]], axis=1)
        shifted = joined[:, offset : offset + q]
        after[offset - 1] = masked[:, :128]
        d_pre = d_pre + conv[:, 3 - offset : 4 - offset] * shifted
        acc_conv[3 - offset] += lane_fold(shifted * values)
    low_scr[0:conv_rows] = d_pre.astype(BF16)
    low = low_scr[...]
    dn_own[...] = dot_tn(low, weights[0:out_at, pl.ds(own_at, half)]).astype(BF16)
    dn_sib[...] = dot_tn(low, weights[0:out_at, pl.ds(sib_at, half)]).astype(BF16)
    acc_w[0:out_at, pl.ds(own_at, half)] += dot_nn(low, normed_own[...])
    acc_w[0:out_at, pl.ds(sib_at, half)] += dot_nn(low, normed_sib[...])

    @pl.when(pl.program_id(0) == pl.num_programs(0) - 1)
    def _():
        grad_w[...] = acc_w[...].astype(BF16)

        def gather_columns(ref, count):
            lanes = lax.broadcasted_iota(jnp.int32, ref.shape[1:], 1)
            total = jnp.zeros(ref.shape[1:], F32)
            for at in range(count):
                total = jnp.where(lanes == at, jnp.sum(ref[at], axis=1, keepdims=True), total)
            return total

        conv_grad[...] = gather_columns(acc_conv, 5)
        chan_grad[...] = gather_columns(acc_chan, 2)
        head_grad[...] = gather_columns(acc_head, 2)


def per_device(
    inputs,
    segments,
    cotangent,
    norm_gain,
    gate_proj,
    inner_proj,
    state_proj,
    step_proj,
    conv_inner,
    bias_inner,
    conv_state,
    bias_state,
    step_bias,
    decay_log,
    skip_gain,
    gate_norm,
    out_proj,
):
    length, half = inputs.shape
    row_count = lax.axis_size("row")
    col_count = lax.axis_size("col")
    col_at = lax.axis_index("col")
    width = half * row_count
    share, nh, pc = gate_proj.shape
    inner = nh * pc
    state_width = state_proj.shape[1]
    ns = state_width // 2
    conv_rows = inner + state_width
    gate_at = conv_rows + STEP_ROWS
    out_at = gate_at + inner
    rows = out_at + inner
    q = BLOCK_LEN
    blocks = length // q
    swap = [(0, 1), (1, 0)]
    dims = (nh, pc, ns, width)

    def channel_rows(w):
        return jnp.transpose(w, (1, 2, 0)).reshape(inner, share)

    stacked = jnp.concatenate(
        [
            channel_rows(inner_proj),
            state_proj.T,
            jnp.pad(step_proj.T, ((0, STEP_ROWS - nh), (0, 0))),
            channel_rows(gate_proj),
            channel_rows(out_proj),
        ],
        axis=0,
    ).astype(BF16)
    weights = lax.all_gather(stacked, "dp", axis=1, tiled=True)
    x_sib = lax.ppermute(inputs, "row", swap)
    c_sib = lax.ppermute(cotangent, "row", swap)
    gain_own = norm_gain[None, :]
    gain_sib = lax.ppermute(gain_own, "row", swap)

    seg = segments[0]
    seg_blocks = seg.reshape(blocks, q)
    last_seg = seg_blocks[:, -1]
    before_seg = jnp.concatenate([jnp.full((1,), -1, seg.dtype), last_seg[:-1]])
    shift_masks = [
        (jnp.pad(seg, (offset, 0), constant_values=-1)[:length] == seg).astype(F32)
        for offset in range(1, 4)
    ]
    flags = [
        seg.astype(F32),
        (seg_blocks == before_seg[:, None]).astype(F32).reshape(length),
        (seg_blocks == last_seg[:, None]).astype(F32).reshape(length),
        jnp.repeat((last_seg == before_seg).astype(F32), q),
        jnp.zeros((length,), F32),
    ]
    aux = jnp.stack(shift_masks + flags, axis=0)
    conv_cols = jnp.concatenate(
        [conv_inner.reshape(4, inner), conv_state], axis=1
    )
    bias_row = jnp.concatenate([bias_inner.reshape(inner), bias_state])[None]
    conv_par = jnp.concatenate([conv_cols, bias_row, jnp.zeros((3, conv_rows), F32)], axis=0).T
    chan_par = jnp.concatenate(
        [
            gate_norm.reshape(1, inner),
            jnp.repeat(skip_gain, pc)[None],
            jnp.zeros((6, inner), F32),
        ],
        axis=0,
    ).T
    decay_rate = -jnp.exp(decay_log)
    head_par = jnp.pad(
        jnp.stack([step_bias, decay_rate], axis=1), ((0, STEP_ROWS - nh), (0, 6))
    )

    def token_block(order):
        return pl.BlockSpec((q, half), lambda i: (order(i), 0))

    def lane_block(count, order):
        return pl.BlockSpec((count, q), lambda i: (0, order(i)))

    def whole(*shape):
        return pl.BlockSpec(shape, lambda i: (0,) * len(shape), pipeline_mode=pl.Buffered(1))

    def up(i):
        return i

    def down(i):
        return blocks - 1 - i

    sds = jax.ShapeDtypeStruct
    forward = pl.pallas_call(
        functools.partial(forward_kernel, dims),
        name="forward",
        grid=(blocks,),
        in_specs=[
            token_block(up),
            token_block(up),
            token_block(up),
            token_block(up),
            whole(rows, width),
            whole(1, half),
            whole(1, half),
            lane_block(8, up),
            whole(conv_rows, 8),
            whole(inner, 8),
            whole(STEP_ROWS, 8),
        ],
        out_specs=[
            token_block(up),
            token_block(up),
            lane_block(conv_rows, up),
            lane_block(conv_rows, up),
            lane_block(inner, up),
            lane_block(STEP_ROWS, up),
            lane_block(inner, up),
            lane_block(inner, up),
            pl.BlockSpec((1, inner, ns), lambda i: (i, 0, 0)),
            lane_block(8, up),
            token_block(up),
            token_block(up),
        ],
        out_shape=[
            sds((length, half), BF16),
            sds((length, half), BF16),
            sds((conv_rows, length), F32),
            sds((conv_rows, length), F32),
            sds((inner, length), F32),
            sds((STEP_ROWS, length), F32),
            sds((inner, length), F32),
            sds((inner, length), F32),
            sds((blocks, inner, ns), F32),
            sds((8, length), F32),
            sds((length, half), BF16),
            sds((length, half), BF16),
        ],
        scratch_shapes=[
            pltpu.VMEM((conv_rows, 128), F32),
            pltpu.VMEM((inner, ns), F32),
            pltpu.VMEM((inner, q), F32),
        ],
        compiler_params=pltpu.CompilerParams(vmem_limit_bytes=56 << 20),
        cost_estimate=pl.CostEstimate(
            flops=2 * length * width * (out_at + 2 * inner),
            bytes_accessed=50 << 20,
            transcendentals=nh * length * q,
        ),
    )
    (
        normed_own,
        normed_sib,
        pre_vals,
        arg_vals,
        gate_vals,
        step_vals,
        mixed_vals,
        dng_vals,
        states,
        stats,
        out_own,
        out_sib,
    ) = forward(
        inputs,
        x_sib,
        cotangent,
        c_sib,
        weights,
        gain_own,
        gain_sib,
        aux,
        conv_par,
        chan_par,
        head_par,
    )
    stats = lax.psum(stats, ("row", "col"))

    out_recv = lax.ppermute(out_sib, "row", swap)
    out_pair = (out_own.astype(F32) + out_recv.astype(F32)).astype(BF16)
    out_sum = lax.psum(out_pair, "col")
    gate_scale = lax.rsqrt(stats[0] / (H * P_SIZE) + EPSILON)
    plain = inputs.astype(F32)
    output = (plain + gate_scale[:, None] * out_sum.astype(F32)).astype(BF16)

    backward = pl.pallas_call(
        functools.partial(backward_kernel, dims),
        name="backward",
        grid=(blocks,),
        in_specs=[
            token_block(down),
            token_block(down),
            token_block(down),
            token_block(down),
            whole(rows, width),
            lane_block(8, down),
            whole(conv_rows, 8),
            whole(inner, 8),
            whole(STEP_ROWS, 8),
            lane_block(conv_rows, down),
            lane_block(conv_rows, down),
            lane_block(inner, down),
            lane_block(STEP_ROWS, down),
            lane_block(inner, down),
            lane_block(inner, down),
            pl.BlockSpec((1, inner, ns), lambda i: (down(i), 0, 0)),
            lane_block(8, down),
        ],
        out_specs=[
            token_block(down),
            token_block(down),
            whole(rows, width),
            whole(conv_rows, 128),
            whole(inner, 128),
            whole(STEP_ROWS, 128),
        ],
        out_shape=[
            sds((length, half), BF16),
            sds((length, half), BF16),
            sds((rows, width), BF16),
            sds((conv_rows, 128), F32),
            sds((inner, 128), F32),
            sds((STEP_ROWS, 128), F32),
        ],
        scratch_shapes=[
            pltpu.VMEM((3, conv_rows, 128), F32),
            pltpu.VMEM((inner, ns), F32),
            pltpu.VMEM((rows, width), F32),
            pltpu.VMEM((5, conv_rows, 128), F32),
            pltpu.VMEM((2, inner, 128), F32),
            pltpu.VMEM((2, STEP_ROWS, 128), F32),
            pltpu.VMEM((inner, q), F32),
            pltpu.VMEM((out_at, q), BF16),
        ],
        compiler_params=pltpu.CompilerParams(vmem_limit_bytes=60 << 20),
        cost_estimate=pl.CostEstimate(
            flops=4 * length * width * (out_at + inner),
            bytes_accessed=60 << 20,
            transcendentals=nh * length * q,
        ),
    )
    dn_own, dn_sib, grad_w, conv_grad, chan_grad, head_grad = backward(
        normed_own,
        normed_sib,
        cotangent,
        c_sib,
        weights,
        aux,
        conv_par,
        chan_par,
        head_par,
        pre_vals,
        arg_vals,
        gate_vals,
        step_vals,
        mixed_vals,
        dng_vals,
        states,
        stats,
    )

    dn_recv = lax.ppermute(dn_sib, "row", swap)
    dn_pair = (dn_own.astype(F32) + dn_recv.astype(F32)).astype(BF16)
    d_half = lax.psum(dn_pair, "col").astype(F32)
    x_sib_plain = x_sib.astype(F32)
    squares = jnp.sum(plain * plain, axis=1) + jnp.sum(x_sib_plain * x_sib_plain, axis=1)
    scaling = lax.rsqrt(squares / width + EPSILON)
    weighted = d_half * gain_own
    dot_own = jnp.sum(weighted * plain, axis=1)
    input_dot = dot_own + lax.ppermute(dot_own, "row", swap)
    grad_inputs = (
        cotangent.astype(F32)
        + scaling[:, None] * weighted
        - plain * (scaling**3 * input_dot / width)[:, None]
    )
    grad_norm = jnp.sum(d_half * plain * scaling[:, None], axis=0)

    grads = lax.psum_scatter(grad_w, "dp", scatter_dimension=1, tiled=True).astype(F32)
    head_wide = head_grad[:nh, :2].T
    skip_part = jnp.sum(chan_grad[:, 1].reshape(nh, pc), axis=1)[None]
    heads = jnp.concatenate([head_wide, skip_part], axis=0)

    def widen(part):
        wide = jnp.zeros((col_count,) + part.shape, F32)
        return lax.dynamic_update_slice_in_dim(wide, part[None], col_at, 0)

    step_wide = widen(grads[conv_rows : conv_rows + nh])
    head_all = widen(heads)
    grad_norm, conv_sum, gate_gain_sum, head_all = lax.psum(
        (grad_norm, conv_grad[:, :5].T, chan_grad[:, 0], head_all), "dp"
    )
    state_sum, step_wide, conv_state_sum, head_all = lax.psum(
        (grads[inner:conv_rows], step_wide, conv_sum[:, inner:], head_all), ("row", "col")
    )

    def take(wide):
        return lax.dynamic_slice_in_dim(wide, col_at, 1, 0)[0]

    step_grad = take(step_wide)
    head_own = take(head_all)

    def feature_rows(w):
        return jnp.transpose(w.reshape(nh, pc, share), (2, 0, 1))

    return (
        output,
        grad_inputs,
        grad_norm,
        feature_rows(grads[gate_at:out_at]),
        feature_rows(grads[0:inner]),
        state_sum.T,
        step_grad.T,
        conv_sum[:4, :inner].reshape(4, nh, pc),
        conv_sum[4, :inner].reshape(nh, pc),
        conv_state_sum[:4],
        conv_state_sum[4],
        head_own[0],
        head_own[1] * decay_rate,
        head_own[2],
        gate_gain_sum.reshape(nh, pc),
        feature_rows(grads[out_at:]),
    )


def solution(mesh):
    return jax.shard_map(
        per_device,
        mesh=mesh,
        in_specs=(
            P("dp", "row"),
            P("dp", None),
            P("dp", "row"),
            P("row"),
            P("dp", "col", "row"),
            P("dp", "col", "row"),
            P("dp", None),
            P("dp", "col"),
            P(None, "col", "row"),
            P("col", "row"),
            P(),
            P(),
            P("col"),
            P("col"),
            P("col"),
            P("col", "row"),
            P("dp", "col", "row"),
        ),
        out_specs=(
            P("dp", "row"),
            P("dp", "row"),
            P("row"),
            P("dp", "col", "row"),
            P("dp", "col", "row"),
            P("dp", None),
            P("dp", "col"),
            P(None, "col", "row"),
            P("col", "row"),
            P(),
            P(),
            P("col"),
            P("col"),
            P("col"),
            P("col", "row"),
            P("dp", "col", "row"),
        ),
        check_vma=False,
    )
```

```python
import functools

import jax
import jax.numpy as jnp
from jax import lax
from jax.experimental import pallas as pl
from jax.experimental.pallas import tpu as pltpu
from jax.sharding import PartitionSpec as P

H = 48
P_SIZE = 64
BLOCK_LEN = 256
EPSILON = 1e-05
NEG = -1e30
STEP_ROWS = 16
F32 = jnp.float32
BF16 = jnp.bfloat16
HIGHEST = lax.Precision.HIGHEST


def dot_nn(left, right, precision=None):
    return lax.dot_general(
        left, right, (((1,), (0,)), ((), ())), preferred_element_type=F32, precision=precision
    )


def dot_nt(left, right, precision=None):
    return lax.dot_general(
        left, right, (((1,), (1,)), ((), ())), preferred_element_type=F32, precision=precision
    )


def dot_tn(left, right):
    return lax.dot_general(left, right, (((0,), (0,)), ((), ())), preferred_element_type=F32)


def sigmoid(values):
    return 0.5 * jnp.tanh(0.5 * values) + 0.5


def softplus(values):
    return jnp.maximum(values, 0.0) + jnp.log1p(jnp.exp(-jnp.abs(values)))


def lane_fold(values):
    total = values[:, :128]
    for at in range(128, values.shape[1], 128):
        total = total + values[:, at : at + 128]
    return total


def columns_of(rows):
    padded = jnp.concatenate([rows, jnp.zeros((128 - rows.shape[0], rows.shape[1]), F32)], axis=0)
    return padded.T


def block_rows(dims, step_pre, hrow, aux):
    q = step_pre.shape[1]
    step_arg = step_pre + hrow[:, 0:1]
    step = softplus(step_arg)
    log_decay = step * hrow[:, 1:2]
    source = lax.broadcasted_iota(jnp.int32, (q, q), 0)
    target = lax.broadcasted_iota(jnp.int32, (q, q), 1)
    upper = (source <= target).astype(F32)
    cumul = dot_nn(log_decay, upper, HIGHEST)
    last = cumul[:, q - 1 : q]
    cols = columns_of(jnp.concatenate([cumul, aux], axis=0))
    return step_arg, step, cumul, last, cols


MESH = pl.DeviceIdType.MESH


def send(src, dst, sems, at, **device):
    return pltpu.make_async_remote_copy(
        src_ref=src,
        dst_ref=dst,
        send_sem=sems[0].at[at],
        recv_sem=sems[1].at[at],
        device_id=device,
        device_id_type=MESH,
    )


def group_peers(row_count, col_count):
    row_at, col_at = lax.axis_index("row"), lax.axis_index("col")
    return [
        dict(row=lax.rem(row_at + j, row_count), col=lax.rem(col_at + k, col_count))
        for k in range(col_count)
        for j in range(row_count)
        if (j, k) != (0, 0)
    ]


def greet(peers):
    barrier = pltpu.get_barrier_semaphore()
    for peer in peers:
        pl.semaphore_signal(barrier, inc=1, device_id=peer, device_id_type=MESH)
    pl.semaphore_wait(barrier, len(peers))


def add_low(left, right):
    return (left.astype(F32) + right.astype(F32)).astype(BF16)


class Chain:
    def __init__(self, own, sib, bufs, sems, result, q, place):
        self.place = place
        self.own, self.sib, self.result, self.q = own, sib, result, q
        self.first, self.pair, self.cross = bufs
        self.sems = sems
        self.row_at, self.col_at = lax.axis_index("row"), lax.axis_index("col")
        self.is_outer = (self.col_at == 0) | (self.col_at == 3)
        self.inward = 1 + lax.div(self.col_at, 2)
        self.outward = 3 * lax.div(self.col_at, 2)

    def exchange(self, b):
        return send(
            self.sib.at[b], self.first.at[b], self.sems[0], b, row=1 - self.row_at
        )

    def to_inner(self, b):
        return send(self.first.at[b], self.pair.at[b], self.sems[1], b, col=self.inward)

    def across(self, b):
        return send(self.pair.at[b], self.cross.at[b], self.sems[2], b, col=3 - self.col_at)

    def rows(self, b):
        return self.result.at[pl.ds(pl.multiple_of(self.place(b) * self.q, self.q), self.q)]

    def to_outer(self, b):
        return send(self.cross.at[b], self.rows(b), self.sems[3], b, col=self.outward)

    def keep(self, b):
        return pltpu.make_async_copy(self.cross.at[b], self.rows(b), self.sems[4].at[b])

    def stage_first(self, b):
        self.exchange(b).wait_recv()
        self.first[b] = add_low(self.own[b], self.first[b])

        @pl.when(self.is_outer)
        def _():
            self.to_inner(b).start()

    def stage_pair(self, b):
        @pl.when(~self.is_outer)
        def _():
            self.to_inner(b).wait_recv()
            self.pair[b] = add_low(self.first[b], self.pair[b])
            self.across(b).start()

    def stage_cross(self, b):
        @pl.when(~self.is_outer)
        def _():
            self.across(b).wait_recv()
            self.cross[b] = add_low(self.pair[b], self.cross[b])
            self.keep(b).start()
            self.to_outer(b).start()

    def progress(self, i):
        for lag, stage in ((1, self.stage_first), (2, self.stage_pair), (3, self.stage_cross)):

            @pl.when(i >= lag)
            def _():
                stage(i - lag)

    def drain(self, blocks):
        for extra in range(3):
            for lag, stage in ((1, self.stage_first), (2, self.stage_pair), (3, self.stage_cross)):
                if lag > extra:
                    stage(blocks + extra - lag)

        def finish(b, _):
            self.exchange(b).wait_send()

            @pl.when(self.is_outer)
            def _():
                self.to_inner(b).wait_send()
                self.to_outer(b).wait_recv()

            @pl.when(~self.is_outer)
            def _():
                self.across(b).wait_send()
                self.to_outer(b).wait_send()
                self.keep(b).wait()

            return 0

        lax.fori_loop(0, blocks, finish, 0)


def chain_scratch(blocks, q, half):
    dma = pltpu.SemaphoreType.DMA
    buffers = [pltpu.VMEM((blocks, q, half), BF16) for _ in range(5)]
    return buffers + [dma((blocks,)) for _ in range(9)]


def chain_of(refs, result, q, place):
    own, sib, first, pair, cross = refs[:5]
    sems = [tuple(refs[5 + 2 * k : 7 + 2 * k]) for k in range(4)] + [refs[13]]
    return Chain(own, sib, (first, pair, cross), sems, result, q, place)


class Gather:
    def __init__(self, mine, whole, sems, groups):
        self.mine, self.whole, self.groups = mine, whole, groups
        self.sems = sems
        at = lax.axis_index("dp")
        self.at = at
        self.near = at + 1 - 2 * lax.rem(at, 2)
        self.far = lax.rem(at + 2, 4)
        self.share = mine.shape[1]

    def part(self, shard, lo, hi):
        return self.whole.at[
            lo:hi, pl.ds(pl.multiple_of(shard * self.share, 128), self.share)
        ]

    def direct(self, g, to_near):
        lo, _, hi = self.groups[g]
        return send(
            self.mine.at[lo:hi],
            self.part(self.at, lo, hi),
            self.sems[0 if to_near else 1],
            g,
            dp=self.near if to_near else self.far,
        )

    def onward(self, g, from_near):
        lo, mid, hi = self.groups[g]
        lo, hi = (lo, mid) if from_near else (mid, hi)
        part = self.part(self.near if from_near else self.far, lo, hi)
        return send(
            part,
            part,
            self.sems[2 if from_near else 3],
            g,
            dp=self.far if from_near else self.near,
        )

    def start(self):
        for g in range(len(self.groups)):
            self.direct(g, True).start()
            self.direct(g, False).start()

    def take(self, g):
        self.direct(g, True).wait_recv()
        self.onward(g, True).start()
        self.direct(g, False).wait_recv()
        self.onward(g, False).start()
        self.onward(g, True).wait_recv()
        self.onward(g, False).wait_recv()

    def finish(self):
        for g in range(len(self.groups)):
            for which in (True, False):
                self.direct(g, which).wait_send()
                self.onward(g, which).wait_send()


def forward_kernel(
    dims,
    mesh_dims,
    x_own,
    c_own,
    x_any,
    c_any,
    weights_in,
    gain_own,
    aux_ref,
    conv_ref,
    chan_ref,
    hrow_ref,
    normed_own,
    normed_sib,
    pre_out,
    arg_out,
    gate_out,
    step_out,
    mixed_out,
    dng_out,
    state_out,
    stats_out,
    out_total,
    c_out,
    w_out,
    prev,
    state,
    act_scr,
    x_scr,
    c_scr,
    gain_sib,
    stats_scr,
    swap_sems,
    local_sems,
    stat_sems,
    *rest,
):
    nh, pc, ns, width = dims
    row_count, col_count, gathers = mesh_dims
    step_at = pl.program_id(0)
    blocks = x_scr.shape[0]
    inner = nh * pc
    conv_rows = inner + 2 * ns
    gate_at = conv_rows + STEP_ROWS
    out_at = gate_at + inner
    half = x_own.shape[1]
    q = x_own.shape[0]
    row_at, col_at = lax.axis_index("row"), lax.axis_index("col")
    own_at = pl.multiple_of(row_at * half, 128)
    sib_at = pl.multiple_of((1 - row_at) * half, 128)
    sib = dict(row=1 - row_at)
    me = row_at * col_count + col_at
    peers = group_peers(row_count, col_count)
    chain = chain_of(rest[:14], out_total, q, lambda b: b)

    def token_rows(ref, b):
        return ref.at[pl.ds(pl.multiple_of(b * q, q), q)]

    def swap(which, b):
        src, dst = ((x_any, x_scr), (c_any, c_scr))[which]
        sems = (swap_sems.at[2 * which], swap_sems.at[2 * which + 1])
        return send(token_rows(src, b), dst.at[b], sems, b, **sib)

    gain_swap = send(
        gain_own, gain_sib, (swap_sems.at[0], swap_sems.at[1]), blocks, **sib
    )

    def keep_cot(b):
        return pltpu.make_async_copy(c_scr.at[b], token_rows(c_out, b), local_sems.at[b])

    def stat_copy(k):
        return send(
            stats_scr.at[me], stats_scr.at[me], (stat_sems.at[0], stat_sems.at[1]), k, **peers[k]
        )

    if gathers:
        weights = rest[14]
        bounds = ((0, 336, gate_at), (gate_at, gate_at + 192, out_at), (out_at, out_at + 192, out_at + inner))
        gather = Gather(weights_in, weights, [tuple(rest[15 + 2 * k : 17 + 2 * k]) for k in range(4)], bounds)
        others = [dict(dp=gather.near), dict(dp=gather.far)]
        keep_weights = pltpu.make_async_copy(weights, w_out, local_sems.at[blocks])
    else:
        weights, gather, others = weights_in, None, []

    @pl.when(step_at == 0)
    def _():
        greet(peers + others)
        if gathers:
            gather.start()
        gain_swap.start()
        for b in range(blocks):
            swap(0, b).start()
            swap(1, b).start()
        prev[...] = jnp.zeros_like(prev)
        state[...] = jnp.zeros_like(state)
        if gathers:
            share = weights_in.shape[1]
            mine_at = pl.multiple_of(lax.axis_index("dp") * share, 128)
            weights[:, pl.ds(mine_at, share)] = weights_in[...]
        gain_swap.wait_recv()
        if gathers:
            gather.take(0)

    swap(0, step_at).wait_recv()
    xo = x_own[...].astype(F32)
    xs = x_scr[step_at].astype(F32)
    squares = jnp.sum(xo * xo, axis=1, keepdims=True) + jnp.sum(xs * xs, axis=1, keepdims=True)
    scaling = lax.rsqrt(squares / width + EPSILON)
    no = (xo * scaling * gain_own[...]).astype(BF16)
    nsib = (xs * scaling * gain_sib[...]).astype(BF16)
    normed_own[...] = no
    normed_sib[...] = nsib
    pre = dot_nt(weights[0:gate_at, pl.ds(own_at, half)], no) + dot_nt(
        weights[0:gate_at, pl.ds(sib_at, half)], nsib
    )
    values = pre[0:conv_rows]
    step_pre = pre[conv_rows:gate_at]
    pre_out[...] = values
    step_out[...] = step_pre
    aux = aux_ref[...]
    conv = conv_ref[...]
    joined = jnp.concatenate([prev[...], values], axis=1)
    arg = conv[:, 4:5] + conv[:, 3:4] * values
    for offset in range(1, 4):
        arg = arg + conv[:, 3 - offset : 4 - offset] * (
            aux[offset - 1 : offset] * joined[:, 128 - offset : 128 - offset + q]
        )
    prev[...] = values[:, q - 128 :]
    arg_out[...] = arg
    act = arg * sigmoid(arg)
    act_scr[...] = act[0:inner]
    in_low = act[inner : inner + ns].astype(BF16)
    out_low = act[inner + ns :].astype(BF16)

    _, step, cumul, last, cols = block_rows(dims, step_pre, hrow_ref[...], aux)
    source = lax.broadcasted_iota(jnp.int32, (q, q), 0)
    target = lax.broadcasted_iota(jnp.int32, (q, q), 1)
    seg_col = cols[:, STEP_ROWS + 3 : STEP_ROWS + 4]
    bias = jnp.where((source <= target) & (seg_col == aux[3:4]), 0.0, NEG)
    pairs = dot_tn(in_low, out_low)
    entering = state[...]
    state_out[0] = entering
    from_state = dot_nn(entering.astype(BF16), out_low)
    reach = aux[4:5] * jnp.exp(cumul)
    tails = aux[5:6] * jnp.exp(last - cumul)
    keep = aux[6:7, 0:1] * jnp.exp(last)
    hq = q // 2
    gain = chan_ref[...]
    squares_row = jnp.zeros((1, q), F32)
    tail_parts = []
    for h in range(nh):
        lo = h * pc
        x_h = act_scr[lo : lo + pc]
        u_h = (x_h * step[h : h + 1]).astype(BF16)
        tail_parts.append((x_h * (step[h : h + 1] * tails[h : h + 1])).astype(BF16))
        col = cols[:, h : h + 1]
        row = cumul[h : h + 1]
        top = (jnp.exp((row - col[:hq]) + bias[:hq]) * pairs[:hq]).astype(BF16)
        low = (jnp.exp((row[:, hq:] - col[hq:]) + bias[hq:, hq:]) * pairs[hq:, hq:]).astype(BF16)
        y_top = dot_nn(u_h[:, :hq], top)
        y_low = dot_nn(u_h[:, hq:], low)
        y_h = jnp.concatenate([y_top[:, :hq], y_top[:, hq:] + y_low], axis=1)
        y_h = y_h + from_state[lo : lo + pc] * reach[h : h + 1]
        mixed_out[lo : lo + pc] = y_h + gain[lo : lo + pc, 1:2] * x_h
    chain.progress(step_at)
    contrib = dot_nt(jnp.concatenate(tail_parts, axis=0), in_low)
    for h in range(nh):
        lo = h * pc
        state[lo : lo + pc] = keep[h : h + 1] * entering[lo : lo + pc] + contrib[lo : lo + pc]
    if gathers:

        @pl.when(step_at == 0)
        def _():
            gather.take(1)

    gate = dot_nt(weights[gate_at:out_at, pl.ds(own_at, half)], no) + dot_nt(
        weights[gate_at:out_at, pl.ds(sib_at, half)], nsib
    )
    gate_out[...] = gate
    gated = mixed_out[...] * (gate * sigmoid(gate))
    squares_row = jnp.sum(gated * gated, axis=0, keepdims=True)
    weighted = gated * gain[:, 0:1]
    low = weighted.astype(BF16)
    if gathers:

        @pl.when(step_at == 0)
        def _():
            gather.take(2)
            keep_weights.start()

    chain.sib[step_at] = dot_tn(low, weights[out_at:, pl.ds(sib_at, half)]).astype(BF16)
    chain.exchange(step_at).start()
    chain.own[step_at] = dot_tn(low, weights[out_at:, pl.ds(own_at, half)]).astype(BF16)
    swap(1, step_at).wait_recv()
    keep_cot(step_at).start()
    dng = dot_nt(weights[out_at:, pl.ds(own_at, half)], c_own[...]) + dot_nt(
        weights[out_at:, pl.ds(sib_at, half)], c_scr[step_at]
    )
    dng_out[...] = dng
    dot_row = jnp.sum(dng * weighted, axis=0, keepdims=True)
    stats_scr[me, pl.ds(step_at, 1)] = squares_row
    stats_scr[me, pl.ds(blocks + step_at, 1)] = dot_row

    @pl.when(step_at == blocks - 1)
    def _():
        for k in range(len(peers)):
            stat_copy(k).start()
        chain.drain(blocks)
        for k in range(len(peers)):
            stat_copy(k).wait()
        total = stats_scr[0]
        for k in range(1, len(peers) + 1):
            total = total + stats_scr[k]
        stats_out[...] = total
        gain_swap.wait_send()
        for b in range(blocks):
            swap(0, b).wait_send()
            swap(1, b).wait_send()
            keep_cot(b).wait()
        if gathers:
            gather.finish()
            keep_weights.wait()


def backward_kernel(
    dims,
    mesh_dims,
    normed_own,
    normed_sib,
    c_own,
    c_sib,
    weights,
    aux_ref,
    conv_ref,
    chan_ref,
    hrow_ref,
    pre_ref,
    arg_ref,
    gate_ref,
    step_ref,
    mixed_ref,
    dng_ref,
    state_ref,
    stats_ref,
    dn_total,
    grad_w,
    conv_grad,
    chan_grad,
    head_grad,
    after,
    d_state,
    acc_w,
    acc_conv,
    acc_chan,
    acc_head,
    du_scr,
    low_scr,
    *rest,
):
    nh, pc, ns, width = dims
    row_count, col_count, _ = mesh_dims
    step_at = pl.program_id(0)
    blocks = stats_ref.shape[0] // 2
    inner = nh * pc
    conv_rows = inner + 2 * ns
    gate_at = conv_rows + STEP_ROWS
    out_at = gate_at + inner
    half = c_own.shape[1]
    q = c_own.shape[0]
    inner_width = H * P_SIZE
    row_at = lax.axis_index("row")
    own_at = pl.multiple_of(row_at * half, 128)
    sib_at = pl.multiple_of((1 - row_at) * half, 128)

    chain = chain_of(rest, dn_total, q, lambda b: blocks - 1 - b)
    block_at = blocks - 1 - step_at

    @pl.when(step_at == 0)
    def _():
        greet(
            [dict(row=1 - row_at), dict(col=lax.rem(chain.col_at + 1, col_count)), dict(col=lax.rem(chain.col_at + 3, col_count))]
        )
        after[...] = jnp.zeros_like(after)
        d_state[...] = jnp.zeros_like(d_state)
        acc_w[...] = jnp.zeros_like(acc_w)
        acc_conv[...] = jnp.zeros_like(acc_conv)
        acc_chan[...] = jnp.zeros_like(acc_chan)
        acc_head[...] = jnp.zeros_like(acc_head)

    aux = aux_ref[...]
    conv = conv_ref[...]
    chan = chan_ref[...]
    hrow = hrow_ref[...]
    gate_scale = lax.rsqrt(stats_ref[pl.ds(block_at, 1)] / inner_width + EPSILON)
    gate_dot = stats_ref[pl.ds(blocks + block_at, 1)]
    pull = gate_scale * gate_scale * gate_scale * gate_dot / inner_width
    gate = gate_ref[...]
    sig = sigmoid(gate)
    silu = gate * sig
    mixed = mixed_ref[...]
    gated = mixed * silu
    dng_scaled = dng_ref[...] * gate_scale
    d_gated = chan[:, 0:1] * dng_scaled - gated * pull
    acc_chan[0] += lane_fold(dng_scaled * gated)
    normed_gate = (gated * (gate_scale * chan[:, 0:1])).astype(BF16)
    acc_w[out_at:, pl.ds(own_at, half)] += dot_nn(normed_gate, c_own[...])
    acc_w[out_at:, pl.ds(sib_at, half)] += dot_nn(normed_gate, c_sib[...])
    grad_mixed = d_gated * silu
    low_scr[gate_at:out_at] = (d_gated * mixed * (sig * (1.0 + gate * (1.0 - sig)))).astype(BF16)

    arg = arg_ref[...]
    sig_arg = sigmoid(arg)
    act = arg * sig_arg
    act_slope = sig_arg * (1.0 + arg * (1.0 - sig_arg))
    x_all = act[0:inner]
    in_low = act[inner : inner + ns].astype(BF16)
    out_low = act[inner + ns :].astype(BF16)
    step_arg, step, cumul, last, cols = block_rows(dims, step_ref[...], hrow, aux)
    t_at = lax.broadcasted_iota(jnp.int32, (q, q), 0)
    s_at = lax.broadcasted_iota(jnp.int32, (q, q), 1)
    seg_col = cols[:, STEP_ROWS + 3 : STEP_ROWS + 4]
    bias = jnp.where((s_at <= t_at) & (seg_col == aux[3:4]), 0.0, NEG)
    pairs = dot_tn(out_low, in_low)
    reach = aux[4:5] * jnp.exp(cumul)
    tails = aux[5:6] * jnp.exp(last - cumul)
    keep = aux[6:7, 0:1] * jnp.exp(last)
    entering = state_ref[0]
    d_next = d_state[...]
    from_next = dot_nn(d_next.astype(BF16), in_low)
    hq = q // 2
    acc_chan[1] += lane_fold(grad_mixed * x_all)
    d_pairs_top = jnp.zeros((hq, hq), F32)
    d_pairs_low = jnp.zeros((hq, q), F32)
    reach_parts, tail_parts = [], []
    row_sums, col_sums, x_sums, tail_sums, carry_sums = [], [], [], [], []
    for h in range(nh):
        lo = h * pc
        x_h = x_all[lo : lo + pc]
        u_h = x_h * step[h : h + 1]
        u_low = u_h.astype(BF16)
        g_h = grad_mixed[lo : lo + pc]
        g_low = g_h.astype(BF16)
        col = cols[:, h : h + 1]
        row = cumul[h : h + 1]
        reach_parts.append((g_h * reach[h : h + 1]).astype(BF16))
        tail_parts.append((u_h * tails[h : h + 1]).astype(BF16))
        e_top = jnp.exp((col[:hq] - row[:, :hq]) + bias[:hq, :hq])
        e_low = jnp.exp((col[hq:] - row) + bias[hq:])
        m_top = (e_top * pairs[:hq, :hq]).astype(BF16)
        m_low = (e_low * pairs[hq:]).astype(BF16)
        dm_top = dot_tn(g_low[:, :hq], u_low[:, :hq])
        dm_low = dot_tn(g_low[:, hq:], u_low)
        d_pairs_top = d_pairs_top + dm_top * e_top
        d_pairs_low = d_pairs_low + dm_low * e_low
        du_top = dot_nn(g_low[:, :hq], m_top)
        du_low = dot_nn(g_low[:, hq:], m_low)
        du_local = jnp.concatenate([du_top + du_low[:, :hq], du_low[:, hq:]], axis=1)
        du_next = from_next[lo : lo + pc] * tails[h : h + 1]
        du = du_local + du_next
        du_scr[lo : lo + pc] = du * step[h : h + 1] + chan[lo : lo + pc, 1:2] * g_h
        u_round = u_low.astype(F32)
        y_h = mixed[lo : lo + pc] - chan[lo : lo + pc, 1:2] * x_h
        row_sums.append(jnp.sum(g_low.astype(F32) * y_h, axis=0, keepdims=True))
        next_sum = jnp.sum(u_round * du_next, axis=0, keepdims=True)
        col_sums.append(jnp.sum(u_round * du_local, axis=0, keepdims=True) + next_sum)
        tail_sums.append(next_sum)
        x_sums.append(jnp.sum(x_h * du, axis=0, keepdims=True))
        flow = jnp.sum(entering[lo : lo + pc] * d_next[lo : lo + pc], axis=0, keepdims=True)
        carry_sums.append(flow)
    chain.progress(step_at)
    pad_rows = [jnp.zeros((STEP_ROWS - nh, q), F32)]
    row_sum = jnp.concatenate(row_sums + pad_rows, axis=0)
    col_sum = jnp.concatenate(col_sums + pad_rows, axis=0)
    tail_sum = jnp.concatenate(tail_sums + pad_rows, axis=0)
    x_sum = jnp.concatenate(x_sums + pad_rows, axis=0)
    carry = jnp.concatenate(carry_sums + [jnp.zeros((STEP_ROWS - nh, ns), F32)], axis=0)
    d_last = jnp.sum(tail_sum, axis=1, keepdims=True) + keep * jnp.sum(
        carry, axis=1, keepdims=True
    )
    later = (t_at >= s_at).astype(F32)
    d_log = dot_nn(row_sum - col_sum, later, HIGHEST) + d_last
    d_step = x_sum + hrow[:, 1:2] * d_log
    d_step_arg = d_step * sigmoid(step_arg)
    acc_head[0] += lane_fold(d_step_arg)
    acc_head[1] += lane_fold(step * d_log)
    low_scr[conv_rows:gate_at] = d_step_arg.astype(BF16)

    g_reach = jnp.concatenate(reach_parts, axis=0)
    u_tail = jnp.concatenate(tail_parts, axis=0)
    d_top_low = d_pairs_top.astype(BF16)
    d_low_low = d_pairs_low.astype(BF16)
    d_out = dot_tn(entering.astype(BF16), g_reach)
    d_out = d_out + jnp.concatenate(
        [dot_nt(in_low[:, :hq], d_top_low), dot_nt(in_low, d_low_low)], axis=1
    )
    d_in = dot_tn(d_next.astype(BF16), u_tail) + dot_nn(out_low[:, hq:], d_low_low)
    d_in_top = dot_nn(out_low[:, :hq], d_top_low)
    d_in = jnp.concatenate([d_in[:, :hq] + d_in_top, d_in[:, hq:]], axis=1)
    d_enter = dot_nt(g_reach, out_low)
    for h in range(nh):
        lo = h * pc
        d_state[lo : lo + pc] = keep[h : h + 1] * d_next[lo : lo + pc] + d_enter[lo : lo + pc]

    err = jnp.concatenate([du_scr[...], d_in, d_out], axis=0) * act_slope
    values = pre_ref[...]
    d_pre = conv[:, 3:4] * err
    acc_conv[3] += lane_fold(err * values)
    acc_conv[4] += lane_fold(err)
    for offset in range(1, 4):
        masked = err * aux[offset - 1 : offset]
        joined = jnp.concatenate([masked, after[offset - 1]], axis=1)
        shifted = joined[:, offset : offset + q]
        after[offset - 1] = masked[:, :128]
        d_pre = d_pre + conv[:, 3 - offset : 4 - offset] * shifted
        acc_conv[3 - offset] += lane_fold(shifted * values)
    low_scr[0:conv_rows] = d_pre.astype(BF16)
    low = low_scr[...]
    chain.sib[step_at] = dot_tn(low, weights[0:out_at, pl.ds(sib_at, half)]).astype(BF16)
    chain.exchange(step_at).start()
    chain.own[step_at] = dot_tn(low, weights[0:out_at, pl.ds(own_at, half)]).astype(BF16)
    acc_w[0:out_at, pl.ds(own_at, half)] += dot_nn(low, normed_own[...])
    acc_w[0:out_at, pl.ds(sib_at, half)] += dot_nn(low, normed_sib[...])

    @pl.when(pl.program_id(0) == pl.num_programs(0) - 1)
    def _():
        grad_w[...] = acc_w[...].astype(BF16)

        def gather_columns(ref, count):
            lanes = lax.broadcasted_iota(jnp.int32, ref.shape[1:], 1)
            total = jnp.zeros(ref.shape[1:], F32)
            for at in range(count):
                total = jnp.where(lanes == at, jnp.sum(ref[at], axis=1, keepdims=True), total)
            return total

        conv_grad[...] = gather_columns(acc_conv, 5)
        chan_grad[...] = gather_columns(acc_chan, 2)
        head_grad[...] = gather_columns(acc_head, 2)
        chain.drain(blocks)


def per_device(
    inputs,
    segments,
    cotangent,
    norm_gain,
    gate_proj,
    inner_proj,
    state_proj,
    step_proj,
    conv_inner,
    bias_inner,
    conv_state,
    bias_state,
    step_bias,
    decay_log,
    skip_gain,
    gate_norm,
    out_proj,
):
    length, half = inputs.shape
    row_count = lax.axis_size("row")
    col_count = lax.axis_size("col")
    col_at = lax.axis_index("col")
    width = half * row_count
    share, nh, pc = gate_proj.shape
    inner = nh * pc
    state_width = state_proj.shape[1]
    ns = state_width // 2
    conv_rows = inner + state_width
    gate_at = conv_rows + STEP_ROWS
    out_at = gate_at + inner
    rows = out_at + inner
    q = BLOCK_LEN
    blocks = length // q
    swap = [(0, 1), (1, 0)]
    dims = (nh, pc, ns, width)

    def channel_rows(w):
        return jnp.transpose(w, (1, 2, 0)).reshape(inner, share)

    stacked = jnp.concatenate(
        [
            channel_rows(inner_proj),
            state_proj.T,
            jnp.pad(step_proj.T, ((0, STEP_ROWS - nh), (0, 0))),
            channel_rows(gate_proj),
            channel_rows(out_proj),
        ],
        axis=0,
    ).astype(BF16)
    gathers = lax.axis_size("dp") == 4 and share % 128 == 0
    if not gathers:
        stacked = lax.all_gather(stacked, "dp", axis=1, tiled=True)
    gain_own = norm_gain[None, :]
    mesh_dims = (row_count, col_count, gathers)
    group = row_count * col_count

    seg = segments[0]
    seg_blocks = seg.reshape(blocks, q)
    last_seg = seg_blocks[:, -1]
    before_seg = jnp.concatenate([jnp.full((1,), -1, seg.dtype), last_seg[:-1]])
    shift_masks = [
        (jnp.pad(seg, (offset, 0), constant_values=-1)[:length] == seg).astype(F32)
        for offset in range(1, 4)
    ]
    flags = [
        seg.astype(F32),
        (seg_blocks == before_seg[:, None]).astype(F32).reshape(length),
        (seg_blocks == last_seg[:, None]).astype(F32).reshape(length),
        jnp.repeat((last_seg == before_seg).astype(F32), q),
        jnp.zeros((length,), F32),
    ]
    aux = jnp.stack(shift_masks + flags, axis=0)
    conv_cols = jnp.concatenate(
        [conv_inner.reshape(4, inner), conv_state], axis=1
    )
    bias_row = jnp.concatenate([bias_inner.reshape(inner), bias_state])[None]
    conv_par = jnp.concatenate([conv_cols, bias_row, jnp.zeros((3, conv_rows), F32)], axis=0).T
    chan_par = jnp.concatenate(
        [
            gate_norm.reshape(1, inner),
            jnp.repeat(skip_gain, pc)[None],
            jnp.zeros((6, inner), F32),
        ],
        axis=0,
    ).T
    decay_rate = -jnp.exp(decay_log)
    head_par = jnp.pad(
        jnp.stack([step_bias, decay_rate], axis=1), ((0, STEP_ROWS - nh), (0, 6))
    )

    def token_block(order):
        return pl.BlockSpec((q, half), lambda i: (order(i), 0))

    def lane_block(count, order):
        return pl.BlockSpec((count, q), lambda i: (0, order(i)))

    def whole(*shape):
        return pl.BlockSpec(shape, lambda i: (0,) * len(shape), pipeline_mode=pl.Buffered(1))

    def up(i):
        return i

    def down(i):
        return blocks - 1 - i

    sds = jax.ShapeDtypeStruct
    forward = pl.pallas_call(
        functools.partial(forward_kernel, dims, mesh_dims),
        name="forward",
        grid=(blocks,),
        in_specs=[
            token_block(up),
            token_block(up),
            pl.BlockSpec(memory_space=pl.ANY),
            pl.BlockSpec(memory_space=pl.ANY),
            whole(*stacked.shape),
            whole(1, half),
            lane_block(8, up),
            whole(conv_rows, 8),
            whole(inner, 8),
            whole(STEP_ROWS, 8),
        ],
        out_specs=[
            token_block(up),
            token_block(up),
            lane_block(conv_rows, up),
            lane_block(conv_rows, up),
            lane_block(inner, up),
            lane_block(STEP_ROWS, up),
            lane_block(inner, up),
            lane_block(inner, up),
            pl.BlockSpec((1, inner, ns), lambda i: (i, 0, 0)),
            whole(2 * blocks, q),
            pl.BlockSpec(memory_space=pl.ANY),
            pl.BlockSpec(memory_space=pl.ANY),
            pl.BlockSpec(memory_space=pl.ANY),
        ],
        out_shape=[
            sds((length, half), BF16),
            sds((length, half), BF16),
            sds((conv_rows, length), F32),
            sds((conv_rows, length), F32),
            sds((inner, length), F32),
            sds((STEP_ROWS, length), F32),
            sds((inner, length), F32),
            sds((inner, length), F32),
            sds((blocks, inner, ns), F32),
            sds((2 * blocks, q), F32),
            sds((length, half), BF16),
            sds((length, half), BF16),
            sds((rows, width) if gathers else (16, 128), BF16),
        ],
        scratch_shapes=[
            pltpu.VMEM((conv_rows, 128), F32),
            pltpu.VMEM((inner, ns), F32),
            pltpu.VMEM((inner, q), F32),
            pltpu.VMEM((blocks, q, half), BF16),
            pltpu.VMEM((blocks, q, half), BF16),
            pltpu.VMEM((1, half), F32),
            pltpu.VMEM((group, 2 * blocks, q), F32),
            pltpu.SemaphoreType.DMA((4, blocks + 1)),
            pltpu.SemaphoreType.DMA((blocks + 1,)),
            pltpu.SemaphoreType.DMA((2, group - 1)),
        ]
        + chain_scratch(blocks, q, half)
        + (
            [pltpu.VMEM((rows, width), BF16)] + [pltpu.SemaphoreType.DMA((3,)) for _ in range(8)]
            if gathers
            else []
        ),
        compiler_params=pltpu.CompilerParams(
            vmem_limit_bytes=60 << 20, collective_id=1, has_side_effects=True
        ),
        cost_estimate=pl.CostEstimate(
            flops=2 * length * width * (out_at + 2 * inner),
            bytes_accessed=50 << 20,
            transcendentals=nh * length * q,
        ),
    )
    (
        normed_own,
        normed_sib,
        pre_vals,
        arg_vals,
        gate_vals,
        step_vals,
        mixed_vals,
        dng_vals,
        states,
        stats,
        out_sum,
        c_sib,
        weights,
    ) = forward(
        inputs,
        cotangent,
        inputs,
        cotangent,
        stacked,
        gain_own,
        aux,
        conv_par,
        chan_par,
        head_par,
    )
    if not gathers:
        weights = stacked
    gate_scale = lax.rsqrt(stats[:blocks].reshape(length) / (H * P_SIZE) + EPSILON)
    plain = inputs.astype(F32)
    output = (plain + gate_scale[:, None] * out_sum.astype(F32)).astype(BF16)

    backward = pl.pallas_call(
        functools.partial(backward_kernel, dims, mesh_dims),
        name="backward",
        grid=(blocks,),
        in_specs=[
            token_block(down),
            token_block(down),
            token_block(down),
            token_block(down),
            whole(rows, width),
            lane_block(8, down),
            whole(conv_rows, 8),
            whole(inner, 8),
            whole(STEP_ROWS, 8),
            lane_block(conv_rows, down),
            lane_block(conv_rows, down),
            lane_block(inner, down),
            lane_block(STEP_ROWS, down),
            lane_block(inner, down),
            lane_block(inner, down),
            pl.BlockSpec((1, inner, ns), lambda i: (down(i), 0, 0)),
            whole(2 * blocks, q),
        ],
        out_specs=[
            pl.BlockSpec(memory_space=pl.ANY),
            whole(rows, width),
            whole(conv_rows, 128),
            whole(inner, 128),
            whole(STEP_ROWS, 128),
        ],
        out_shape=[
            sds((length, half), BF16),
            sds((rows, width), BF16),
            sds((conv_rows, 128), F32),
            sds((inner, 128), F32),
            sds((STEP_ROWS, 128), F32),
        ],
        scratch_shapes=[
            pltpu.VMEM((3, conv_rows, 128), F32),
            pltpu.VMEM((inner, ns), F32),
            pltpu.VMEM((rows, width), F32),
            pltpu.VMEM((5, conv_rows, 128), F32),
            pltpu.VMEM((2, inner, 128), F32),
            pltpu.VMEM((2, STEP_ROWS, 128), F32),
            pltpu.VMEM((inner, q), F32),
            pltpu.VMEM((out_at, q), BF16),
        ]
        + chain_scratch(blocks, q, half),
        compiler_params=pltpu.CompilerParams(
            vmem_limit_bytes=60 << 20, collective_id=2, has_side_effects=True
        ),
        cost_estimate=pl.CostEstimate(
            flops=4 * length * width * (out_at + inner),
            bytes_accessed=60 << 20,
            transcendentals=nh * length * q,
        ),
    )
    dn_total, grad_w, conv_grad, chan_grad, head_grad = backward(
        normed_own,
        normed_sib,
        cotangent,
        c_sib,
        weights,
        aux,
        conv_par,
        chan_par,
        head_par,
        pre_vals,
        arg_vals,
        gate_vals,
        step_vals,
        mixed_vals,
        dng_vals,
        states,
        stats,
    )

    d_half = dn_total.astype(F32)
    weighted = d_half * gain_own
    sums = jnp.stack([jnp.sum(weighted * plain, axis=1), jnp.sum(plain * plain, axis=1)])
    sums = sums + lax.ppermute(sums, "row", swap)
    input_dot = sums[0]
    scaling = lax.rsqrt(sums[1] / width + EPSILON)
    grad_inputs = (
        cotangent.astype(F32)
        + scaling[:, None] * weighted
        - plain * (scaling**3 * input_dot / width)[:, None]
    )
    grad_norm = jnp.sum(d_half * plain * scaling[:, None], axis=0)

    grads = lax.psum_scatter(grad_w, "dp", scatter_dimension=1, tiled=True).astype(F32)
    head_wide = head_grad[:nh, :2].T
    skip_part = jnp.sum(chan_grad[:, 1].reshape(nh, pc), axis=1)[None]
    heads = jnp.concatenate([head_wide, skip_part], axis=0)

    def widen(part):
        wide = jnp.zeros((col_count,) + part.shape, F32)
        return lax.dynamic_update_slice_in_dim(wide, part[None], col_at, 0)

    step_wide = widen(grads[conv_rows : conv_rows + nh])
    head_all = widen(heads)
    grad_norm, conv_sum, gate_gain_sum, head_all = lax.psum(
        (grad_norm, conv_grad[:, :5].T, chan_grad[:, 0], head_all), "dp"
    )
    state_sum, step_wide, conv_state_sum, head_all = lax.psum(
        (grads[inner:conv_rows], step_wide, conv_sum[:, inner:], head_all), ("row", "col")
    )

    def take(wide):
        return lax.dynamic_slice_in_dim(wide, col_at, 1, 0)[0]

    step_grad = take(step_wide)
    head_own = take(head_all)

    def feature_rows(w):
        return jnp.transpose(w.reshape(nh, pc, share), (2, 0, 1))

    return (
        output,
        grad_inputs,
        grad_norm,
        feature_rows(grads[gate_at:out_at]),
        feature_rows(grads[0:inner]),
        state_sum.T,
        step_grad.T,
        conv_sum[:4, :inner].reshape(4, nh, pc),
        conv_sum[4, :inner].reshape(nh, pc),
        conv_state_sum[:4],
        conv_state_sum[4],
        head_own[0],
        head_own[1] * decay_rate,
        head_own[2],
        gate_gain_sum.reshape(nh, pc),
        feature_rows(grads[out_at:]),
    )


def solution(mesh):
    return jax.shard_map(
        per_device,
        mesh=mesh,
        in_specs=(
            P("dp", "row"),
            P("dp", None),
            P("dp", "row"),
            P("row"),
            P("dp", "col", "row"),
            P("dp", "col", "row"),
            P("dp", None),
            P("dp", "col"),
            P(None, "col", "row"),
            P("col", "row"),
            P(),
            P(),
            P("col"),
            P("col"),
            P("col"),
            P("col", "row"),
            P("dp", "col", "row"),
        ),
        out_specs=(
            P("dp", "row"),
            P("dp", "row"),
            P("row"),
            P("dp", "col", "row"),
            P("dp", "col", "row"),
            P("dp", None),
            P("dp", "col"),
            P(None, "col", "row"),
            P("col", "row"),
            P(),
            P(),
            P("col"),
            P("col"),
            P("col"),
            P("col", "row"),
            P("dp", "col", "row"),
        ),
        check_vma=False,
    )
```

```python
import functools

import jax
import jax.numpy as jnp
from jax import lax
from jax.experimental import pallas as pl
from jax.experimental.pallas import tpu as pltpu
from jax.sharding import PartitionSpec as P

H = 48
P_SIZE = 64
BLOCK_LEN = 256
EPSILON = 1e-05
NEG = -1e30
STEP_ROWS = 16
F32 = jnp.float32
BF16 = jnp.bfloat16
HIGHEST = lax.Precision.HIGHEST


def dot_nn(left, right, precision=None):
    return lax.dot_general(
        left, right, (((1,), (0,)), ((), ())), preferred_element_type=F32, precision=precision
    )


def dot_nt(left, right, precision=None):
    return lax.dot_general(
        left, right, (((1,), (1,)), ((), ())), preferred_element_type=F32, precision=precision
    )


def dot_tn(left, right):
    return lax.dot_general(left, right, (((0,), (0,)), ((), ())), preferred_element_type=F32)


def sigmoid(values):
    return 0.5 * jnp.tanh(0.5 * values) + 0.5


def softplus(values):
    return jnp.maximum(values, 0.0) + jnp.log1p(jnp.exp(-jnp.abs(values)))


def lane_fold(values):
    total = values[:, :128]
    for at in range(128, values.shape[1], 128):
        total = total + values[:, at : at + 128]
    return total


def columns_of(rows):
    padded = jnp.concatenate([rows, jnp.zeros((128 - rows.shape[0], rows.shape[1]), F32)], axis=0)
    return padded.T


def rows_of(ref):
    lanes = lax.broadcasted_iota(jnp.int32, ref.shape[1:], 1)
    total = jnp.zeros(ref.shape[1:], F32)
    for at in range(ref.shape[0]):
        total = jnp.where(lanes == at, jnp.sum(ref[at], axis=1, keepdims=True), total)
    if total.shape[0] % 128:
        total = jnp.concatenate([total, jnp.zeros((128 - total.shape[0], 128), F32)], axis=0)
    return total.T[0:8]


def load_columns(par_rows, head_rows, conv_scr, head_scr):
    conv_scr[...] = columns_of(par_rows[...])
    heads = columns_of(head_rows[...])[0:STEP_ROWS]
    lanes = lax.broadcasted_iota(jnp.int32, heads.shape, 1)
    head_scr[...] = jnp.where(lanes == 1, -jnp.exp(heads), heads)


def block_rows(dims, step_pre, hrow, aux):
    q = step_pre.shape[1]
    step_arg = step_pre + hrow[:, 0:1]
    step = softplus(step_arg)
    log_decay = step * hrow[:, 1:2]
    source = lax.broadcasted_iota(jnp.int32, (q, q), 0)
    target = lax.broadcasted_iota(jnp.int32, (q, q), 1)
    upper = (source <= target).astype(F32)
    cumul = dot_nn(log_decay, upper, HIGHEST)
    last = cumul[:, q - 1 : q]
    cols = columns_of(jnp.concatenate([cumul, aux], axis=0))
    return step_arg, step, cumul, last, cols


MESH = pl.DeviceIdType.MESH


def send(src, dst, sems, at, **device):
    return pltpu.make_async_remote_copy(
        src_ref=src,
        dst_ref=dst,
        send_sem=sems[0].at[at],
        recv_sem=sems[1].at[at],
        device_id=device,
        device_id_type=MESH,
    )


def group_peers(row_count, col_count):
    row_at, col_at = lax.axis_index("row"), lax.axis_index("col")
    return [
        dict(row=lax.rem(row_at + j, row_count), col=lax.rem(col_at + k, col_count))
        for k in range(col_count)
        for j in range(row_count)
        if (j, k) != (0, 0)
    ]


def greet(peers):
    barrier = pltpu.get_barrier_semaphore()
    for peer in peers:
        pl.semaphore_signal(barrier, inc=1, device_id=peer, device_id_type=MESH)


def greeted(peers):
    pl.semaphore_wait(pltpu.get_barrier_semaphore(), len(peers))


def add_low(left, right):
    return (left.astype(F32) + right.astype(F32)).astype(BF16)


class Chain:
    def __init__(self, own, sib, bufs, sems, result, q, place):
        self.place = place
        self.own, self.sib, self.result, self.q = own, sib, result, q
        self.first, self.pair, self.cross = bufs
        self.sems = sems
        self.row_at, self.col_at = lax.axis_index("row"), lax.axis_index("col")
        self.is_outer = (self.col_at == 0) | (self.col_at == 3)
        self.inward = 1 + lax.div(self.col_at, 2)
        self.outward = 3 * lax.div(self.col_at, 2)

    def exchange(self, b):
        return send(
            self.sib.at[b], self.first.at[b], self.sems[0], b, row=1 - self.row_at
        )

    def to_inner(self, b):
        return send(self.first.at[b], self.pair.at[b], self.sems[1], b, col=self.inward)

    def across(self, b):
        return send(self.pair.at[b], self.cross.at[b], self.sems[2], b, col=3 - self.col_at)

    def rows(self, b):
        return self.result.at[pl.ds(pl.multiple_of(self.place(b) * self.q, self.q), self.q)]

    def to_outer(self, b):
        return send(self.cross.at[b], self.rows(b), self.sems[3], b, col=self.outward)

    def keep(self, b):
        return pltpu.make_async_copy(self.cross.at[b], self.rows(b), self.sems[4].at[b])

    def stage_first(self, b):
        self.exchange(b).wait_recv()
        self.first[b] = add_low(self.own[b], self.first[b])

        @pl.when(self.is_outer)
        def _():
            self.to_inner(b).start()

    def stage_pair(self, b):
        @pl.when(~self.is_outer)
        def _():
            self.to_inner(b).wait_recv()
            self.pair[b] = add_low(self.first[b], self.pair[b])
            self.across(b).start()

    def stage_cross(self, b):
        @pl.when(~self.is_outer)
        def _():
            self.across(b).wait_recv()
            self.cross[b] = add_low(self.pair[b], self.cross[b])
            self.keep(b).start()
            self.to_outer(b).start()

    def progress(self, i):
        for lag, stage in ((1, self.stage_first), (2, self.stage_pair), (3, self.stage_cross)):

            @pl.when(i >= lag)
            def _():
                stage(i - lag)

    def drain(self, blocks, extra):
        for lag, stage in ((1, self.stage_first), (2, self.stage_pair), (3, self.stage_cross)):
            if lag > extra:
                stage(blocks + extra - lag)

    def finish(self, blocks):
        def finish(b, _):
            self.exchange(b).wait_send()

            @pl.when(self.is_outer)
            def _():
                self.to_inner(b).wait_send()
                self.to_outer(b).wait_recv()

            @pl.when(~self.is_outer)
            def _():
                self.across(b).wait_send()
                self.to_outer(b).wait_send()
                self.keep(b).wait()

            return 0

        lax.fori_loop(0, blocks, finish, 0)


def chain_scratch(blocks, q, half):
    dma = pltpu.SemaphoreType.DMA
    buffers = [pltpu.VMEM((blocks, q, half), BF16) for _ in range(5)]
    return buffers + [dma((blocks,)) for _ in range(9)]


def chain_of(refs, result, q, place):
    own, sib, first, pair, cross = refs[:5]
    sems = [tuple(refs[5 + 2 * k : 7 + 2 * k]) for k in range(4)] + [refs[13]]
    return Chain(own, sib, (first, pair, cross), sems, result, q, place)


class Gather:
    def __init__(self, mine, whole, sems, groups):
        self.mine, self.whole, self.groups = mine, whole, groups
        self.sems = sems
        at = lax.axis_index("dp")
        self.at = at
        self.near = at + 1 - 2 * lax.rem(at, 2)
        self.far = lax.rem(at + 2, 4)
        self.share = mine.shape[1]

    def part(self, shard, lo, hi):
        return self.whole.at[
            lo:hi, pl.ds(pl.multiple_of(shard * self.share, 128), self.share)
        ]

    def direct(self, g, to_near):
        lo, _, hi = self.groups[g]
        return send(
            self.mine.at[lo:hi],
            self.part(self.at, lo, hi),
            self.sems[0 if to_near else 1],
            g,
            dp=self.near if to_near else self.far,
        )

    def onward(self, g, from_near):
        lo, mid, hi = self.groups[g]
        lo, hi = (lo, mid) if from_near else (mid, hi)
        part = self.part(self.near if from_near else self.far, lo, hi)
        return send(
            part,
            part,
            self.sems[2 if from_near else 3],
            g,
            dp=self.far if from_near else self.near,
        )

    def start(self):
        for g in range(len(self.groups)):
            self.direct(g, True).start()
            self.direct(g, False).start()

    def take(self, g):
        self.direct(g, True).wait_recv()
        self.onward(g, True).start()
        self.direct(g, False).wait_recv()
        self.onward(g, False).start()
        self.onward(g, True).wait_recv()
        self.onward(g, False).wait_recv()

    def finish(self):
        for g in range(len(self.groups)):
            for which in (True, False):
                self.direct(g, which).wait_send()
                self.onward(g, which).wait_send()


class Reduce:
    def __init__(self, acc, stage, split, rows, bufs, sems):
        self.acc, self.stage = acc, stage
        self.halves = ((0, split), (split, rows))
        self.bufs, self.sems = bufs, sems
        at = lax.axis_index("dp")
        self.at = at
        self.near = at + 1 - 2 * lax.rem(at, 2)
        self.far = lax.rem(at + 2, 4)
        self.share = acc.shape[1] // 4

    def cols(self, shard):
        return pl.ds(pl.multiple_of(shard * self.share, 128), self.share)

    def first(self, half, slot):
        lo, hi = self.halves[half]
        to = (self.near, self.far)[half]
        shard = to if slot == 0 else 3 - self.at
        return send(
            self.stage.at[lo:hi, self.cols(shard)],
            self.bufs[half].at[slot],
            self.sems[half],
            slot,
            dp=to,
        )

    def second(self, half):
        return send(
            self.bufs[half].at[1],
            self.bufs[2 + half],
            self.sems[half],
            2,
            dp=(self.far, self.near)[half],
        )

    def start(self):
        for slot in (1, 0):
            for half in range(2):
                self.first(half, slot).start()

    def middle(self):
        for half in range(2):
            lo, hi = self.halves[half]
            other = (self.far, self.near)[half]
            self.first(half, 1).wait_recv()
            self.bufs[half][1] = (
                self.acc[lo:hi, self.cols(other)] + self.bufs[half][1].astype(F32)
            ).astype(BF16)
            self.second(half).start()

    def end(self):
        for half in range(2):
            lo, hi = self.halves[half]
            self.first(half, 0).wait_recv()
            self.second(half).wait_recv()
            mine = self.cols(self.at)
            self.acc[lo:hi, mine] = (
                self.acc[lo:hi, mine]
                + self.bufs[half][0].astype(F32)
                + self.bufs[2 + half][...].astype(F32)
            )

    def finish(self):
        for half in range(2):
            self.first(half, 0).wait_send()
            self.first(half, 1).wait_send()
            self.second(half).wait_send()


def forward_kernel(
    dims,
    mesh_dims,
    x_own,
    c_own,
    x_any,
    c_any,
    gain_own,
    seg_ref,
    par_rows,
    head_rows,
    *refs,
):
    gathers = mesh_dims[2]
    count = 5 if gathers else 1
    forward_body(
        dims,
        mesh_dims,
        x_own,
        c_own,
        x_any,
        c_any,
        gain_own,
        seg_ref,
        par_rows,
        head_rows,
        refs[:count],
        *refs[count:],
    )


def stack_weights(mine, parts, gate_at, out_at):
    inner_w, state_w, step_w, gate_w, out_w = parts
    inner, share = inner_w.shape
    nh = step_w.shape[0]
    conv_rows = gate_at - STEP_ROWS
    mine[0:inner] = inner_w[...].astype(BF16)
    mine[inner:conv_rows] = state_w[...].T.astype(BF16)
    mine[conv_rows:gate_at] = jnp.concatenate(
        [step_w[...], jnp.zeros((STEP_ROWS - nh, share), F32)], axis=0
    ).astype(BF16)
    mine[gate_at:out_at] = gate_w[...].astype(BF16)
    mine[out_at:] = out_w[...].astype(BF16)


def forward_body(
    dims,
    mesh_dims,
    x_own,
    c_own,
    x_any,
    c_any,
    gain_own,
    seg_ref,
    par_rows,
    head_rows,
    weight_parts,
    normed_own,
    normed_sib,
    pre_out,
    arg_out,
    gate_out,
    step_out,
    mixed_out,
    dng_out,
    state_out,
    aux_out,
    scale_out,
    stats_out,
    out_total,
    c_out,
    w_out,
    prev,
    prev_seg,
    state,
    act_scr,
    conv_scr,
    head_scr,
    x_scr,
    c_scr,
    gain_sib,
    stats_scr,
    swap_sems,
    local_sems,
    stat_sems,
    *rest,
):
    nh, pc, ns, width = dims
    row_count, col_count, gathers = mesh_dims
    step_at = pl.program_id(0)
    blocks = x_scr.shape[0]
    inner = nh * pc
    conv_rows = inner + 2 * ns
    gate_at = conv_rows + STEP_ROWS
    out_at = gate_at + inner
    half = x_own.shape[1]
    q = x_own.shape[0]
    row_at, col_at = lax.axis_index("row"), lax.axis_index("col")
    own_at = pl.multiple_of(row_at * half, 128)
    sib_at = pl.multiple_of((1 - row_at) * half, 128)
    sib = dict(row=1 - row_at)
    me = row_at * col_count + col_at
    peers = group_peers(row_count, col_count)
    chain = chain_of(rest[:14], out_total, q, lambda b: b)

    def token_rows(ref, b):
        return ref.at[pl.ds(pl.multiple_of(b * q, q), q)]

    def swap(which, b):
        src, dst = ((x_any, x_scr), (c_any, c_scr))[which]
        sems = (swap_sems.at[2 * which], swap_sems.at[2 * which + 1])
        return send(token_rows(src, b), dst.at[b], sems, b, **sib)

    gain_swap = send(
        gain_own, gain_sib, (swap_sems.at[0], swap_sems.at[1]), blocks, **sib
    )

    def keep_cot(b):
        return pltpu.make_async_copy(c_scr.at[b], token_rows(c_out, b), local_sems.at[b])

    def stat_copy(k):
        return send(
            stats_scr.at[me], stats_scr.at[me], (stat_sems.at[0], stat_sems.at[1]), k, **peers[k]
        )

    if gathers:
        weights, mine = rest[14:16]
        bounds = (
            (0, 336, gate_at),
            (gate_at, gate_at + inner // 2, out_at),
            (out_at, out_at + inner // 2, out_at + inner),
        )
        sems = [tuple(rest[16 + 2 * k : 18 + 2 * k]) for k in range(4)]
        gather = Gather(mine, weights, sems, bounds)
        others = [dict(dp=gather.near), dict(dp=gather.far)]
        keep_weights = pltpu.make_async_copy(weights, w_out, local_sems.at[blocks])
    else:
        weights, gather, others = weight_parts[0], None, []

    @pl.when(step_at == 0)
    def _():
        greet(peers + others)
        if gathers:
            stack_weights(mine, weight_parts, gate_at, out_at)
        greeted(peers + others)
        if gathers:
            gather.start()
        gain_swap.start()
        for b in range(blocks):
            swap(0, b).start()
            swap(1, b).start()
        prev[...] = jnp.zeros_like(prev)
        prev_seg[...] = jnp.full_like(prev_seg, -1.0)
        state[...] = jnp.zeros_like(state)
        load_columns(par_rows, head_rows, conv_scr, head_scr)
        if gathers:
            share = mine.shape[1]
            mine_at = pl.multiple_of(lax.axis_index("dp") * share, 128)
            weights[:, pl.ds(mine_at, share)] = mine[...]
        gain_swap.wait_recv()
        if gathers:
            gather.take(0)

    swap(0, step_at).wait_recv()
    xo = x_own[...].astype(F32)
    xs = x_scr[step_at].astype(F32)
    squares = jnp.sum(xo * xo, axis=1, keepdims=True) + jnp.sum(xs * xs, axis=1, keepdims=True)
    scaling = lax.rsqrt(squares / width + EPSILON)
    scale_out[...] = jnp.broadcast_to(scaling, (q, 128))
    no = (xo * scaling * gain_own[...]).astype(BF16)
    nsib = (xs * scaling * gain_sib[...]).astype(BF16)
    normed_own[...] = no
    normed_sib[...] = nsib
    pre = dot_nt(weights[0:gate_at, pl.ds(own_at, half)], no) + dot_nt(
        weights[0:gate_at, pl.ds(sib_at, half)], nsib
    )
    values = pre[0:conv_rows]
    step_pre = pre[conv_rows:gate_at]
    pre_out[...] = values
    step_out[...] = step_pre
    seg = seg_ref[...].astype(F32)
    seg_before = prev_seg[...]
    seg_joined = jnp.concatenate([seg_before, seg], axis=1)
    before, final = seg_before[:, 127:128], seg[:, q - 1 : q]
    aux = jnp.concatenate(
        [
            (seg_joined[:, 128 - offset : 128 - offset + q] == seg).astype(F32)
            for offset in range(1, 4)
        ]
        + [
            seg,
            (seg == before).astype(F32),
            (seg == final).astype(F32),
            jnp.broadcast_to((before == final).astype(F32), (1, q)),
            jnp.zeros((1, q), F32),
        ],
        axis=0,
    )
    prev_seg[...] = seg[:, q - 128 :]
    aux_out[...] = aux
    conv = conv_scr[...]
    head = head_scr[...]
    joined = jnp.concatenate([prev[...], values], axis=1)
    arg = conv[:, 4:5] + conv[:, 3:4] * values
    for offset in range(1, 4):
        arg = arg + conv[:, 3 - offset : 4 - offset] * (
            aux[offset - 1 : offset] * joined[:, 128 - offset : 128 - offset + q]
        )
    prev[...] = values[:, q - 128 :]
    arg_out[...] = arg
    act = arg * sigmoid(arg)
    act_scr[...] = act[0:inner]
    in_low = act[inner : inner + ns].astype(BF16)
    out_low = act[inner + ns :].astype(BF16)

    _, step, cumul, last, cols = block_rows(dims, step_pre, head, aux)
    source = lax.broadcasted_iota(jnp.int32, (q, q), 0)
    target = lax.broadcasted_iota(jnp.int32, (q, q), 1)
    seg_col = cols[:, STEP_ROWS + 3 : STEP_ROWS + 4]
    bias = jnp.where((source <= target) & (seg_col == aux[3:4]), 0.0, NEG)
    pairs = dot_tn(in_low, out_low)
    entering = state[...]
    state_out[0] = entering
    from_state = dot_nn(entering.astype(BF16), out_low)
    reach = aux[4:5] * jnp.exp(cumul)
    tails = aux[5:6] * jnp.exp(last - cumul)
    keep = aux[6:7, 0:1] * jnp.exp(last)
    hq = q // 2
    gain = conv[0:inner, 5:6]
    tail_parts = []
    for h in range(nh):
        lo = h * pc
        x_h = act_scr[lo : lo + pc]
        u_h = (x_h * step[h : h + 1]).astype(BF16)
        tail_parts.append((x_h * (step[h : h + 1] * tails[h : h + 1])).astype(BF16))
        col = cols[:, h : h + 1]
        row = cumul[h : h + 1]
        top = (jnp.exp((row - col[:hq]) + bias[:hq]) * pairs[:hq]).astype(BF16)
        low = (jnp.exp((row[:, hq:] - col[hq:]) + bias[hq:, hq:]) * pairs[hq:, hq:]).astype(BF16)
        y_top = dot_nn(u_h[:, :hq], top)
        y_low = dot_nn(u_h[:, hq:], low)
        y_h = jnp.concatenate([y_top[:, :hq], y_top[:, hq:] + y_low], axis=1)
        y_h = y_h + from_state[lo : lo + pc] * reach[h : h + 1]
        mixed_out[lo : lo + pc] = y_h + head[h : h + 1, 2:3] * x_h
    chain.progress(step_at)
    contrib = dot_nt(jnp.concatenate(tail_parts, axis=0), in_low)
    for h in range(nh):
        lo = h * pc
        state[lo : lo + pc] = keep[h : h + 1] * entering[lo : lo + pc] + contrib[lo : lo + pc]
    if gathers:

        @pl.when(step_at == 0)
        def _():
            gather.take(1)

    gate = dot_nt(weights[gate_at:out_at, pl.ds(own_at, half)], no) + dot_nt(
        weights[gate_at:out_at, pl.ds(sib_at, half)], nsib
    )
    gate_out[...] = gate
    gated = mixed_out[...] * (gate * sigmoid(gate))
    squares_row = jnp.sum(gated * gated, axis=0, keepdims=True)
    weighted = gated * gain
    low = weighted.astype(BF16)
    if gathers:

        @pl.when(step_at == 0)
        def _():
            gather.take(2)
            keep_weights.start()

    chain.sib[step_at] = dot_tn(low, weights[out_at:, pl.ds(sib_at, half)]).astype(BF16)
    chain.exchange(step_at).start()
    chain.own[step_at] = dot_tn(low, weights[out_at:, pl.ds(own_at, half)]).astype(BF16)
    swap(1, step_at).wait_recv()
    keep_cot(step_at).start()
    dng = dot_nt(weights[out_at:, pl.ds(own_at, half)], c_own[...]) + dot_nt(
        weights[out_at:, pl.ds(sib_at, half)], c_scr[step_at]
    )
    dng_out[...] = dng
    dot_row = jnp.sum(dng * weighted, axis=0, keepdims=True)
    stats_scr[me, pl.ds(step_at, 1)] = squares_row
    stats_scr[me, pl.ds(blocks + step_at, 1)] = dot_row

    @pl.when(step_at == blocks - 1)
    def _():
        for k in range(len(peers)):
            stat_copy(k).start()
        for extra in range(3):
            chain.drain(blocks, extra)
        chain.finish(blocks)
        for k in range(len(peers)):
            stat_copy(k).wait()
        total = stats_scr[0]
        for k in range(1, len(peers) + 1):
            total = total + stats_scr[k]
        stats_out[...] = total
        gain_swap.wait_send()
        for b in range(blocks):
            swap(0, b).wait_send()
            swap(1, b).wait_send()
            keep_cot(b).wait()
        if gathers:
            gather.finish()
            keep_weights.wait()


def backward_kernel(
    dims,
    mesh_dims,
    normed_own,
    normed_sib,
    c_own,
    c_sib,
    weights,
    aux_ref,
    par_rows,
    head_rows,
    gain_own,
    pre_ref,
    arg_ref,
    gate_ref,
    step_ref,
    mixed_ref,
    dng_ref,
    state_ref,
    stats_ref,
    dn_total,
    dot_out,
    vec_out,
    *refs,
):
    gathers = mesh_dims[2]
    grad_outs, refs = (refs[:5], refs[5:]) if gathers else (refs[:1], refs[1:])
    (
        after,
        d_state,
        acc_w,
        acc_conv,
        acc_chan,
        acc_head,
        acc_norm,
        acc_dot,
        du_scr,
        low_scr,
        conv_scr,
        head_scr,
        stage,
        group_vec,
        dp_vec,
        group_sems,
        dp_sems,
    ) = refs[:17]
    rest = refs[17:]
    nh, pc, ns, width = dims
    row_count, col_count = mesh_dims[:2]
    step_at = pl.program_id(0)
    blocks = stats_ref.shape[0] // 2
    inner = nh * pc
    conv_rows = inner + 2 * ns
    gate_at = conv_rows + STEP_ROWS
    out_at = gate_at + inner
    half = c_own.shape[1]
    q = c_own.shape[0]
    inner_width = H * P_SIZE
    row_at = lax.axis_index("row")
    own_at = pl.multiple_of(row_at * half, 128)
    sib_at = pl.multiple_of((1 - row_at) * half, 128)

    chain = chain_of(rest[:14], dn_total, q, lambda b: blocks - 1 - b)
    block_at = blocks - 1 - step_at
    col_at = chain.col_at
    group = row_count * col_count
    me = row_at * col_count + col_at
    peers = group_peers(row_count, col_count)
    dp_at = lax.axis_index("dp")
    friends = [dict(dp=lax.rem(dp_at + k, 4)) for k in range(1, 4)] if gathers else []

    @pl.when(step_at == 0)
    def _():
        greet(peers + friends)
        load_columns(par_rows, head_rows, conv_scr, head_scr)
        acc_norm[...] = jnp.zeros_like(acc_norm)
        acc_dot[...] = jnp.zeros_like(acc_dot)
        after[...] = jnp.zeros_like(after)
        d_state[...] = jnp.zeros_like(d_state)
        acc_w[...] = jnp.zeros_like(acc_w)
        acc_conv[...] = jnp.zeros_like(acc_conv)
        acc_chan[...] = jnp.zeros_like(acc_chan)
        acc_head[...] = jnp.zeros_like(acc_head)
        greeted(peers + friends)

    aux = aux_ref[...]
    conv = conv_scr[...]
    gain = conv[0:inner, 5:6]
    hrow = head_scr[...]
    gate_scale = lax.rsqrt(stats_ref[pl.ds(block_at, 1)] / inner_width + EPSILON)
    gate_dot = stats_ref[pl.ds(blocks + block_at, 1)]
    pull = gate_scale * gate_scale * gate_scale * gate_dot / inner_width
    gate = gate_ref[...]
    sig = sigmoid(gate)
    silu = gate * sig
    mixed = mixed_ref[...]
    gated = mixed * silu
    dng_scaled = dng_ref[...] * gate_scale
    d_gated = gain * dng_scaled - gated * pull
    acc_chan[0] += lane_fold(dng_scaled * gated)
    normed_gate = (gated * (gate_scale * gain)).astype(BF16)
    acc_w[out_at:, pl.ds(own_at, half)] += dot_nn(normed_gate, c_own[...])
    acc_w[out_at:, pl.ds(sib_at, half)] += dot_nn(normed_gate, c_sib[...])
    grad_mixed = d_gated * silu
    low_scr[gate_at:out_at] = (d_gated * mixed * (sig * (1.0 + gate * (1.0 - sig)))).astype(BF16)

    arg = arg_ref[...]
    sig_arg = sigmoid(arg)
    act = arg * sig_arg
    act_slope = sig_arg * (1.0 + arg * (1.0 - sig_arg))
    x_all = act[0:inner]
    in_low = act[inner : inner + ns].astype(BF16)
    out_low = act[inner + ns :].astype(BF16)
    step_arg, step, cumul, last, cols = block_rows(dims, step_ref[...], hrow, aux)
    t_at = lax.broadcasted_iota(jnp.int32, (q, q), 0)
    s_at = lax.broadcasted_iota(jnp.int32, (q, q), 1)
    seg_col = cols[:, STEP_ROWS + 3 : STEP_ROWS + 4]
    bias = jnp.where((s_at <= t_at) & (seg_col == aux[3:4]), 0.0, NEG)
    pairs = dot_tn(out_low, in_low)
    reach = aux[4:5] * jnp.exp(cumul)
    tails = aux[5:6] * jnp.exp(last - cumul)
    keep = aux[6:7, 0:1] * jnp.exp(last)
    entering = state_ref[0]
    d_next = d_state[...]
    from_next = dot_nn(d_next.astype(BF16), in_low)
    hq = q // 2
    acc_chan[1] += lane_fold(grad_mixed * x_all)
    d_pairs_top = jnp.zeros((hq, hq), F32)
    d_pairs_low = jnp.zeros((hq, q), F32)
    reach_parts, tail_parts = [], []
    row_sums, col_sums, x_sums, tail_sums, carry_sums = [], [], [], [], []
    for h in range(nh):
        lo = h * pc
        x_h = x_all[lo : lo + pc]
        u_h = x_h * step[h : h + 1]
        u_low = u_h.astype(BF16)
        g_h = grad_mixed[lo : lo + pc]
        g_low = g_h.astype(BF16)
        col = cols[:, h : h + 1]
        row = cumul[h : h + 1]
        reach_parts.append((g_h * reach[h : h + 1]).astype(BF16))
        tail_parts.append((u_h * tails[h : h + 1]).astype(BF16))
        e_top = jnp.exp((col[:hq] - row[:, :hq]) + bias[:hq, :hq])
        e_low = jnp.exp((col[hq:] - row) + bias[hq:])
        m_top = (e_top * pairs[:hq, :hq]).astype(BF16)
        m_low = (e_low * pairs[hq:]).astype(BF16)
        dm_top = dot_tn(g_low[:, :hq], u_low[:, :hq])
        dm_low = dot_tn(g_low[:, hq:], u_low)
        d_pairs_top = d_pairs_top + dm_top * e_top
        d_pairs_low = d_pairs_low + dm_low * e_low
        du_top = dot_nn(g_low[:, :hq], m_top)
        du_low = dot_nn(g_low[:, hq:], m_low)
        du_local = jnp.concatenate([du_top + du_low[:, :hq], du_low[:, hq:]], axis=1)
        du_next = from_next[lo : lo + pc] * tails[h : h + 1]
        du = du_local + du_next
        du_scr[lo : lo + pc] = du * step[h : h + 1] + hrow[h : h + 1, 2:3] * g_h
        u_round = u_low.astype(F32)
        y_h = mixed[lo : lo + pc] - hrow[h : h + 1, 2:3] * x_h
        row_sums.append(jnp.sum(g_low.astype(F32) * y_h, axis=0, keepdims=True))
        next_sum = jnp.sum(u_round * du_next, axis=0, keepdims=True)
        col_sums.append(jnp.sum(u_round * du_local, axis=0, keepdims=True) + next_sum)
        tail_sums.append(next_sum)
        x_sums.append(jnp.sum(x_h * du, axis=0, keepdims=True))
        flow = jnp.sum(entering[lo : lo + pc] * d_next[lo : lo + pc], axis=0, keepdims=True)
        carry_sums.append(flow)
    chain.progress(step_at)
    pad_rows = [jnp.zeros((STEP_ROWS - nh, q), F32)]
    row_sum = jnp.concatenate(row_sums + pad_rows, axis=0)
    col_sum = jnp.concatenate(col_sums + pad_rows, axis=0)
    tail_sum = jnp.concatenate(tail_sums + pad_rows, axis=0)
    x_sum = jnp.concatenate(x_sums + pad_rows, axis=0)
    carry = jnp.concatenate(carry_sums + [jnp.zeros((STEP_ROWS - nh, ns), F32)], axis=0)
    d_last = jnp.sum(tail_sum, axis=1, keepdims=True) + keep * jnp.sum(
        carry, axis=1, keepdims=True
    )
    later = (t_at >= s_at).astype(F32)
    d_log = dot_nn(row_sum - col_sum, later, HIGHEST) + d_last
    d_step = x_sum + hrow[:, 1:2] * d_log
    d_step_arg = d_step * sigmoid(step_arg)
    acc_head[0] += lane_fold(d_step_arg)
    acc_head[1] += lane_fold(step * d_log)
    low_scr[conv_rows:gate_at] = d_step_arg.astype(BF16)

    g_reach = jnp.concatenate(reach_parts, axis=0)
    u_tail = jnp.concatenate(tail_parts, axis=0)
    d_top_low = d_pairs_top.astype(BF16)
    d_low_low = d_pairs_low.astype(BF16)
    d_out = dot_tn(entering.astype(BF16), g_reach)
    d_out = d_out + jnp.concatenate(
        [dot_nt(in_low[:, :hq], d_top_low), dot_nt(in_low, d_low_low)], axis=1
    )
    d_in = dot_tn(d_next.astype(BF16), u_tail) + dot_nn(out_low[:, hq:], d_low_low)
    d_in_top = dot_nn(out_low[:, :hq], d_top_low)
    d_in = jnp.concatenate([d_in[:, :hq] + d_in_top, d_in[:, hq:]], axis=1)
    d_enter = dot_nt(g_reach, out_low)
    for h in range(nh):
        lo = h * pc
        d_state[lo : lo + pc] = keep[h : h + 1] * d_next[lo : lo + pc] + d_enter[lo : lo + pc]

    err = jnp.concatenate([du_scr[...], d_in, d_out], axis=0) * act_slope
    values = pre_ref[...]
    d_pre = conv[:, 3:4] * err
    acc_conv[3] += lane_fold(err * values)
    acc_conv[4] += lane_fold(err)
    for offset in range(1, 4):
        masked = err * aux[offset - 1 : offset]
        joined = jnp.concatenate([masked, after[offset - 1]], axis=1)
        shifted = joined[:, offset : offset + q]
        after[offset - 1] = masked[:, :128]
        d_pre = d_pre + conv[:, 3 - offset : 4 - offset] * shifted
        acc_conv[3 - offset] += lane_fold(shifted * values)
    low_scr[0:conv_rows] = d_pre.astype(BF16)
    low = low_scr[...]
    dn_sib = dot_tn(low, weights[0:out_at, pl.ds(sib_at, half)])
    chain.sib[step_at] = dn_sib.astype(BF16)
    chain.exchange(step_at).start()
    dn_own = dot_tn(low, weights[0:out_at, pl.ds(own_at, half)])
    chain.own[step_at] = dn_own.astype(BF16)
    token_dot = jnp.zeros((q, 1), F32)
    for which, (part, seen) in enumerate(((dn_own, normed_own), (dn_sib, normed_sib))):
        product = part * seen[...].astype(F32)
        token_dot = token_dot + jnp.sum(product, axis=1, keepdims=True)
        acc_norm[which] += jnp.sum(product.reshape(q // 8, 8, half), axis=0)
    lanes = lax.broadcasted_iota(jnp.int32, acc_dot.shape, 1)
    acc_dot[...] = jnp.where(lanes == block_at, token_dot, acc_dot[...])
    acc_w[0:out_at, pl.ds(own_at, half)] += dot_nn(low, normed_own[...])
    acc_w[0:out_at, pl.ds(sib_at, half)] += dot_nn(low, normed_sib[...])

    @pl.when(step_at == blocks - 1)
    def _():
        conv_vec = rows_of(acc_conv)
        chan_vec = rows_of(acc_chan)
        head_vec = rows_of(acc_head)
        norm_vec = [jnp.sum(acc_norm[which], axis=0, keepdims=True) for which in range(2)]
        lane = 256
        zeros = jnp.zeros((1, 128), F32)
        skip = chan_vec[1:2]
        group_vec[me] = jnp.concatenate(
            [
                conv_vec[0:5, inner:],
                skip[:, 0:lane],
                jnp.concatenate([skip[:, lane:], head_vec[0:1]], axis=1),
                jnp.concatenate([head_vec[1:2], zeros], axis=1),
                acc_dot[...].T[0:blocks],
            ]
            + [vec[:, at : at + lane] for vec in norm_vec for at in range(0, half, lane)]
            + [jnp.zeros((2, lane), F32)],
            axis=0,
        )

        def group_copy(k):
            return send(
                group_vec.at[me],
                group_vec.at[me],
                (group_sems.at[0], group_sems.at[1]),
                k,
                **peers[k],
            )

        for k in range(group - 1):
            group_copy(k).start()
        stage[...] = acc_w[...].astype(BF16)
        if gathers:
            reduce = Reduce(
                acc_w,
                stage,
                rest[14].shape[1],
                out_at + inner,
                rest[14:18],
                (tuple(rest[18:20]), tuple(rest[20:22])),
            )
            reduce.start()
        chain.drain(blocks, 0)
        for k in range(group - 1):
            group_copy(k).wait()
        shared = group_vec[0]
        for k in range(1, group):
            shared = shared + group_vec[k]
        by_row, by_head = jnp.zeros((6, lane), F32), jnp.zeros((3, lane), F32)
        for k in range(group):
            same = (k // col_count) == row_at
            one = group_vec[k]
            picked = jnp.concatenate([one[16:22], one[5:8]], axis=0)
            near = jnp.where(same, picked[0:3], picked[3:6])
            by_row = by_row + jnp.concatenate([near, near], axis=0)
            by_head = by_head + jnp.where((k % col_count) == col_at, picked[6:9], 0.0)
        dot_out[...] = shared[8:16]
        norm_sum = jnp.concatenate([by_row[at : at + 1] for at in range(half // lane)], axis=1)
        norm_sum = norm_sum / gain_own[...]
        skip_sum = jnp.concatenate([by_head[0:1], by_head[1:2, 0:128]], axis=1)
        dp_vec[0] = jnp.concatenate(
            [
                jnp.concatenate([conv_vec[0:5, 0:inner], shared[0:5]], axis=1),
                jnp.concatenate([chan_vec[0:1], by_head[1:2, 128:], by_head[2:3, 0:128]], axis=1),
                jnp.concatenate([skip_sum, norm_sum[:, 0:lane]], axis=1),
                jnp.concatenate([norm_sum[:, lane:], zeros], axis=1),
            ],
            axis=0,
        )

        def dp_copy(k):
            return send(
                dp_vec.at[0], dp_vec.at[k], (dp_sems.at[0], dp_sems.at[1]), k - 1, **friends[k - 1]
            )

        if gathers:
            for k in range(1, 4):
                dp_copy(k).start()
        chain.drain(blocks, 1)
        if gathers:
            reduce.middle()
        chain.drain(blocks, 2)
        if gathers:
            for k in range(1, 4):
                dp_copy(k).wait()
            ordered = [lax.rem(dp_at - k + 4, 4) for k in range(4)]
            total = dp_vec[ordered[0]]
            for k in range(1, 4):
                total = total + dp_vec[ordered[k]]
            vec_out[...] = total
            reduce.end()
            mine = reduce.cols(dp_at)
            step_scr, state_send, state_recv, state_all, step_sems, state_sems = rest[22:28]
            slice_rows = 2 * ns // group
            for k in range(group):
                lo = inner + k * slice_rows
                state_send[k] = acc_w[lo : lo + slice_rows, mine].astype(BF16)
            step_scr[0] = acc_w[conv_rows:gate_at, mine]

            def state_copy(phase, k):
                peer = peers[k]
                sems = (state_sems.at[2 * phase], state_sems.at[2 * phase + 1])
                to = peer["row"] * col_count + peer["col"]
                if phase == 0:
                    return send(state_send.at[to], state_recv.at[me], sems, k, **peer)
                return send(state_all.at[me], state_all.at[me], sems, k, **peer)

            step_copy = send(
                step_scr.at[0],
                step_scr.at[1],
                (step_sems.at[0], step_sems.at[1]),
                0,
                row=1 - row_at,
            )
            for k in range(group - 1):
                state_copy(0, k).start()
            step_copy.start()
            g_inner, g_state, g_step, g_gate, g_out = grad_outs
            g_inner[...] = acc_w[0:inner, mine]
            g_gate[...] = acc_w[gate_at:out_at, mine]
            g_out[...] = acc_w[out_at:, mine]
            state_recv[me] = state_send[me]
            for k in range(group - 1):
                state_copy(0, k).wait()
            summed = state_recv[0].astype(F32)
            for k in range(1, group):
                summed = summed + state_recv[k].astype(F32)
            state_all[me] = summed.astype(BF16)
            for k in range(group - 1):
                state_copy(1, k).start()
            step_copy.wait()
            g_step[...] = step_scr[0] + step_scr[1]
            reduce.finish()
            chain.finish(blocks)
            for k in range(group - 1):
                state_copy(1, k).wait()
            whole_state = jnp.concatenate([state_all[k].astype(F32) for k in range(group)], axis=0)
            g_state[...] = whole_state.T
        else:
            vec_out[...] = dp_vec[0]
            grad_outs[0][...] = stage[...]
            chain.finish(blocks)


def per_device(
    inputs,
    segments,
    cotangent,
    norm_gain,
    gate_proj,
    inner_proj,
    state_proj,
    step_proj,
    conv_inner,
    bias_inner,
    conv_state,
    bias_state,
    step_bias,
    decay_log,
    skip_gain,
    gate_norm,
    out_proj,
):
    length, half = inputs.shape
    row_count = lax.axis_size("row")
    col_count = lax.axis_size("col")
    col_at = lax.axis_index("col")
    width = half * row_count
    share, nh, pc = gate_proj.shape
    inner = nh * pc
    state_width = state_proj.shape[1]
    ns = state_width // 2
    conv_rows = inner + state_width
    gate_at = conv_rows + STEP_ROWS
    out_at = gate_at + inner
    rows = out_at + inner
    q = BLOCK_LEN
    blocks = length // q
    swap = [(0, 1), (1, 0)]
    dims = (nh, pc, ns, width)

    def channel_rows(w):
        return jnp.transpose(w, (1, 2, 0)).reshape(inner, share)

    gathers = lax.axis_size("dp") == 4 and share % 128 == 0
    parts = [
        channel_rows(inner_proj),
        state_proj,
        step_proj.T,
        channel_rows(gate_proj),
        channel_rows(out_proj),
    ]
    if not gathers:
        parts[1] = state_proj.T
        parts[2] = jnp.pad(step_proj.T, ((0, STEP_ROWS - nh), (0, 0)))
        stacked = jnp.concatenate(parts, axis=0).astype(BF16)
        parts = [lax.all_gather(stacked, "dp", axis=1, tiled=True)]
    gain_own = norm_gain[None, :]
    mesh_dims = (row_count, col_count, gathers)
    group = row_count * col_count

    chan_rows = jnp.concatenate(
        [
            conv_inner,
            bias_inner[None],
            gate_norm[None],
            jnp.zeros((2, nh, pc), F32),
        ],
        axis=0,
    ).reshape(8, inner)
    state_rows = jnp.concatenate(
        [conv_state, bias_state[None], jnp.zeros((3, state_width), F32)], axis=0
    )
    par_rows = jnp.concatenate([chan_rows, state_rows], axis=1)
    head_rows = jnp.pad(
        jnp.stack([step_bias, decay_log, skip_gain]), ((0, 5), (0, 128 - nh))
    )

    def token_block(order):
        return pl.BlockSpec((q, half), lambda i: (order(i), 0))

    def lane_block(count, order):
        return pl.BlockSpec((count, q), lambda i: (0, order(i)))

    def whole(*shape):
        return pl.BlockSpec(shape, lambda i: (0,) * len(shape), pipeline_mode=pl.Buffered(1))

    def up(i):
        return i

    def down(i):
        return blocks - 1 - i

    sds = jax.ShapeDtypeStruct
    forward = pl.pallas_call(
        functools.partial(forward_kernel, dims, mesh_dims),
        name="forward",
        grid=(blocks,),
        in_specs=[
            token_block(up),
            token_block(up),
            pl.BlockSpec(memory_space=pl.ANY),
            pl.BlockSpec(memory_space=pl.ANY),
            whole(1, half),
            lane_block(1, up),
            whole(8, conv_rows),
            whole(8, 128),
        ]
        + [whole(*part.shape) for part in parts],
        out_specs=[
            token_block(up),
            token_block(up),
            lane_block(conv_rows, up),
            lane_block(conv_rows, up),
            lane_block(inner, up),
            lane_block(STEP_ROWS, up),
            lane_block(inner, up),
            lane_block(inner, up),
            pl.BlockSpec((1, inner, ns), lambda i: (i, 0, 0)),
            lane_block(8, up),
            pl.BlockSpec((q, 128), lambda i: (i, 0)),
            whole(2 * blocks, q),
            pl.BlockSpec(memory_space=pl.ANY),
            pl.BlockSpec(memory_space=pl.ANY),
            pl.BlockSpec(memory_space=pl.ANY),
        ],
        out_shape=[
            sds((length, half), BF16),
            sds((length, half), BF16),
            sds((conv_rows, length), F32),
            sds((conv_rows, length), F32),
            sds((inner, length), F32),
            sds((STEP_ROWS, length), F32),
            sds((inner, length), F32),
            sds((inner, length), F32),
            sds((blocks, inner, ns), F32),
            sds((8, length), F32),
            sds((length, 128), F32),
            sds((2 * blocks, q), F32),
            sds((length, half), BF16),
            sds((length, half), BF16),
            sds((rows, width) if gathers else (16, 128), BF16),
        ],
        scratch_shapes=[
            pltpu.VMEM((conv_rows, 128), F32),
            pltpu.VMEM((1, 128), F32),
            pltpu.VMEM((inner, ns), F32),
            pltpu.VMEM((inner, q), F32),
            pltpu.VMEM((conv_rows, 128), F32),
            pltpu.VMEM((STEP_ROWS, 128), F32),
            pltpu.VMEM((blocks, q, half), BF16),
            pltpu.VMEM((blocks, q, half), BF16),
            pltpu.VMEM((1, half), F32),
            pltpu.VMEM((group, 2 * blocks, q), F32),
            pltpu.SemaphoreType.DMA((4, blocks + 1)),
            pltpu.SemaphoreType.DMA((blocks + 1,)),
            pltpu.SemaphoreType.DMA((2, group - 1)),
        ]
        + chain_scratch(blocks, q, half)
        + (
            [pltpu.VMEM((rows, width), BF16), pltpu.VMEM((rows, share), BF16)]
            + [pltpu.SemaphoreType.DMA((3,)) for _ in range(8)]
            if gathers
            else []
        ),
        compiler_params=pltpu.CompilerParams(
            vmem_limit_bytes=60 << 20, collective_id=1, has_side_effects=True
        ),
        cost_estimate=pl.CostEstimate(
            flops=2 * length * width * (out_at + 2 * inner),
            bytes_accessed=50 << 20,
            transcendentals=nh * length * q,
        ),
    )
    (
        normed_own,
        normed_sib,
        pre_vals,
        arg_vals,
        gate_vals,
        step_vals,
        mixed_vals,
        dng_vals,
        states,
        aux,
        scaling,
        stats,
        out_sum,
        c_sib,
        weights,
    ) = forward(
        inputs,
        cotangent,
        inputs,
        cotangent,
        gain_own,
        segments,
        par_rows,
        head_rows,
        *parts,
    )
    if not gathers:
        weights = parts[0]
    gate_scale = lax.rsqrt(stats[:blocks].reshape(length) / (H * P_SIZE) + EPSILON)
    plain = inputs.astype(F32)
    output = (plain + gate_scale[:, None] * out_sum.astype(F32)).astype(BF16)

    dma = pltpu.SemaphoreType.DMA
    split = 704
    if gathers:
        grad_shapes = [
            sds((inner, share), F32),
            sds((share, state_width), F32),
            sds((STEP_ROWS, share), F32),
            sds((inner, share), F32),
            sds((inner, share), F32),
        ]
        slice_rows = state_width // group
        reduce_scratch = [
            pltpu.VMEM((2, split, share), BF16),
            pltpu.VMEM((2, rows - split, share), BF16),
            pltpu.VMEM((split, share), BF16),
            pltpu.VMEM((rows - split, share), BF16),
            dma((3,)),
            dma((3,)),
            dma((3,)),
            dma((3,)),
            pltpu.VMEM((2, STEP_ROWS, share), F32),
            pltpu.VMEM((group, slice_rows, share), BF16),
            pltpu.VMEM((group, slice_rows, share), BF16),
            pltpu.VMEM((group, slice_rows, share), BF16),
            dma((2, 1)),
            dma((4, group - 1)),
        ]
    else:
        grad_shapes = [sds((rows, width), BF16)]
        reduce_scratch = []
    backward = pl.pallas_call(
        functools.partial(backward_kernel, dims, mesh_dims),
        name="backward",
        grid=(blocks,),
        in_specs=[
            token_block(down),
            token_block(down),
            token_block(down),
            token_block(down),
            whole(rows, width),
            lane_block(8, down),
            whole(8, conv_rows),
            whole(8, 128),
            whole(1, half),
            lane_block(conv_rows, down),
            lane_block(conv_rows, down),
            lane_block(inner, down),
            lane_block(STEP_ROWS, down),
            lane_block(inner, down),
            lane_block(inner, down),
            pl.BlockSpec((1, inner, ns), lambda i: (down(i), 0, 0)),
            whole(2 * blocks, q),
        ],
        out_specs=[
            pl.BlockSpec(memory_space=pl.ANY),
            whole(blocks, q),
            whole(8, conv_rows),
        ]
        + [whole(*shape.shape) for shape in grad_shapes],
        out_shape=[
            sds((length, half), BF16),
            sds((blocks, q), F32),
            sds((8, conv_rows), F32),
        ]
        + grad_shapes,
        scratch_shapes=[
            pltpu.VMEM((3, conv_rows, 128), F32),
            pltpu.VMEM((inner, ns), F32),
            pltpu.VMEM((rows, width), F32),
            pltpu.VMEM((5, conv_rows, 128), F32),
            pltpu.VMEM((2, inner, 128), F32),
            pltpu.VMEM((2, STEP_ROWS, 128), F32),
            pltpu.VMEM((2, 8, half), F32),
            pltpu.VMEM((q, 128), F32),
            pltpu.VMEM((inner, q), F32),
            pltpu.VMEM((out_at, q), BF16),
            pltpu.VMEM((conv_rows, 128), F32),
            pltpu.VMEM((STEP_ROWS, 128), F32),
            pltpu.VMEM((rows, width), BF16),
            pltpu.VMEM((group, 24, 256), F32),
            pltpu.VMEM((4, 8, conv_rows), F32),
            dma((2, group - 1)),
            dma((2, 3)),
        ]
        + chain_scratch(blocks, q, half)
        + reduce_scratch,
        compiler_params=pltpu.CompilerParams(
            vmem_limit_bytes=60 << 20, collective_id=2, has_side_effects=True
        ),
        cost_estimate=pl.CostEstimate(
            flops=4 * length * width * (out_at + inner),
            bytes_accessed=60 << 20,
            transcendentals=nh * length * q,
        ),
    )
    dn_total, token_dots, vectors, *grad_parts = backward(
        normed_own,
        normed_sib,
        cotangent,
        c_sib,
        weights,
        aux,
        par_rows,
        head_rows,
        gain_own,
        pre_vals,
        arg_vals,
        gate_vals,
        step_vals,
        mixed_vals,
        dng_vals,
        states,
        stats,
    )

    scale = scaling[:, 0:1]
    pull = token_dots.reshape(length)[:, None] * scale * scale / width
    grad_inputs = (
        cotangent.astype(F32) + scale * (dn_total.astype(F32) * gain_own) - plain * pull
    )
    if gathers:
        g_inner, g_state, g_step, g_gate, g_out = grad_parts
    else:
        grads = lax.psum_scatter(grad_parts[0], "dp", scatter_dimension=1, tiled=True)
        grads = grads.astype(F32)
        vectors = lax.psum(vectors, "dp")
        g_inner = grads[0:inner]
        g_state = lax.psum(grads[inner:conv_rows], ("row", "col")).T
        g_step = lax.psum(grads[conv_rows:gate_at], "row")
        g_gate = grads[gate_at:out_at]
        g_out = grads[out_at:]

    def feature_rows(w):
        return jnp.transpose(w.reshape(nh, pc, share), (2, 0, 1))

    channel_vecs = vectors[:, 0:inner].reshape(8, nh, pc)
    grad_norm = jnp.concatenate([vectors[6, inner:], vectors[7, : half - 2 * ns]])
    return (
        output,
        grad_inputs,
        grad_norm,
        feature_rows(g_gate),
        feature_rows(g_inner),
        g_state,
        g_step[:nh].T,
        channel_vecs[0:4],
        channel_vecs[4],
        vectors[0:4, inner:],
        vectors[4, inner:],
        vectors[5, inner : inner + nh],
        -vectors[5, inner + 128 : inner + 128 + nh] * jnp.exp(decay_log),
        jnp.sum(channel_vecs[6], axis=1),
        channel_vecs[5],
        feature_rows(g_out),
    )


def solution(mesh):
    return jax.shard_map(
        per_device,
        mesh=mesh,
        in_specs=(
            P("dp", "row"),
            P("dp", None),
            P("dp", "row"),
            P("row"),
            P("dp", "col", "row"),
            P("dp", "col", "row"),
            P("dp", None),
            P("dp", "col"),
            P(None, "col", "row"),
            P("col", "row"),
            P(),
            P(),
            P("col"),
            P("col"),
            P("col"),
            P("col", "row"),
            P("dp", "col", "row"),
        ),
        out_specs=(
            P("dp", "row"),
            P("dp", "row"),
            P("row"),
            P("dp", "col", "row"),
            P("dp", "col", "row"),
            P("dp", None),
            P("dp", "col"),
            P(None, "col", "row"),
            P("col", "row"),
            P(),
            P(),
            P("col"),
            P("col"),
            P("col"),
            P("col", "row"),
            P("dp", "col", "row"),
        ),
        check_vma=False,
    )
```

```python
import functools
import types

import jax
import jax.numpy as jnp
from jax import lax
from jax.experimental import pallas as pl
from jax.experimental.pallas import tpu as pltpu
from jax.sharding import PartitionSpec as P

H = 48
P_SIZE = 64
BLOCK_LEN = 256
EPSILON = 1e-05
NEG = -1e30
STEP_ROWS = 16
UNITS = 2
UP_AT = (0.45, None, None, None, None, None, None, 0.8)
DOWN_AT = (None, None, None, 0.22, 0.35, 0.5, 0.65, 0.78)
TURN_AT = (0.3, 0.6, 0.9)
AHEAD = 5
MODEL = (2.4, 3.7, 10.0, 8.2, 8.0, 0.5)
FORWARD_AT = (2, 4)
STOPS = (1, 1, 2, 3, 4, 7, 7, 8, 10)
DEPTH = 2
VMEM_LIMIT = 63 << 20
F32 = jnp.float32
BF16 = jnp.bfloat16
HIGHEST = lax.Precision.HIGHEST


def dot_nn(left, right, precision=None):
    return lax.dot_general(
        left, right, (((1,), (0,)), ((), ())), preferred_element_type=F32, precision=precision
    )


def dot_nt(left, right, precision=None):
    return lax.dot_general(
        left, right, (((1,), (1,)), ((), ())), preferred_element_type=F32, precision=precision
    )


def dot_tn(left, right):
    return lax.dot_general(left, right, (((0,), (0,)), ((), ())), preferred_element_type=F32)


def sigmoid(values):
    return 0.5 * jnp.tanh(0.5 * values) + 0.5


def softplus(values):
    return jnp.maximum(values, 0.0) + jnp.log1p(jnp.exp(-jnp.abs(values)))


def lane_fold(values):
    total = values[:, :128]
    for at in range(128, values.shape[1], 128):
        total = total + values[:, at : at + 128]
    return total


def columns_of(rows):
    padded = jnp.concatenate([rows, jnp.zeros((128 - rows.shape[0], rows.shape[1]), F32)], axis=0)
    return padded.T


def rows_of(ref):
    lanes = lax.broadcasted_iota(jnp.int32, ref.shape[1:], 1)
    total = jnp.zeros(ref.shape[1:], F32)
    for at in range(ref.shape[0]):
        total = jnp.where(lanes == at, jnp.sum(ref[at], axis=1, keepdims=True), total)
    if total.shape[0] % 128:
        total = jnp.concatenate([total, jnp.zeros((128 - total.shape[0], 128), F32)], axis=0)
    return total.T[0:8]


def load_columns(par_rows, head_rows, conv_scr, head_scr):
    conv_scr[...] = columns_of(par_rows[...])
    heads = columns_of(head_rows[...])[0:STEP_ROWS]
    lanes = lax.broadcasted_iota(jnp.int32, heads.shape, 1)
    head_scr[...] = jnp.where(lanes == 1, -jnp.exp(heads), heads)


def block_rows(dims, step_pre, hrow, aux):
    q = step_pre.shape[1]
    step_arg = step_pre + hrow[:, 0:1]
    step = softplus(step_arg)
    log_decay = step * hrow[:, 1:2]
    source = lax.broadcasted_iota(jnp.int32, (q, q), 0)
    target = lax.broadcasted_iota(jnp.int32, (q, q), 1)
    upper = (source <= target).astype(F32)
    cumul = dot_nn(log_decay, upper, HIGHEST)
    last = cumul[:, q - 1 : q]
    cols = columns_of(jnp.concatenate([cumul, aux], axis=0))
    return step_arg, step, cumul, last, cols


MESH = pl.DeviceIdType.MESH


def send(src, dst, sems, at, **device):
    return pltpu.make_async_remote_copy(
        src_ref=src,
        dst_ref=dst,
        send_sem=sems[0].at[at],
        recv_sem=sems[1].at[at],
        device_id=device,
        device_id_type=MESH,
    )


def group_peers(row_count, col_count):
    row_at, col_at = lax.axis_index("row"), lax.axis_index("col")
    return [
        dict(row=lax.rem(row_at + j, row_count), col=lax.rem(col_at + k, col_count))
        for k in range(col_count)
        for j in range(row_count)
        if (j, k) != (0, 0)
    ]


def greet(peers):
    barrier = pltpu.get_barrier_semaphore()
    for peer in peers:
        pl.semaphore_signal(barrier, inc=1, device_id=peer, device_id_type=MESH)


def greeted(peers):
    pl.semaphore_wait(pltpu.get_barrier_semaphore(), len(peers))


def add_low(left, right):
    return left + right


class Chain:
    def __init__(self, r, total, turn, first_rows, second_rows):
        self.total, self.turn = total, turn
        self.own, self.sib = r.ch_own, r.ch_sib
        self.first, self.pair, self.cross = r.ch_first, r.ch_pair, r.ch_cross
        self.slots = self.first.shape[0]
        self.out_slots = self.own.shape[0]
        self.sems = [(r.cs_send.at[k], r.cs_recv.at[k]) for k in range(4)]
        self.keep_sems = r.cs_keep
        self.free = r.ch_free
        self.first_rows, self.second_rows = first_rows, second_rows
        self.row_at, self.col_at = lax.axis_index("row"), lax.axis_index("col")
        self.is_outer = (self.col_at == 0) | (self.col_at == 3)
        self.inward = 1 + lax.div(self.col_at, 2)
        self.outward = 3 * lax.div(self.col_at, 2)

    def slot(self, m):
        return lax.rem(m, self.slots)

    def out_slot(self, m):
        return lax.rem(m, self.out_slots)

    def exchange(self, m):
        return send(
            self.sib.at[self.out_slot(m)],
            self.first.at[self.slot(m)],
            self.sems[0],
            self.slot(m),
            row=1 - self.row_at,
        )

    def to_inner(self, m):
        at = self.slot(m)
        return send(self.first.at[at], self.pair.at[at], self.sems[1], at, col=self.inward)

    def across(self, m):
        at = self.slot(m)
        return send(self.pair.at[at], self.cross.at[at], self.sems[2], at, col=3 - self.col_at)

    def to_outer(self, m, rows):
        at = self.slot(m)
        return send(self.cross.at[at], rows, self.sems[3], at, col=self.outward)

    def keep(self, m, rows):
        at = self.slot(m)
        return pltpu.make_async_copy(self.cross.at[at], rows, self.keep_sems.at[at])

    def credit(self, which, m, **device):
        @pl.when(m < self.total - self.slots)
        def _():
            pl.semaphore_signal(
                self.free.at[which], inc=1, device_id=device, device_id_type=MESH
            )

    def spend(self, which, m):
        @pl.when(m >= self.slots)
        def _():
            pl.semaphore_wait(self.free.at[which], 1)

    def begin(self, m, sib_part):
        @pl.when(m >= self.out_slots)
        def _():
            self.exchange(m - self.out_slots).wait_send()

        self.sib[self.out_slot(m)] = sib_part
        self.spend(0, m)
        self.exchange(m).start()

    def put_own(self, m, own_part):
        self.own[self.out_slot(m)] = own_part

    def stage_first(self, m):
        at = self.slot(m)
        self.exchange(m).wait_recv()
        self.first[at] = add_low(self.own[self.out_slot(m)], self.first[at])

        @pl.when(self.is_outer & (m < DEPTH))
        def _():
            self.to_inner(m).start()

    def stage_pair(self, m):
        at = self.slot(m)

        @pl.when(self.is_outer)
        def _():
            self.to_inner(m).wait_send()

            @pl.when(m + DEPTH < self.total)
            def _():
                self.spend(1, m + DEPTH)
                self.to_inner(m + DEPTH).start()

        @pl.when(~self.is_outer)
        def _():
            self.to_inner(m).wait_recv()
            self.pair[at] = add_low(self.first[at], self.pair[at])
            self.spend(2, m)
            self.across(m).start()

        self.credit(0, m, row=1 - self.row_at)

    def stage_cross(self, m):
        at = self.slot(m)

        @pl.when(~self.is_outer)
        def _():
            self.across(m).wait()
            self.cross[at] = add_low(self.pair[at], self.cross[at])
            self.credit(1, m, col=self.outward)

            @pl.when(m < self.turn)
            def _():
                self.keep(m, self.first_rows(m)).start()
                self.to_outer(m, self.first_rows(m)).start()

            @pl.when(m >= self.turn)
            def _():
                self.keep(m, self.second_rows(m)).start()
                self.to_outer(m, self.second_rows(m)).start()

    def stage_done(self, m):
        rows = self.first_rows(0)

        @pl.when(self.is_outer)
        def _():
            self.to_outer(m, rows).wait_recv()

        @pl.when(~self.is_outer)
        def _():
            self.keep(m, rows).wait()
            self.to_outer(m, rows).wait_send()
            self.credit(2, m, col=3 - self.col_at)


class Plan:
    def __init__(self, blocks, units, slots, up_us, scan_us, gap, down_us, hop, lag):
        steps = 2 * blocks
        self.total = steps * units
        self.per_step = len(UP_AT)
        self.points = steps * self.per_step
        hop = hop / units
        mixed = blocks - AHEAD
        lengths = [up_us + scan_us] * mixed + [up_us] * AHEAD + [down_us] * blocks
        starts = [0.0]
        for step in range(1, steps):
            pause = gap if step == blocks else 0.0
            starts.append(starts[-1] + lengths[step - 1] + pause)
        times = []
        for step in range(steps):
            if step < blocks:
                times += [None if at is None else starts[step] + at * up_us for at in UP_AT]
            else:
                times += [
                    None if at is None else starts[step] + at * down_us for at in DOWN_AT
                ]
        for which, at in enumerate(TURN_AT):
            times[self.per_step * blocks + which] = starts[blocks] - gap * (1.0 - at)
        ends = [at + up_us for at in starts[:blocks]]
        ends += [at + down_us for at in starts[blocks:]]

        def point_after(when):
            fits = [p for p, at in enumerate(times) if at is not None and at >= when]
            return fits[0] if fits else self.points

        def exact(point, when):
            known = point < len(times) and times[point] is not None
            return times[point] if known else when

        self.pair, self.cross, self.done = [], [], []
        one = two = three = 0.0
        for m in range(self.total):
            ready = ends[m // units] + 2.0
            if m >= DEPTH:
                ready = max(ready, taken[m - DEPTH])
            else:
                taken = taken if m else []
            one = max(one, ready) + hop
            point = point_after(one + lag)
            if m + DEPTH < self.total:
                point = max(point, self.per_step * ((m + DEPTH) // units + 1))
            if m + slots < self.total:
                point = min(point, self.per_step * ((m + slots) // units + 1) - 1)
            point = min(point, self.points)
            self.pair.append(point)
            taken_at = exact(point, one + lag)
            taken.append(taken_at)
            two = max(two, taken_at) + hop
            point = max(point_after(two + lag), point)
            self.cross.append(point)
            three = max(three, exact(point, two + lag)) + hop
            self.done.append(point_after(three + lag))
        for m in range(self.total - slots):
            self.done[m] = max(min(self.done[m], self.pair[m + slots]), self.cross[m])
        self.end = three + lag

    def span(self, table, which, step, steps):
        first = count = 0
        for point in sorted(set(table)):
            on = point // self.per_step
            if on in steps and point % self.per_step == which:
                hit = (step == on).astype(jnp.int32)
                first = first + table.index(point) * hit
                count = count + table.count(point) * hit
        return first, first + count

    def left(self, table):
        return sum(1 for at in table if at < self.points)


class Gather:
    def __init__(self, whole, sems, groups):
        self.whole, self.groups = whole, groups
        self.sems = sems
        at = lax.axis_index("dp")
        self.at = at
        self.near = at + 1 - 2 * lax.rem(at, 2)
        self.far = lax.rem(at + 2, 4)
        self.share = whole.shape[1] // 4

    def part(self, shard, lo, hi):
        return self.whole.at[
            lo:hi, pl.ds(pl.multiple_of(shard * self.share, 128), self.share)
        ]

    def direct(self, g, to_near):
        lo, _, hi = self.groups[g]
        return send(
            self.part(self.at, lo, hi),
            self.part(self.at, lo, hi),
            self.sems[0 if to_near else 1],
            g,
            dp=self.near if to_near else self.far,
        )

    def onward(self, g, from_near):
        lo, mid, hi = self.groups[g]
        lo, hi = (lo, mid) if from_near else (mid, hi)
        part = self.part(self.near if from_near else self.far, lo, hi)
        return send(
            part,
            part,
            self.sems[2 if from_near else 3],
            g,
            dp=self.far if from_near else self.near,
        )

    def start(self, g):
        self.direct(g, True).start()
        self.direct(g, False).start()

    def forward(self, g):
        for which in (True, False):
            self.direct(g, which).wait_recv()
            self.onward(g, which).start()

    def take(self, g):
        self.onward(g, True).wait_recv()
        self.onward(g, False).wait_recv()

    def finish(self):
        for g in range(len(self.groups)):
            for which in (True, False):
                self.direct(g, which).wait_send()
                self.onward(g, which).wait_send()


class Reduce:
    def __init__(self, acc, stage, bounds, bufs, sems):
        self.acc, self.stage = acc, stage
        self.halves = (bounds[0:2], bounds[1:3])
        self.bufs, self.sems = bufs, sems
        at = lax.axis_index("dp")
        self.at = at
        self.near = at + 1 - 2 * lax.rem(at, 2)
        self.far = lax.rem(at + 2, 4)
        self.share = acc.shape[1] // 4

    def cols(self, shard):
        return pl.ds(pl.multiple_of(shard * self.share, 128), self.share)

    def first(self, half, slot):
        lo, hi = self.halves[half]
        to = (self.near, self.far)[half]
        shard = to if slot == 0 else 3 - self.at
        return send(
            self.stage.at[lo:hi, self.cols(shard)],
            self.bufs[half].at[slot],
            self.sems[half],
            slot,
            dp=to,
        )

    def second(self, half):
        return send(
            self.bufs[half].at[1],
            self.bufs[2 + half],
            self.sems[half],
            2,
            dp=(self.far, self.near)[half],
        )

    def start(self):
        for slot in (1, 0):
            for half in range(2):
                self.first(half, slot).start()

    def middle(self):
        for half in range(2):
            lo, hi = self.halves[half]
            other = (self.far, self.near)[half]
            self.first(half, 1).wait_recv()
            self.bufs[half][1] = (
                self.acc[lo:hi, self.cols(other)] + self.bufs[half][1].astype(F32)
            ).astype(BF16)
            self.second(half).start()

    def end(self):
        for half in range(2):
            lo, hi = self.halves[half]
            self.first(half, 0).wait_recv()
            self.second(half).wait_recv()
            mine = self.cols(self.at)
            self.acc[lo:hi, mine] = (
                self.acc[lo:hi, mine]
                + self.bufs[half][0].astype(F32)
                + self.bufs[2 + half][...].astype(F32)
            )

    def finish(self):
        for half in range(2):
            self.first(half, 0).wait_send()
            self.first(half, 1).wait_send()
            self.second(half).wait_send()


def layer_kernel(cfg, plan, names, *refs):
    r = types.SimpleNamespace(**dict(zip(names, refs, strict=True)))
    nh, pc, ns, width = cfg.nh, cfg.pc, cfg.ns, cfg.width
    gathers, blocks, units = cfg.gathers, cfg.blocks, cfg.units
    inner = nh * pc
    conv_rows = inner + 2 * ns
    step_row = 2 * ns
    inner_at = step_row + STEP_ROWS
    gate_at = inner_at + inner
    out_at = gate_at + inner
    rows = out_at + inner
    q, half = r.x_own.shape
    hq = q // 2
    unit_rows = q // units
    inner_width = H * P_SIZE
    step_at = pl.program_id(0)
    scans, block_at = walk(step_at, blocks)
    goes_down = step_at >= 2 * blocks
    chain_step = jnp.where(goes_down, step_at - blocks, block_at)
    row_at, col_at, dp_at = (lax.axis_index(name) for name in ("row", "col", "dp"))
    own_at = pl.multiple_of(row_at * half, 128)
    sib_at = pl.multiple_of((1 - row_at) * half, 128)
    own_cols, sib_cols = pl.ds(own_at, half), pl.ds(sib_at, half)
    group = cfg.row_count * cfg.col_count
    me = row_at * cfg.col_count + col_at
    peers = group_peers(cfg.row_count, cfg.col_count)
    friends = [dict(dp=lax.rem(dp_at + k, 4)) for k in range(1, 4)] if gathers else []
    weights = r.weights

    def out_rows(m):
        return r.out_total.at[pl.ds(pl.multiple_of(m * unit_rows, unit_rows), unit_rows)]

    def dn_rows(m):
        at = (2 * blocks - 1 - lax.div(m, units)) * q + lax.rem(m, units) * unit_rows
        return r.dn_total.at[pl.ds(pl.multiple_of(at, unit_rows), unit_rows)]

    chain = Chain(r, plan.total, blocks * units, out_rows, dn_rows)

    def send_parts(sib_part, own_part):
        for u in range(units):
            lo = u * unit_rows
            chain.begin(chain_step * units + u, sib_part[lo : lo + unit_rows])
        own = own_part()
        for u in range(units):
            lo = u * unit_rows
            chain.put_own(chain_step * units + u, own[lo : lo + unit_rows].astype(BF16))
        return own

    def progress(which, steps):
        if which == 0:

            @pl.when(chain_step > 0)
            def _():
                for u in range(units):
                    chain.stage_first((chain_step - 1) * units + u)

        for table, stage in (
            (plan.done, chain.stage_done),
            (plan.pair, chain.stage_pair),
            (plan.cross, chain.stage_cross),
        ):

            def one(m, _, stage=stage):
                stage(m)
                return 0

            lo, hi = plan.span(table, which, chain_step, steps)
            if lo is not hi:
                lax.fori_loop(lo, hi, one, 0)

    up_steps, down_steps = range(blocks), range(blocks, 2 * blocks)

    def token_rows(ref, b):
        return ref.at[pl.ds(pl.multiple_of(b * q, q), q)]

    def swap(which, b):
        src, dst = ((r.x_any, r.x_scr), (r.c_any, r.c_scr))[which]
        sems = (r.swap_sems.at[2 * which], r.swap_sems.at[2 * which + 1])
        return send(token_rows(src, b), dst.at[b], sems, b, row=1 - row_at)

    gain_swap = send(
        r.gain_own,
        r.gain_sib,
        (r.swap_sems.at[0], r.swap_sems.at[1]),
        blocks,
        row=1 - row_at,
    )

    def stat_copy(k):
        sems = (r.stat_sems.at[0], r.stat_sems.at[1])
        return send(r.stats.at[me], r.stats.at[me], sems, k, **peers[k])

    if gathers:
        bounds = (
            (0, cfg.early_split, inner_at),
            (inner_at, inner_at + inner // 2, gate_at),
            (gate_at, gate_at + inner // 2, out_at),
            (out_at, out_at + inner // 2, rows),
        )
        sems = [(r.gather_sems.at[2 * k], r.gather_sems.at[2 * k + 1]) for k in range(4)]
        gather = Gather(weights, sems, bounds)
        early = Reduce(
            r.acc_w,
            weights,
            (0, cfg.early_split, inner_at),
            (r.ea_top, r.ea_low, r.ea_top_last, r.ea_low_last),
            [(r.ea_sems.at[2 * k], r.ea_sems.at[2 * k + 1]) for k in range(2)],
        )
        late = Reduce(
            r.acc_w,
            weights,
            (inner_at, (inner_at + rows) // 2, rows),
            (r.rs_top, r.rs_low, r.rs_top_last, r.rs_low_last),
            [(r.rs_sems.at[2 * k], r.rs_sems.at[2 * k + 1]) for k in range(2)],
        )
        share = width // 4
        mine = early.cols(dp_at)
        raw = (
            (r.inner_w, 0, inner, 0, share),
            (r.state_w, 0, share, share, 2 * ns),
            (r.gate_w, inner, inner, 0, share),
            (r.out_w, 2 * inner, inner, 0, share),
        )

        def raw_copy(k):
            src, lo, count, at, size = raw[k]
            return pltpu.make_async_copy(
                src, r.acc_w.at[lo : lo + count, at : at + size], r.raw_sems.at[k]
            )

        def raw_value(k):
            _, lo, count, at, size = raw[k]
            return r.acc_w[lo : lo + count, at : at + size]

    @pl.when(step_at == 0)
    def _():
        greet(peers + friends)
        if gathers:
            for k in range(len(raw)):
                raw_copy(k).start()
            for k in range(len(raw)):
                raw_copy(k).wait()
            step_rows = jnp.concatenate(
                [r.step_w[...], jnp.zeros((STEP_ROWS - nh, share), F32)], axis=0
            )
            weights[0:step_row, mine] = raw_value(1).T.astype(BF16)
            weights[step_row:inner_at, mine] = step_rows.astype(BF16)
            weights[inner_at:gate_at, mine] = raw_value(0).astype(BF16)
            weights[gate_at:out_at, mine] = raw_value(2).astype(BF16)
            weights[out_at:, mine] = raw_value(3).astype(BF16)
        greeted(peers + friends)
        if gathers:
            gather.start(0)
            gather.start(1)
        gain_swap.start()
        for b in range(blocks):
            swap(0, b).start()
            swap(1, b).start()
        load_columns(r.par_rows, r.head_rows, r.conv, r.head)
        for ref in (r.acc_w, r.state, r.after, r.acc_conv, r.acc_chan, r.acc_head):
            ref[...] = jnp.zeros_like(ref)
        for ref in (r.acc_norm, r.acc_dot, r.scale):
            ref[...] = jnp.zeros_like(ref)
        r.pre[:, 0:128] = jnp.zeros((conv_rows, 128), F32)
        r.prev_seg[...] = jnp.full_like(r.prev_seg, -1.0)
        gain_swap.wait_recv()
        if gathers:
            gather.forward(0)
            gather.forward(1)
            gather.start(2)
            gather.start(3)
            gather.take(0)
            gather.take(1)

    def scan_step():
        b = block_at
        here = pl.ds(pl.multiple_of(b * q, q), q)
        swap(0, b).wait_recv()
        xo = r.x_own[...].astype(F32)
        xs = r.x_scr[b].astype(F32)
        squares = jnp.sum(xo * xo, axis=1, keepdims=True) + jnp.sum(
            xs * xs, axis=1, keepdims=True
        )
        scaling = lax.rsqrt(squares / width + EPSILON)
        lanes = lax.broadcasted_iota(jnp.int32, r.scale.shape, 1)
        r.scale[...] = jnp.where(lanes == b, scaling, r.scale[...])
        no = (xo * scaling * r.gain_own[...]).astype(BF16)
        nsib = (xs * scaling * r.gain_sib[...]).astype(BF16)
        pre = dot_nt(weights[0:gate_at, own_cols], no) + dot_nt(weights[0:gate_at, sib_cols], nsib)
        values = jnp.concatenate([pre[inner_at:gate_at], pre[0:step_row]], axis=0)
        step_pre = pre[step_row:inner_at]
        r.pre[:, pl.ds(pl.multiple_of(b * q + 128, 128), q)] = values
        r.step[:, here] = step_pre
        seg = r.seg[...].astype(F32)
        seg_before = r.prev_seg[...]
        seg_joined = jnp.concatenate([seg_before, seg], axis=1)
        before, final = seg_before[:, 127:128], seg[:, q - 1 : q]
        aux = jnp.concatenate(
            [
                (seg_joined[:, 128 - offset : 128 - offset + q] == seg).astype(F32)
                for offset in range(1, 4)
            ]
            + [
                seg,
                (seg == before).astype(F32),
                (seg == final).astype(F32),
                jnp.broadcast_to((before == final).astype(F32), (1, q)),
                jnp.zeros((1, q), F32),
            ],
            axis=0,
        )
        r.prev_seg[...] = seg[:, q - 128 :]
        r.aux[:, here] = aux
        conv = r.conv[...]
        head = r.head[...]
        arg = conv_args(r, conv, aux, b, q)
        act = arg * sigmoid(arg)
        r.work[...] = act[0:inner]
        in_low = act[inner : inner + ns].astype(BF16)
        out_low = act[inner + ns :].astype(BF16)

        _, step, cumul, last, cols = block_rows(None, step_pre, head, aux)
        source = lax.broadcasted_iota(jnp.int32, (q, q), 0)
        target = lax.broadcasted_iota(jnp.int32, (q, q), 1)
        seg_col = cols[:, STEP_ROWS + 3 : STEP_ROWS + 4]
        bias = jnp.where((source <= target) & (seg_col == aux[3:4]), 0.0, NEG)
        pairs = dot_tn(in_low, out_low)
        entering = r.state[...]
        r.states[b] = entering
        from_state = dot_nn(entering.astype(BF16), out_low)
        reach = aux[4:5] * jnp.exp(cumul)
        tails = aux[5:6] * jnp.exp(last - cumul)
        keep = aux[6:7, 0:1] * jnp.exp(last)
        tail_parts = []
        for h in range(nh):
            lo = h * pc
            x_h = r.work[lo : lo + pc]
            u_h = (x_h * step[h : h + 1]).astype(BF16)
            tail_parts.append((x_h * (step[h : h + 1] * tails[h : h + 1])).astype(BF16))
            col = cols[:, h : h + 1]
            row = cumul[h : h + 1]
            top = (jnp.exp((row - col[:hq]) + bias[:hq]) * pairs[:hq]).astype(BF16)
            low = jnp.exp((row[:, hq:] - col[hq:]) + bias[hq:, hq:]) * pairs[hq:, hq:]
            y_top = dot_nn(u_h[:, :hq], top)
            y_low = dot_nn(u_h[:, hq:], low.astype(BF16))
            y_h = jnp.concatenate([y_top[:, :hq], y_top[:, hq:] + y_low], axis=1)
            y_h = y_h + from_state[lo : lo + pc] * reach[h : h + 1]
            r.mixed[lo : lo + pc, here] = y_h + head[h : h + 1, 2:3] * x_h
        contrib = dot_nt(jnp.concatenate(tail_parts, axis=0), in_low)
        for h in range(nh):
            lo = h * pc
            r.state[lo : lo + pc] = keep[h : h + 1] * entering[lo : lo + pc] + contrib[lo : lo + pc]

    def out_step():
        b = block_at
        here = pl.ds(pl.multiple_of(b * q, q), q)
        gain = r.conv[0:inner, 5:6]
        if gathers:

            @pl.when(step_at == AHEAD)
            def _():
                gather.take(2)

        no, nsib, _ = normed_block(b)
        gate = dot_nt(weights[gate_at:out_at, own_cols], no) + dot_nt(
            weights[gate_at:out_at, sib_cols], nsib
        )
        r.gate[:, here] = gate.astype(BF16)
        progress(0, up_steps)
        gated = r.mixed[:, here] * (gate * sigmoid(gate))
        squares_row = jnp.sum(gated * gated, axis=0, keepdims=True)
        weighted = gated * gain
        low = weighted.astype(BF16)
        if gathers:

            @pl.when(step_at == AHEAD)
            def _():
                gather.take(3)

        send_parts(
            dot_tn(low, weights[out_at:, sib_cols]).astype(BF16),
            lambda: dot_tn(low, weights[out_at:, own_cols]),
        )
        progress(7, up_steps)
        swap(1, b).wait_recv()
        dng = dot_nt(weights[out_at:, own_cols], r.c_own[...]) + dot_nt(
            weights[out_at:, sib_cols], r.c_scr[b]
        )
        r.dng[:, here] = dng.astype(BF16)
        r.stats[me, pl.ds(b, 1)] = squares_row
        r.stats[me, pl.ds(blocks + b, 1)] = jnp.sum(dng * weighted, axis=0, keepdims=True)

    def normed_block(b):
        lanes = lax.broadcasted_iota(jnp.int32, r.scale.shape, 1)
        scaling = jnp.sum(jnp.where(lanes == b, r.scale[...], 0.0), axis=1, keepdims=True)
        no = (r.x_own[...].astype(F32) * scaling * r.gain_own[...]).astype(BF16)
        nsib = (r.x_scr[b].astype(F32) * scaling * r.gain_sib[...]).astype(BF16)
        return no, nsib, lanes

    def backward_step():
        b = block_at
        here = pl.ds(pl.multiple_of(b * q, q), q)
        aux = r.aux[:, here]
        conv = r.conv[...]
        gain = conv[0:inner, 5:6]
        head = r.head[...]
        no, nsib, lanes = normed_block(b)
        arg = conv_args(r, conv, aux, b, q)
        sig_arg = sigmoid(arg)
        act = arg * sig_arg
        r.slope[...] = sig_arg * (1.0 + arg * (1.0 - sig_arg))
        x_all = act[0:inner]
        in_low = act[inner : inner + ns].astype(BF16)
        out_low = act[inner + ns :].astype(BF16)
        step_arg, step, cumul, last, cols = block_rows(None, r.step[:, here], head, aux)
        gate = r.gate[:, here].astype(F32)
        sig = sigmoid(gate)
        silu = gate * sig
        mixed = r.mixed[:, here]
        gated = mixed * silu

        for which in range(len(TURN_AT)):
            progress(which, down_steps)

        @pl.when(step_at == 2 * blocks)
        def _():
            for k in range(group - 1):
                stat_copy(k).wait()

        square_sum, gate_dot = jnp.zeros((1, q), F32), jnp.zeros((1, q), F32)
        for k in range(group):
            square_sum = square_sum + r.stats[k, pl.ds(b, 1)]
            gate_dot = gate_dot + r.stats[k, pl.ds(blocks + b, 1)]
        gate_scale = lax.rsqrt(square_sum / inner_width + EPSILON)
        pull = gate_scale * gate_scale * gate_scale * gate_dot / inner_width
        dng_scaled = r.dng[:, here].astype(F32) * gate_scale
        d_gated = gain * dng_scaled - gated * pull
        r.acc_chan[0] += lane_fold(dng_scaled * gated)
        normed_gate = (gated * (gate_scale * gain)).astype(BF16)
        r.acc_w[out_at:, own_cols] += dot_nn(normed_gate, r.c_own[...])
        r.acc_w[out_at:, sib_cols] += dot_nn(normed_gate, r.c_scr[b])
        grad_mixed = d_gated * silu
        r.low[gate_at:out_at] = (d_gated * mixed * (sig * (1.0 + gate * (1.0 - sig)))).astype(BF16)
        progress(3, down_steps)

        t_at = lax.broadcasted_iota(jnp.int32, (q, q), 0)
        s_at = lax.broadcasted_iota(jnp.int32, (q, q), 1)
        seg_col = cols[:, STEP_ROWS + 3 : STEP_ROWS + 4]
        bias = jnp.where((s_at <= t_at) & (seg_col == aux[3:4]), 0.0, NEG)
        pairs = dot_tn(out_low, in_low)
        reach = aux[4:5] * jnp.exp(cumul)
        tails = aux[5:6] * jnp.exp(last - cumul)
        keep = aux[6:7, 0:1] * jnp.exp(last)
        entering = r.states[b]

        @pl.when(step_at == 2 * blocks)
        def _():
            r.state[...] = jnp.zeros_like(r.state)

        d_next = r.state[...]
        from_next = dot_nn(d_next.astype(BF16), in_low)
        r.acc_chan[1] += lane_fold(grad_mixed * x_all)
        d_pairs_top = jnp.zeros((hq, hq), F32)
        d_pairs_low = jnp.zeros((hq, q), F32)
        reach_parts, tail_parts = [], []
        row_sums, col_sums, x_sums, tail_sums, carry_sums = [], [], [], [], []
        for h in range(nh):
            lo = h * pc
            x_h = x_all[lo : lo + pc]
            u_h = x_h * step[h : h + 1]
            u_low = u_h.astype(BF16)
            g_h = grad_mixed[lo : lo + pc]
            g_low = g_h.astype(BF16)
            col = cols[:, h : h + 1]
            row = cumul[h : h + 1]
            reach_parts.append((g_h * reach[h : h + 1]).astype(BF16))
            tail_parts.append((u_h * tails[h : h + 1]).astype(BF16))
            e_top = jnp.exp((col[:hq] - row[:, :hq]) + bias[:hq, :hq])
            e_low = jnp.exp((col[hq:] - row) + bias[hq:])
            m_top = (e_top * pairs[:hq, :hq]).astype(BF16)
            m_low = (e_low * pairs[hq:]).astype(BF16)
            dm_top = dot_tn(g_low[:, :hq], u_low[:, :hq])
            dm_low = dot_tn(g_low[:, hq:], u_low)
            d_pairs_top = d_pairs_top + dm_top * e_top
            d_pairs_low = d_pairs_low + dm_low * e_low
            du_top = dot_nn(g_low[:, :hq], m_top)
            du_low = dot_nn(g_low[:, hq:], m_low)
            du_local = jnp.concatenate([du_top + du_low[:, :hq], du_low[:, hq:]], axis=1)
            du_next = from_next[lo : lo + pc] * tails[h : h + 1]
            du = du_local + du_next
            skip = head[h : h + 1, 2:3]
            r.work[lo : lo + pc] = du * step[h : h + 1] + skip * g_h
            u_round = u_low.astype(F32)
            y_h = mixed[lo : lo + pc] - skip * x_h
            row_sums.append(jnp.sum(g_low.astype(F32) * y_h, axis=0, keepdims=True))
            next_sum = jnp.sum(u_round * du_next, axis=0, keepdims=True)
            col_sums.append(jnp.sum(u_round * du_local, axis=0, keepdims=True) + next_sum)
            tail_sums.append(next_sum)
            x_sums.append(jnp.sum(x_h * du, axis=0, keepdims=True))
            carry_sums.append(
                jnp.sum(entering[lo : lo + pc] * d_next[lo : lo + pc], axis=0, keepdims=True)
            )
            if h in (nh // 3, 2 * nh // 3):
                progress(3 + h // (nh // 3), down_steps)
        progress(6, down_steps)
        pad_rows = [jnp.zeros((STEP_ROWS - nh, q), F32)]
        row_sum = jnp.concatenate(row_sums + pad_rows, axis=0)
        col_sum = jnp.concatenate(col_sums + pad_rows, axis=0)
        tail_sum = jnp.concatenate(tail_sums + pad_rows, axis=0)
        x_sum = jnp.concatenate(x_sums + pad_rows, axis=0)
        carry = jnp.concatenate(carry_sums + [jnp.zeros((STEP_ROWS - nh, ns), F32)], axis=0)
        d_last = jnp.sum(tail_sum, axis=1, keepdims=True) + keep * jnp.sum(
            carry, axis=1, keepdims=True
        )
        later = (t_at >= s_at).astype(F32)
        d_log = dot_nn(row_sum - col_sum, later, HIGHEST) + d_last
        d_step = x_sum + head[:, 1:2] * d_log
        d_step_arg = d_step * sigmoid(step_arg)
        r.acc_head[0] += lane_fold(d_step_arg)
        r.acc_head[1] += lane_fold(step * d_log)
        r.low[step_row:inner_at] = d_step_arg.astype(BF16)

        g_reach = jnp.concatenate(reach_parts, axis=0)
        u_tail = jnp.concatenate(tail_parts, axis=0)
        d_top_low = d_pairs_top.astype(BF16)
        d_low_low = d_pairs_low.astype(BF16)
        d_out = dot_tn(entering.astype(BF16), g_reach)
        d_out = d_out + jnp.concatenate(
            [dot_nt(in_low[:, :hq], d_top_low), dot_nt(in_low, d_low_low)], axis=1
        )
        d_in = dot_tn(d_next.astype(BF16), u_tail) + dot_nn(out_low[:, hq:], d_low_low)
        d_in_top = dot_nn(out_low[:, :hq], d_top_low)
        d_in = jnp.concatenate([d_in[:, :hq] + d_in_top, d_in[:, hq:]], axis=1)
        d_enter = dot_nt(g_reach, out_low)
        for h in range(nh):
            lo = h * pc
            r.state[lo : lo + pc] = keep[h : h + 1] * d_next[lo : lo + pc] + d_enter[lo : lo + pc]

        err = jnp.concatenate([r.work[...], d_in, d_out], axis=0) * r.slope[...]
        values = r.pre[:, pl.ds(pl.multiple_of(b * q + 128, 128), q)]
        d_pre = conv[:, 3:4] * err
        r.acc_conv[3] += lane_fold(err * values)
        r.acc_conv[4] += lane_fold(err)
        for offset in range(1, 4):
            masked = err * aux[offset - 1 : offset]
            joined = jnp.concatenate([masked, r.after[offset - 1]], axis=1)
            shifted = joined[:, offset : offset + q]
            r.after[offset - 1] = masked[:, :128]
            d_pre = d_pre + conv[:, 3 - offset : 4 - offset] * shifted
            r.acc_conv[3 - offset] += lane_fold(shifted * values)
        r.low[inner_at:gate_at] = d_pre[0:inner].astype(BF16)
        r.low[0:step_row] = d_pre[inner:].astype(BF16)
        progress(7, down_steps)
        low = r.low[...]
        dn_sib = dot_tn(low, weights[0:out_at, sib_cols])
        dn_own = send_parts(
            dn_sib.astype(BF16), lambda: dot_tn(low, weights[0:out_at, own_cols])
        )
        token_dot = jnp.zeros((q, 1), F32)
        for which, (part, seen) in enumerate(((dn_own, no), (dn_sib, nsib))):
            product = part * seen.astype(F32)
            token_dot = token_dot + jnp.sum(product, axis=1, keepdims=True)
            r.acc_norm[which] += jnp.sum(product.reshape(q // 8, 8, half), axis=0)
        r.acc_dot[...] = jnp.where(lanes == b, token_dot, r.acc_dot[...])
        r.acc_w[0:out_at, own_cols] += dot_nn(low, no)
        r.acc_w[0:out_at, sib_cols] += dot_nn(low, nsib)

    def ending():
        lane = 2 * ns
        if gathers:
            weights[0:inner_at] = r.acc_w[0:inner_at].astype(BF16)
            early.start()
        else:
            r.grad_w[...] = r.acc_w[...].astype(BF16)
        for u in range(units):
            chain.stage_first((2 * blocks - 1) * units + u)
        zeros = jnp.zeros((1, 128), F32)
        conv_vec, chan_vec, head_vec = (
            rows_of(ref) for ref in (r.acc_conv, r.acc_chan, r.acc_head)
        )
        norm_vec = [jnp.sum(r.acc_norm[which], axis=0, keepdims=True) for which in range(2)]
        skip = chan_vec[1:2]
        r.group_vec[me] = jnp.concatenate(
            [
                conv_vec[0:5, inner:],
                skip[:, 0:lane],
                jnp.concatenate([skip[:, lane:], head_vec[0:1]], axis=1),
                jnp.concatenate([head_vec[1:2], zeros], axis=1),
                r.acc_dot[...].T[0:blocks],
            ]
            + [vec[:, at : at + lane] for vec in norm_vec for at in range(0, half, lane)]
            + [jnp.zeros((2, lane), F32)],
            axis=0,
        )

        def group_copy(k):
            sems = (r.group_sems.at[0], r.group_sems.at[1])
            return send(r.group_vec.at[me], r.group_vec.at[me], sems, k, **peers[k])

        for k in range(group - 1):
            group_copy(k).start()

        n_pair, n_cross, n_done = (
            plan.left(table) for table in (plan.pair, plan.cross, plan.done)
        )

        def late_cross(m, _):
            chain.stage_cross(m)
            return 0

        lax.fori_loop(n_cross, max(n_cross, n_pair - 1), late_cross, 0)
        n_cross = max(n_cross, n_pair - 1)
        drained = [n_pair]

        def drain(count=None):
            lo = drained[0]
            hi = plan.total + 1 if count is None else min(plan.total, n_pair + count)
            drained[0] = max(lo, hi)

            def one(m, _):
                @pl.when((m - chain.slots >= n_done) & (m < plan.total))
                def _():
                    chain.stage_done(m - chain.slots)

                @pl.when(m < plan.total)
                def _():
                    chain.stage_pair(m)

                @pl.when(m - 1 >= n_cross)
                def _():
                    chain.stage_cross(m - 1)

                return 0

            lax.fori_loop(lo, max(lo, hi), one, 0)

        if gathers:
            middle = (inner_at + rows) // 2
            for at, (lo, hi) in enumerate(((inner_at, middle), (middle, rows))):
                drain(cfg.stops[at])
                weights[lo:hi] = r.acc_w[lo:hi].astype(BF16)
            drain(cfg.stops[2])
            early.middle()
            late.start()
            drain(cfg.stops[3])
            early.end()
            slice_rows = 2 * ns // group
            for k in range(group):
                lo = k * slice_rows
                r.state_send[k] = r.acc_w[lo : lo + slice_rows, mine].astype(BF16)
            r.step_swap[0] = r.acc_w[step_row:inner_at, mine]

            def state_copy(phase, k):
                peer = peers[k]
                sems = (r.state_sems.at[2 * phase], r.state_sems.at[2 * phase + 1])
                to = peer["row"] * cfg.col_count + peer["col"]
                if phase == 0:
                    return send(r.state_send.at[to], r.state_recv.at[me], sems, k, **peer)
                return send(r.state_all.at[me], r.state_all.at[me], sems, k, **peer)

            step_copy = send(
                r.step_swap.at[0],
                r.step_swap.at[1],
                (r.state_sems.at[0], r.state_sems.at[1]),
                group - 1,
                row=1 - row_at,
            )
            for k in range(group - 1):
                state_copy(0, k).start()
            step_copy.start()
            r.state_recv[me] = r.state_send[me]
        drain(cfg.stops[4])

        for k in range(group - 1):
            group_copy(k).wait()
        shared = r.group_vec[0]
        for k in range(1, group):
            shared = shared + r.group_vec[k]
        by_row, by_head = jnp.zeros((3, lane), F32), jnp.zeros((3, lane), F32)
        for k in range(group):
            one = r.group_vec[k]
            same_row, same_col = (k // cfg.col_count) == row_at, (k % cfg.col_count) == col_at
            by_row = by_row + jnp.where(same_row, one[16:19], one[19:22])
            by_head = by_head + jnp.where(same_col, one[5:8], 0.0)
        scale = r.scale[...].T[0:blocks]
        square_sum = r.stats[0, 0:blocks]
        for k in range(1, group):
            square_sum = square_sum + r.stats[k, 0:blocks]
        gate_scale = lax.rsqrt(square_sum / inner_width + EPSILON)
        r.token_out[...] = jnp.concatenate(
            [scale, shared[8:16] * scale * scale / width, gate_scale], axis=0
        )
        norm_sum = jnp.concatenate([by_row[at : at + 1] for at in range(half // lane)], axis=1)
        norm_sum = norm_sum / r.gain_own[...]
        skip_sum = jnp.concatenate([by_head[0:1], by_head[1:2, 0:128]], axis=1)
        r.dp_vec[0] = jnp.concatenate(
            [
                jnp.concatenate([conv_vec[0:5, 0:inner], shared[0:5]], axis=1),
                jnp.concatenate([chan_vec[0:1], by_head[1:2, 128:], by_head[2:3, 0:128]], axis=1),
                jnp.concatenate([skip_sum, norm_sum[:, 0:lane]], axis=1),
                jnp.concatenate([norm_sum[:, lane:], zeros], axis=1),
            ],
            axis=0,
        )

        def dp_copy(k):
            sems = (r.dp_sems.at[0], r.dp_sems.at[1])
            return send(r.dp_vec.at[0], r.dp_vec.at[k], sems, k - 1, **friends[k - 1])

        if not gathers:
            r.vec_out[...] = r.dp_vec[0]
            drain()
        else:
            for k in range(1, 4):
                dp_copy(k).start()
            drain(cfg.stops[5])
            for k in range(group - 1):
                state_copy(0, k).wait()
            summed = r.state_recv[0].astype(F32)
            for k in range(1, group):
                summed = summed + r.state_recv[k].astype(F32)
            r.state_all[me] = summed.astype(BF16)
            for k in range(group - 1):
                state_copy(1, k).start()
            step_copy.wait()
            r.g_step[...] = r.step_swap[0] + r.step_swap[1]
            drain(cfg.stops[6])
            late.middle()
            drain(cfg.stops[7])
            for k in range(1, 4):
                dp_copy(k).wait()
            ordered = [lax.rem(dp_at - k + 4, 4) for k in range(4)]
            total = r.dp_vec[ordered[0]]
            for k in range(1, 4):
                total = total + r.dp_vec[ordered[k]]
            r.vec_out[...] = total
            drain(cfg.stops[8])
            late.end()
            r.g_inner[...] = r.acc_w[inner_at:gate_at, mine]
            r.g_gate[...] = r.acc_w[gate_at:out_at, mine]
            r.g_out[...] = r.acc_w[out_at:, mine]
            drain()
            for k in range(group - 1):
                state_copy(1, k).wait()
            whole_state = [r.state_all[k].astype(F32) for k in range(group)]
            r.g_state[...] = jnp.concatenate(whole_state, axis=0).T
            early.finish()
            late.finish()
        last_done = max(n_done, plan.total - chain.slots)

        def settle(m, _):
            chain.stage_done(m)
            return 0

        lax.fori_loop(last_done, plan.total, settle, 0)
        for m in range(plan.total - chain.out_slots, plan.total):
            chain.exchange(m).wait_send()

    @pl.when(scans == 1)
    def _():
        scan_step()

    if gathers:
        for g, at in ((2, FORWARD_AT[0]), (3, FORWARD_AT[1])):

            @pl.when(step_at == at)
            def _(g=g):
                gather.forward(g)

    @pl.when((scans == 0) & ~goes_down)
    def _():
        out_step()

    @pl.when(step_at == 2 * blocks - 1)
    def _():
        for k in range(group - 1):
            stat_copy(k).start()
        gain_swap.wait_send()
        for b in range(blocks):
            swap(0, b).wait_send()
            swap(1, b).wait_send()
        if gathers:
            gather.finish()

    @pl.when(step_at >= 2 * blocks)
    def _():
        backward_step()

    @pl.when(step_at == 3 * blocks - 1)
    def _():
        ending()


def walk(step, blocks):
    def flag(test):
        return test.astype(jnp.int32)

    mixed = blocks - AHEAD
    at = step - AHEAD
    early = flag(at < 0)
    late = flag(at >= 2 * mixed)
    down = flag(step >= 2 * blocks)
    turn = (1 - early) * (1 - late)
    ahead = at + early * AHEAD
    odd = turn * lax.rem(ahead, 2)
    pair = lax.div(ahead, 2)
    block = (
        early * step
        + turn * (pair + odd * AHEAD)
        + late * (1 - down) * (step - blocks)
        + down * (3 * blocks - 1 - step)
    )
    return early + odd, block


def conv_args(r, conv, aux, b, q):
    rows = conv.shape[0]
    joined = r.pre[:, pl.ds(pl.multiple_of(b * q, q), q + 128)]
    arg = conv[:, 4:5] + conv[:, 3:4] * joined[:, 128:]
    for offset in range(1, 4):
        arg = arg + conv[:, 3 - offset : 4 - offset] * (
            aux[offset - 1 : offset] * joined[:, 128 - offset : 128 - offset + q]
        )
    return arg


def per_device(
    inputs,
    segments,
    cotangent,
    norm_gain,
    gate_proj,
    inner_proj,
    state_proj,
    step_proj,
    conv_inner,
    bias_inner,
    conv_state,
    bias_state,
    step_bias,
    decay_log,
    skip_gain,
    gate_norm,
    out_proj,
):
    length, half = inputs.shape
    row_count = lax.axis_size("row")
    col_count = lax.axis_size("col")
    col_at = lax.axis_index("col")
    width = half * row_count
    share, nh, pc = gate_proj.shape
    inner = nh * pc
    state_width = state_proj.shape[1]
    ns = state_width // 2
    conv_rows = inner + state_width
    gate_at = conv_rows + STEP_ROWS
    out_at = gate_at + inner
    rows = out_at + inner
    q = BLOCK_LEN
    blocks = length // q

    def channel_rows(w):
        return jnp.transpose(w, (1, 2, 0)).reshape(inner, share)

    gathers = lax.axis_size("dp") == 4 and share % 128 == 0
    parts = [
        channel_rows(inner_proj),
        state_proj,
        step_proj.T,
        channel_rows(gate_proj),
        channel_rows(out_proj),
    ]
    if not gathers:
        step_rows = jnp.pad(step_proj.T, ((0, STEP_ROWS - nh), (0, 0)))
        parts = [state_proj.T, step_rows, parts[0], parts[3], parts[4]]
        stacked = jnp.concatenate(parts, axis=0).astype(BF16)
        parts = [lax.all_gather(stacked, "dp", axis=1, tiled=True)]
    gain_own = norm_gain[None, :]
    group = row_count * col_count

    chan_rows = jnp.concatenate(
        [
            conv_inner,
            bias_inner[None],
            gate_norm[None],
            jnp.zeros((2, nh, pc), F32),
        ],
        axis=0,
    ).reshape(8, inner)
    state_rows = jnp.concatenate(
        [conv_state, bias_state[None], jnp.zeros((3, state_width), F32)], axis=0
    )
    par_rows = jnp.concatenate([chan_rows, state_rows], axis=1)
    head_rows = jnp.pad(
        jnp.stack([step_bias, decay_log, skip_gain]), ((0, 5), (0, 128 - nh))
    )

    units = UNITS
    slots = blocks * units
    cfg = types.SimpleNamespace(
        nh=nh,
        pc=pc,
        ns=ns,
        width=width,
        row_count=row_count,
        col_count=col_count,
        gathers=gathers,
        blocks=blocks,
        units=units,
        early_split=144,
        stops=STOPS,
    )
    plan = Plan(blocks, units, slots, *MODEL)

    def fold(i):
        return walk(i, blocks)[1]

    def whole(*shape):
        return pl.BlockSpec(shape, lambda i: (0,) * len(shape), pipeline_mode=pl.Buffered(1))

    sds, dma, vmem = jax.ShapeDtypeStruct, pltpu.SemaphoreType.DMA, pltpu.VMEM
    anywhere = pl.BlockSpec(memory_space=pl.ANY)
    token_block = pl.BlockSpec((q, half), lambda i: (fold(i), 0))
    ins = {
        "x_own": (inputs, token_block),
        "c_own": (cotangent, token_block),
        "x_any": (inputs, anywhere),
        "c_any": (cotangent, anywhere),
        "gain_own": (gain_own, whole(1, half)),
        "seg": (segments, pl.BlockSpec((1, q), lambda i: (0, fold(i)))),
        "par_rows": (par_rows, whole(8, conv_rows)),
        "head_rows": (head_rows, whole(8, 128)),
    }
    outs = {
        "out_total": (sds((length, half), BF16), anywhere),
        "dn_total": (sds((length, half), BF16), anywhere),
        "token_out": (sds((3 * blocks, q), F32), whole(3 * blocks, q)),
        "vec_out": (sds((8, conv_rows), F32), whole(8, conv_rows)),
    }
    scratch = {
        "acc_w": vmem((rows, width), F32),
        "x_scr": vmem((blocks, q, half), BF16),
        "c_scr": vmem((blocks, q, half), BF16),
        "gain_sib": vmem((1, half), F32),
        "conv": vmem((conv_rows, 128), F32),
        "head": vmem((STEP_ROWS, 128), F32),
        "prev_seg": vmem((1, 128), F32),
        "pre": vmem((conv_rows, length + 128), F32),
        "step": vmem((STEP_ROWS, length), F32),
        "gate": vmem((inner, length), BF16),
        "mixed": vmem((inner, length), F32),
        "dng": vmem((inner, length), BF16),
        "aux": vmem((8, length), F32),
        "scale": vmem((q, 128), F32),
        "states": vmem((blocks, inner, ns), F32),
        "state": vmem((inner, ns), F32),
        "stats": vmem((group, 2 * blocks, q), F32),
        "work": vmem((inner, q), F32),
        "slope": vmem((conv_rows, q), F32),
        "low": vmem((out_at, q), BF16),
        "after": vmem((3, conv_rows, 128), F32),
        "acc_conv": vmem((5, conv_rows, 128), F32),
        "acc_chan": vmem((2, inner, 128), F32),
        "acc_head": vmem((2, STEP_ROWS, 128), F32),
        "acc_norm": vmem((2, 8, half), F32),
        "acc_dot": vmem((q, 128), F32),
        "group_vec": vmem((group, 24, 2 * ns), F32),
        "dp_vec": vmem((4, 8, conv_rows), F32),
        "ch_own": vmem((2 * units, q // units, half), BF16),
        "ch_sib": vmem((2 * units, q // units, half), BF16),
        "ch_first": vmem((slots, q // units, half), BF16),
        "ch_pair": vmem((slots, q // units, half), BF16),
        "ch_cross": vmem((slots, q // units, half), BF16),
        "cs_send": dma((4, slots)),
        "cs_recv": dma((4, slots)),
        "cs_keep": dma((slots,)),
        "ch_free": pltpu.SemaphoreType.REGULAR((3,)),
        "swap_sems": dma((4, blocks + 1)),
        "stat_sems": dma((2, group - 1)),
        "group_sems": dma((2, group - 1)),
        "dp_sems": dma((2, 3)),
    }
    if gathers:
        for name, part in zip(("inner_w", "state_w", "step_w", "gate_w", "out_w"), parts):
            ins[name] = (part, whole(*part.shape) if name == "step_w" else anywhere)
        grad_shape = sds((inner, share), F32)
        outs["g_inner"] = (grad_shape, whole(inner, share))
        outs["g_gate"] = (grad_shape, whole(inner, share))
        outs["g_out"] = (grad_shape, whole(inner, share))
        outs["g_state"] = (sds((share, state_width), F32), whole(share, state_width))
        outs["g_step"] = (sds((STEP_ROWS, share), F32), whole(STEP_ROWS, share))
        pieces = (group, state_width // group, share)
        early_rows = state_width + STEP_ROWS
        late_half = (rows - early_rows) // 2
        scratch.update(
            weights=vmem((rows, width), BF16),
            gather_sems=dma((8, 4)),
            raw_sems=dma((4,)),
            ea_top=vmem((2, cfg.early_split, share), BF16),
            ea_low=vmem((2, early_rows - cfg.early_split, share), BF16),
            ea_top_last=vmem((cfg.early_split, share), BF16),
            ea_low_last=vmem((early_rows - cfg.early_split, share), BF16),
            ea_sems=dma((4, 3)),
            rs_top=vmem((2, late_half, share), BF16),
            rs_low=vmem((2, late_half, share), BF16),
            rs_top_last=vmem((late_half, share), BF16),
            rs_low_last=vmem((late_half, share), BF16),
            rs_sems=dma((4, 3)),
            step_swap=vmem((2, STEP_ROWS, share), F32),
            state_send=vmem(pieces, BF16),
            state_recv=vmem(pieces, BF16),
            state_all=vmem(pieces, BF16),
            state_sems=dma((4, group)),
        )
    else:
        ins["weights"] = (parts[0], whole(rows, width))
        outs["grad_w"] = (sds((rows, width), BF16), whole(rows, width))
    names = (*ins, *outs, *scratch)
    results = pl.pallas_call(
        functools.partial(layer_kernel, cfg, plan, names),
        name="layer",
        grid=(3 * blocks,),
        in_specs=[spec for _, spec in ins.values()],
        out_specs=[spec for _, spec in outs.values()],
        out_shape=[shape for shape, _ in outs.values()],
        scratch_shapes=list(scratch.values()),
        compiler_params=pltpu.CompilerParams(
            vmem_limit_bytes=VMEM_LIMIT, collective_id=1, has_side_effects=True
        ),
        cost_estimate=pl.CostEstimate(
            flops=6 * length * width * rows,
            bytes_accessed=60 << 20,
            transcendentals=2 * nh * length * q,
        ),
    )(*(array for array, _ in ins.values()))
    made = types.SimpleNamespace(**dict(zip(outs, results, strict=True)))
    tokens = made.token_out.reshape(3, length)
    scale, pull, gate_scale = (tokens[k][:, None] for k in range(3))
    plain = inputs.astype(F32)
    output = (plain + gate_scale * made.out_total.astype(F32)).astype(BF16)
    weighted = made.dn_total.astype(F32) * gain_own
    grad_inputs = cotangent.astype(F32) + scale * weighted - plain * pull
    vectors = made.vec_out
    if gathers:
        g_inner, g_gate, g_out = made.g_inner, made.g_gate, made.g_out
        g_state, g_step = made.g_state, made.g_step
    else:
        grads = lax.psum_scatter(made.grad_w, "dp", scatter_dimension=1, tiled=True)
        grads = grads.astype(F32)
        vectors = lax.psum(vectors, "dp")
        g_state = lax.psum(grads[0:state_width], ("row", "col")).T
        g_step = lax.psum(grads[state_width : state_width + STEP_ROWS], "row")
        g_inner = grads[state_width + STEP_ROWS : gate_at]
        g_gate = grads[gate_at:out_at]
        g_out = grads[out_at:]

    def feature_rows(w):
        return jnp.transpose(w.reshape(nh, pc, share), (2, 0, 1))

    channel_vecs = vectors[:, 0:inner].reshape(8, nh, pc)
    grad_norm = jnp.concatenate([vectors[6, inner:], vectors[7, : half - 2 * ns]])
    return (
        output,
        grad_inputs,
        grad_norm,
        feature_rows(g_gate),
        feature_rows(g_inner),
        g_state,
        g_step[:nh].T,
        channel_vecs[0:4],
        channel_vecs[4],
        vectors[0:4, inner:],
        vectors[4, inner:],
        vectors[5, inner : inner + nh],
        -vectors[5, inner + 128 : inner + 128 + nh] * jnp.exp(decay_log),
        jnp.sum(channel_vecs[6], axis=1),
        channel_vecs[5],
        feature_rows(g_out),
    )


def solution(mesh):
    return jax.shard_map(
        per_device,
        mesh=mesh,
        in_specs=(
            P("dp", "row"),
            P("dp", None),
            P("dp", "row"),
            P("row"),
            P("dp", "col", "row"),
            P("dp", "col", "row"),
            P("dp", None),
            P("dp", "col"),
            P(None, "col", "row"),
            P("col", "row"),
            P(),
            P(),
            P("col"),
            P("col"),
            P("col"),
            P("col", "row"),
            P("dp", "col", "row"),
        ),
        out_specs=(
            P("dp", "row"),
            P("dp", "row"),
            P("row"),
            P("dp", "col", "row"),
            P("dp", "col", "row"),
            P("dp", None),
            P("dp", "col"),
            P(None, "col", "row"),
            P("col", "row"),
            P(),
            P(),
            P("col"),
            P("col"),
            P("col"),
            P("col", "row"),
            P("dp", "col", "row"),
        ),
        check_vma=False,
    )
```

```python
import functools
import types

import jax
import jax.numpy as jnp
from jax import lax
from jax.experimental import pallas as pl
from jax.experimental.pallas import tpu as pltpu
from jax.sharding import PartitionSpec as P

H = 48
P_SIZE = 64
BLOCK_LEN = 256
EPSILON = 1e-05
NEG = -1e30
STEP_ROWS = 16
UNITS = 2
UP_AT = (0.45, None, None, None, None, None, None, 0.8)
DOWN_AT = (None, None, None, 0.22, 0.35, 0.5, 0.65, 0.78)
TURN_AT = (0.3, 0.6, 0.9)
AHEAD = 5
MODEL = (2.4, 3.7, 10.0, 8.2, 8.0, 0.5)
FORWARD_AT = (2, 4)
STOPS = (1, 1, 2, 3, 4, 7, 7, 8, 10)
DEPTH = 2
VMEM_LIMIT = 63 << 20
FINISH_STEPS = 2
F32 = jnp.float32
BF16 = jnp.bfloat16
HIGHEST = lax.Precision.HIGHEST


def dot_nn(left, right, precision=None):
    return lax.dot_general(
        left, right, (((1,), (0,)), ((), ())), preferred_element_type=F32, precision=precision
    )


def dot_nt(left, right, precision=None):
    return lax.dot_general(
        left, right, (((1,), (1,)), ((), ())), preferred_element_type=F32, precision=precision
    )


def dot_tn(left, right):
    return lax.dot_general(left, right, (((0,), (0,)), ((), ())), preferred_element_type=F32)


def sigmoid(values):
    return 0.5 * jnp.tanh(0.5 * values) + 0.5


def softplus(values):
    return jnp.maximum(values, 0.0) + jnp.log1p(jnp.exp(-jnp.abs(values)))


def lane_fold(values):
    total = values[:, :128]
    for at in range(128, values.shape[1], 128):
        total = total + values[:, at : at + 128]
    return total


def columns_of(rows):
    padded = jnp.concatenate([rows, jnp.zeros((128 - rows.shape[0], rows.shape[1]), F32)], axis=0)
    return padded.T


def rows_of(ref):
    lanes = lax.broadcasted_iota(jnp.int32, ref.shape[1:], 1)
    total = jnp.zeros(ref.shape[1:], F32)
    for at in range(ref.shape[0]):
        total = jnp.where(lanes == at, jnp.sum(ref[at], axis=1, keepdims=True), total)
    if total.shape[0] % 128:
        total = jnp.concatenate([total, jnp.zeros((128 - total.shape[0], 128), F32)], axis=0)
    return total.T[0:8]


def pad_lanes(rows):
    return jnp.concatenate([rows, jnp.zeros((rows.shape[0], 128 - rows.shape[1]), F32)], axis=1)


def load_columns(r):
    nh, taps, pc = r.conv_in.shape
    rows = []
    for h in range(nh):
        rows += [r.conv_in[h], r.bias_in[h : h + 1], r.gate_gain[h : h + 1]]
        rows += [jnp.zeros((2, pc), F32)]
    cols = columns_of(pad_lanes(jnp.concatenate(rows, axis=0)))[0:pc]
    for h in range(nh):
        turned = pltpu.roll(cols, 128 - 8 * h, axis=1) if h else cols
        r.conv[h * pc : (h + 1) * pc] = turned
    state_rows = jnp.concatenate([r.conv_st[...], r.bias_st[...]], axis=0)
    r.conv[nh * pc :] = columns_of(state_rows)
    head_rows = jnp.concatenate([r.step_bias[...], r.decay_log[...], r.skip_gain[...]], axis=0)
    heads = columns_of(pad_lanes(head_rows))[0:STEP_ROWS]
    lanes = lax.broadcasted_iota(jnp.int32, heads.shape, 1)
    r.head[...] = jnp.where(lanes == 1, -jnp.exp(heads), heads)


def block_rows(dims, step_pre, hrow, aux):
    q = step_pre.shape[1]
    step_arg = step_pre + hrow[:, 0:1]
    step = softplus(step_arg)
    log_decay = step * hrow[:, 1:2]
    source = lax.broadcasted_iota(jnp.int32, (q, q), 0)
    target = lax.broadcasted_iota(jnp.int32, (q, q), 1)
    upper = (source <= target).astype(F32)
    cumul = dot_nn(log_decay, upper, HIGHEST)
    last = cumul[:, q - 1 : q]
    cols = columns_of(jnp.concatenate([cumul, aux], axis=0))
    return step_arg, step, cumul, last, cols


MESH = pl.DeviceIdType.MESH


def send(src, dst, sems, at, **device):
    return pltpu.make_async_remote_copy(
        src_ref=src,
        dst_ref=dst,
        send_sem=sems[0].at[at],
        recv_sem=sems[1].at[at],
        device_id=device,
        device_id_type=MESH,
    )


def group_peers(row_count, col_count):
    row_at, col_at = lax.axis_index("row"), lax.axis_index("col")
    return [
        dict(row=lax.rem(row_at + j, row_count), col=lax.rem(col_at + k, col_count))
        for k in range(col_count)
        for j in range(row_count)
        if (j, k) != (0, 0)
    ]


def greet(peers):
    barrier = pltpu.get_barrier_semaphore()
    for peer in peers:
        pl.semaphore_signal(barrier, inc=1, device_id=peer, device_id_type=MESH)


def greeted(peers):
    pl.semaphore_wait(pltpu.get_barrier_semaphore(), len(peers))


def add_low(left, right):
    return left + right


class Chain:
    def __init__(self, r, total, turn, first_rows, second_rows):
        self.total, self.turn = total, turn
        self.own, self.sib = r.ch_own, r.ch_sib
        self.first, self.pair, self.cross = r.ch_first, r.ch_pair, r.ch_cross
        self.slots = self.first.shape[0]
        self.out_slots = self.own.shape[0]
        self.sems = [(r.cs_send.at[k], r.cs_recv.at[k]) for k in range(3)]
        self.sems.append((r.cs_out.at[0], r.cs_out.at[1]))
        self.keep_sems = r.cs_keep
        self.free = r.ch_free
        self.first_rows, self.second_rows = first_rows, second_rows
        self.row_at, self.col_at = lax.axis_index("row"), lax.axis_index("col")
        self.is_outer = (self.col_at == 0) | (self.col_at == 3)
        self.inward = 1 + lax.div(self.col_at, 2)
        self.outward = 3 * lax.div(self.col_at, 2)

    def slot(self, m):
        return lax.rem(m, self.slots)

    def out_slot(self, m):
        return lax.rem(m, self.out_slots)

    def exchange(self, m):
        return send(
            self.sib.at[self.out_slot(m)],
            self.first.at[self.slot(m)],
            self.sems[0],
            self.slot(m),
            row=1 - self.row_at,
        )

    def to_inner(self, m):
        at = self.slot(m)
        return send(self.first.at[at], self.pair.at[at], self.sems[1], at, col=self.inward)

    def across(self, m):
        at = self.slot(m)
        return send(self.pair.at[at], self.cross.at[at], self.sems[2], at, col=3 - self.col_at)

    def to_outer(self, m, rows):
        return send(self.cross.at[self.slot(m)], rows, self.sems[3], m, col=self.outward)

    def keep(self, m, rows):
        at = self.slot(m)
        return pltpu.make_async_copy(self.cross.at[at], rows, self.keep_sems.at[at])

    def credit(self, which, m, **device):
        @pl.when(m < self.total - self.slots)
        def _():
            pl.semaphore_signal(
                self.free.at[which], inc=1, device_id=device, device_id_type=MESH
            )

    def spend(self, which, m):
        @pl.when(m >= self.slots)
        def _():
            pl.semaphore_wait(self.free.at[which], 1)

    def begin(self, m, sib_part):
        @pl.when(m >= self.out_slots)
        def _():
            self.exchange(m - self.out_slots).wait_send()

        self.sib[self.out_slot(m)] = sib_part
        self.spend(0, m)
        self.exchange(m).start()

    def put_own(self, m, own_part):
        self.own[self.out_slot(m)] = own_part

    def stage_first(self, m):
        at = self.slot(m)
        self.exchange(m).wait_recv()
        self.first[at] = add_low(self.own[self.out_slot(m)], self.first[at])

        @pl.when(self.is_outer & (m < DEPTH))
        def _():
            self.to_inner(m).start()

    def stage_pair(self, m):
        at = self.slot(m)

        @pl.when(self.is_outer)
        def _():
            self.to_inner(m).wait_send()

            @pl.when(m + DEPTH < self.total)
            def _():
                self.spend(1, m + DEPTH)
                self.to_inner(m + DEPTH).start()

        @pl.when(~self.is_outer)
        def _():
            self.to_inner(m).wait_recv()
            self.pair[at] = add_low(self.first[at], self.pair[at])
            self.spend(2, m)
            self.across(m).start()

        self.credit(0, m, row=1 - self.row_at)

    def stage_cross(self, m):
        at = self.slot(m)

        @pl.when(~self.is_outer)
        def _():
            self.across(m).wait()
            self.cross[at] = add_low(self.pair[at], self.cross[at])
            self.credit(1, m, col=self.outward)

            @pl.when(m < self.turn)
            def _():
                self.keep(m, self.first_rows(m)).start()
                self.to_outer(m, self.first_rows(m)).start()

            @pl.when(m >= self.turn)
            def _():
                self.keep(m, self.second_rows(m)).start()
                self.to_outer(m, self.second_rows(m)).start()

    def stage_done(self, m):
        @pl.when(~self.is_outer)
        def _():
            rows = self.first_rows(0)
            self.keep(m, rows).wait()
            self.to_outer(m, rows).wait_send()
            self.credit(2, m, col=3 - self.col_at)

    def totals(self):
        @pl.when(self.is_outer)
        def _():
            def one(m, _):
                self.to_outer(m, self.first_rows(0)).wait_recv()
                return 0

            lax.fori_loop(0, self.total, one, 0)


class Plan:
    def __init__(self, blocks, units, slots, up_us, scan_us, gap, down_us, hop, lag):
        steps = 2 * blocks
        self.total = steps * units
        self.per_step = len(UP_AT)
        self.points = steps * self.per_step
        hop = hop / units
        mixed = blocks - AHEAD
        lengths = [up_us + scan_us] * mixed + [up_us] * AHEAD + [down_us] * blocks
        starts = [0.0]
        for step in range(1, steps):
            pause = gap if step == blocks else 0.0
            starts.append(starts[-1] + lengths[step - 1] + pause)
        times = []
        for step in range(steps):
            if step < blocks:
                times += [None if at is None else starts[step] + at * up_us for at in UP_AT]
            else:
                times += [
                    None if at is None else starts[step] + at * down_us for at in DOWN_AT
                ]
        for which, at in enumerate(TURN_AT):
            times[self.per_step * blocks + which] = starts[blocks] - gap * (1.0 - at)
        ends = [at + up_us for at in starts[:blocks]]
        ends += [at + down_us for at in starts[blocks:]]

        def point_after(when):
            fits = [p for p, at in enumerate(times) if at is not None and at >= when]
            return fits[0] if fits else self.points

        def exact(point, when):
            known = point < len(times) and times[point] is not None
            return times[point] if known else when

        self.pair, self.cross, self.done = [], [], []
        one = two = three = 0.0
        for m in range(self.total):
            ready = ends[m // units] + 2.0
            if m >= DEPTH:
                ready = max(ready, taken[m - DEPTH])
            else:
                taken = taken if m else []
            one = max(one, ready) + hop
            point = point_after(one + lag)
            if m + DEPTH < self.total:
                point = max(point, self.per_step * ((m + DEPTH) // units + 1))
            if m + slots < self.total:
                point = min(point, self.per_step * ((m + slots) // units + 1) - 1)
            point = min(point, self.points)
            self.pair.append(point)
            taken_at = exact(point, one + lag)
            taken.append(taken_at)
            two = max(two, taken_at) + hop
            point = max(point_after(two + lag), point)
            self.cross.append(point)
            three = max(three, exact(point, two + lag)) + hop
            self.done.append(point_after(three + lag))
        for m in range(self.total - slots):
            self.done[m] = max(min(self.done[m], self.pair[m + slots]), self.cross[m])
        self.end = three + lag

    def span(self, table, which, step, steps):
        first = count = 0
        for point in sorted(set(table)):
            on = point // self.per_step
            if on in steps and point % self.per_step == which:
                hit = (step == on).astype(jnp.int32)
                first = first + table.index(point) * hit
                count = count + table.count(point) * hit
        return first, first + count

    def left(self, table):
        return sum(1 for at in table if at < self.points)


class Gather:
    def __init__(self, whole, sems, groups):
        self.whole, self.groups = whole, groups
        self.sems = sems
        at = lax.axis_index("dp")
        self.at = at
        self.near = at + 1 - 2 * lax.rem(at, 2)
        self.far = lax.rem(at + 2, 4)
        self.share = whole.shape[1] // 4

    def part(self, shard, lo, hi):
        return self.whole.at[
            lo:hi, pl.ds(pl.multiple_of(shard * self.share, 128), self.share)
        ]

    def direct(self, g, to_near):
        lo, _, hi = self.groups[g]
        return send(
            self.part(self.at, lo, hi),
            self.part(self.at, lo, hi),
            self.sems[0 if to_near else 1],
            g,
            dp=self.near if to_near else self.far,
        )

    def onward(self, g, from_near):
        lo, mid, hi = self.groups[g]
        lo, hi = (lo, mid) if from_near else (mid, hi)
        part = self.part(self.near if from_near else self.far, lo, hi)
        return send(
            part,
            part,
            self.sems[2 if from_near else 3],
            g,
            dp=self.far if from_near else self.near,
        )

    def start(self, g):
        self.direct(g, True).start()
        self.direct(g, False).start()

    def forward(self, g):
        for which in (True, False):
            self.direct(g, which).wait_recv()
            self.onward(g, which).start()

    def take(self, g):
        self.onward(g, True).wait_recv()
        self.onward(g, False).wait_recv()

    def finish(self):
        for g in range(len(self.groups)):
            for which in (True, False):
                self.direct(g, which).wait_send()
                self.onward(g, which).wait_send()


class Reduce:
    def __init__(self, acc, stage, bounds, bufs, sems):
        self.acc, self.stage = acc, stage
        self.halves = (bounds[0:2], bounds[1:3])
        self.bufs, self.sems = bufs, sems
        at = lax.axis_index("dp")
        self.at = at
        self.near = at + 1 - 2 * lax.rem(at, 2)
        self.far = lax.rem(at + 2, 4)
        self.share = acc.shape[1] // 4

    def cols(self, shard):
        return pl.ds(pl.multiple_of(shard * self.share, 128), self.share)

    def first(self, half, slot):
        lo, hi = self.halves[half]
        to = (self.near, self.far)[half]
        shard = to if slot == 0 else 3 - self.at
        return send(
            self.stage.at[lo:hi, self.cols(shard)],
            self.bufs[half].at[slot],
            self.sems[half],
            slot,
            dp=to,
        )

    def second(self, half):
        return send(
            self.bufs[half].at[1],
            self.bufs[2 + half],
            self.sems[half],
            2,
            dp=(self.far, self.near)[half],
        )

    def start(self):
        for slot in (1, 0):
            for half in range(2):
                self.first(half, slot).start()

    def middle(self):
        for half in range(2):
            lo, hi = self.halves[half]
            other = (self.far, self.near)[half]
            self.first(half, 1).wait_recv()
            self.bufs[half][1] = (
                self.acc[lo:hi, self.cols(other)] + self.bufs[half][1].astype(F32)
            ).astype(BF16)
            self.second(half).start()

    def end(self):
        for half in range(2):
            lo, hi = self.halves[half]
            self.first(half, 0).wait_recv()
            self.second(half).wait_recv()
            mine = self.cols(self.at)
            self.acc[lo:hi, mine] = (
                self.acc[lo:hi, mine]
                + self.bufs[half][0].astype(F32)
                + self.bufs[2 + half][...].astype(F32)
            )

    def finish(self):
        for half in range(2):
            self.first(half, 0).wait_send()
            self.first(half, 1).wait_send()
            self.second(half).wait_send()


def layer_kernel(cfg, plan, names, *refs):
    r = types.SimpleNamespace(**dict(zip(names, refs, strict=True)))
    nh, pc, ns, width = cfg.nh, cfg.pc, cfg.ns, cfg.width
    gathers, blocks, units = cfg.gathers, cfg.blocks, cfg.units
    inner = nh * pc
    conv_rows = inner + 2 * ns
    step_row = 2 * ns
    inner_at = step_row + STEP_ROWS
    gate_at = inner_at + inner
    out_at = gate_at + inner
    rows = out_at + inner
    q, half = r.x_own.shape
    hq = q // 2
    unit_rows = q // units
    inner_width = H * P_SIZE
    step_at = pl.program_id(0)
    scans, block_at = walk(step_at, blocks)
    goes_down = step_at >= 2 * blocks
    chain_step = jnp.where(goes_down, step_at - blocks, block_at)
    row_at, col_at, dp_at = (lax.axis_index(name) for name in ("row", "col", "dp"))
    own_at = pl.multiple_of(row_at * half, 128)
    sib_at = pl.multiple_of((1 - row_at) * half, 128)
    own_cols, sib_cols = pl.ds(own_at, half), pl.ds(sib_at, half)
    group = cfg.row_count * cfg.col_count
    me = row_at * cfg.col_count + col_at
    peers = group_peers(cfg.row_count, cfg.col_count)
    friends = [dict(dp=lax.rem(dp_at + k, 4)) for k in range(1, 4)] if gathers else []
    weights = r.weights

    def out_rows(m):
        return r.out_total.at[pl.ds(pl.multiple_of(m * unit_rows, unit_rows), unit_rows)]

    def dn_rows(m):
        at = (2 * blocks - 1 - lax.div(m, units)) * q + lax.rem(m, units) * unit_rows
        return r.dn_total.at[pl.ds(pl.multiple_of(at, unit_rows), unit_rows)]

    chain = Chain(r, plan.total, blocks * units, out_rows, dn_rows)

    def send_parts(sib_part, own_part):
        for u in range(units):
            lo = u * unit_rows
            chain.begin(chain_step * units + u, sib_part[lo : lo + unit_rows])
        own = own_part()
        for u in range(units):
            lo = u * unit_rows
            chain.put_own(chain_step * units + u, own[lo : lo + unit_rows].astype(BF16))
        return own

    def progress(which, steps):
        if which == 0:

            @pl.when(chain_step > 0)
            def _():
                for u in range(units):
                    chain.stage_first((chain_step - 1) * units + u)

        for table, stage in (
            (plan.done, chain.stage_done),
            (plan.pair, chain.stage_pair),
            (plan.cross, chain.stage_cross),
        ):

            def one(m, _, stage=stage):
                stage(m)
                return 0

            lo, hi = plan.span(table, which, chain_step, steps)
            if lo is not hi:
                lax.fori_loop(lo, hi, one, 0)

    up_steps, down_steps = range(blocks), range(blocks, 2 * blocks)

    def token_rows(ref, b):
        return ref.at[pl.ds(pl.multiple_of(b * q, q), q)]

    def swap(which, b):
        src, dst = ((r.x_any, r.x_scr), (r.c_any, r.c_scr))[which]
        sems = (r.swap_sems.at[2 * which], r.swap_sems.at[2 * which + 1])
        return send(token_rows(src, b), dst.at[b], sems, b, row=1 - row_at)

    gain_swap = send(
        r.gain_own,
        r.gain_sib,
        (r.swap_sems.at[0], r.swap_sems.at[1]),
        blocks,
        row=1 - row_at,
    )

    def stat_copy(k):
        sems = (r.stat_sems.at[0], r.stat_sems.at[1])
        return send(r.stats.at[me], r.stats.at[me], sems, k, **peers[k])

    if gathers:
        bounds = (
            (0, cfg.early_split, inner_at),
            (inner_at, inner_at + inner // 2, gate_at),
            (gate_at, gate_at + inner // 2, out_at),
            (out_at, out_at + inner // 2, rows),
        )
        sems = [(r.gather_sems.at[2 * k], r.gather_sems.at[2 * k + 1]) for k in range(4)]
        gather = Gather(weights, sems, bounds)
        early = Reduce(
            r.acc_w,
            weights,
            (0, cfg.early_split, inner_at),
            (r.ea_top, r.ea_low, r.ea_top_last, r.ea_low_last),
            [(r.ea_sems.at[2 * k], r.ea_sems.at[2 * k + 1]) for k in range(2)],
        )
        late = Reduce(
            r.acc_w,
            weights,
            (inner_at, (inner_at + rows) // 2, rows),
            (r.rs_top, r.rs_low, r.rs_top_last, r.rs_low_last),
            [(r.rs_sems.at[2 * k], r.rs_sems.at[2 * k + 1]) for k in range(2)],
        )
        share = width // 4
        mine = early.cols(dp_at)
        raw = (
            (r.inner_w, 0, inner, 0, share),
            (r.state_w, 0, share, share, 2 * ns),
            (r.gate_w, inner, inner, 0, share),
            (r.out_w, 2 * inner, inner, 0, share),
        )

        def raw_copy(k):
            src, lo, count, at, size = raw[k]
            return pltpu.make_async_copy(
                src, r.acc_w.at[lo : lo + count, at : at + size], r.raw_sems.at[k]
            )

        def raw_value(k):
            _, lo, count, at, size = raw[k]
            return r.acc_w[lo : lo + count, at : at + size]

    @pl.when(step_at == 0)
    def _():
        greet(peers + friends)
        if gathers:
            for k in range(len(raw)):
                raw_copy(k).start()
            for k in range(len(raw)):
                raw_copy(k).wait()
            step_rows = jnp.concatenate(
                [r.step_w[...], jnp.zeros((STEP_ROWS - nh, share), F32)], axis=0
            )
            weights[0:step_row, mine] = raw_value(1).T.astype(BF16)
            weights[step_row:inner_at, mine] = step_rows.astype(BF16)
            weights[inner_at:gate_at, mine] = raw_value(0).astype(BF16)
            weights[gate_at:out_at, mine] = raw_value(2).astype(BF16)
            weights[out_at:, mine] = raw_value(3).astype(BF16)
        greeted(peers + friends)
        if gathers:
            gather.start(0)
            gather.start(1)
        gain_swap.start()
        for b in range(blocks):
            swap(0, b).start()
            swap(1, b).start()
        load_columns(r)
        for ref in (r.acc_w, r.state, r.after, r.acc_conv, r.acc_chan, r.acc_head):
            ref[...] = jnp.zeros_like(ref)
        for ref in (r.acc_norm, r.acc_dot, r.scale):
            ref[...] = jnp.zeros_like(ref)
        r.pre[:, 0:128] = jnp.zeros((conv_rows, 128), F32)
        r.prev_seg[...] = jnp.full_like(r.prev_seg, -1.0)
        gain_swap.wait_recv()
        if gathers:
            gather.forward(0)
            gather.forward(1)
            gather.start(2)
            gather.start(3)
            gather.take(0)
            gather.take(1)

    def scan_step():
        b = block_at
        here = pl.ds(pl.multiple_of(b * q, q), q)
        swap(0, b).wait_recv()
        xo = r.x_own[...].astype(F32)
        xs = r.x_scr[b].astype(F32)
        squares = jnp.sum(xo * xo, axis=1, keepdims=True) + jnp.sum(
            xs * xs, axis=1, keepdims=True
        )
        scaling = lax.rsqrt(squares / width + EPSILON)
        lanes = lax.broadcasted_iota(jnp.int32, r.scale.shape, 1)
        r.scale[...] = jnp.where(lanes == b, scaling, r.scale[...])
        no = (xo * scaling * r.gain_own[...]).astype(BF16)
        nsib = (xs * scaling * r.gain_sib[...]).astype(BF16)
        pre = dot_nt(weights[0:gate_at, own_cols], no) + dot_nt(weights[0:gate_at, sib_cols], nsib)
        values = jnp.concatenate([pre[inner_at:gate_at], pre[0:step_row]], axis=0)
        step_pre = pre[step_row:inner_at]
        r.pre[:, pl.ds(pl.multiple_of(b * q + 128, 128), q)] = values
        r.step[:, here] = step_pre
        seg = r.seg[...].astype(F32)
        seg_before = r.prev_seg[...]
        seg_joined = jnp.concatenate([seg_before, seg], axis=1)
        before, final = seg_before[:, 127:128], seg[:, q - 1 : q]
        aux = jnp.concatenate(
            [
                (seg_joined[:, 128 - offset : 128 - offset + q] == seg).astype(F32)
                for offset in range(1, 4)
            ]
            + [
                seg,
                (seg == before).astype(F32),
                (seg == final).astype(F32),
                jnp.broadcast_to((before == final).astype(F32), (1, q)),
                jnp.zeros((1, q), F32),
            ],
            axis=0,
        )
        r.prev_seg[...] = seg[:, q - 128 :]
        r.aux[:, here] = aux
        conv = r.conv[...]
        head = r.head[...]
        arg = conv_args(r, conv, aux, b, q)
        act = arg * sigmoid(arg)
        r.work[...] = act[0:inner]
        in_low = act[inner : inner + ns].astype(BF16)
        out_low = act[inner + ns :].astype(BF16)

        _, step, cumul, last, cols = block_rows(None, step_pre, head, aux)
        source = lax.broadcasted_iota(jnp.int32, (q, q), 0)
        target = lax.broadcasted_iota(jnp.int32, (q, q), 1)
        seg_col = cols[:, STEP_ROWS + 3 : STEP_ROWS + 4]
        bias = jnp.where((source <= target) & (seg_col == aux[3:4]), 0.0, NEG)
        pairs = dot_tn(in_low, out_low)
        entering = r.state[...]
        r.states[b] = entering
        from_state = dot_nn(entering.astype(BF16), out_low)
        reach = aux[4:5] * jnp.exp(cumul)
        tails = aux[5:6] * jnp.exp(last - cumul)
        keep = aux[6:7, 0:1] * jnp.exp(last)
        tail_parts = []
        for h in range(nh):
            lo = h * pc
            x_h = r.work[lo : lo + pc]
            u_h = (x_h * step[h : h + 1]).astype(BF16)
            tail_parts.append((x_h * (step[h : h + 1] * tails[h : h + 1])).astype(BF16))
            col = cols[:, h : h + 1]
            row = cumul[h : h + 1]
            top = (jnp.exp((row - col[:hq]) + bias[:hq]) * pairs[:hq]).astype(BF16)
            low = jnp.exp((row[:, hq:] - col[hq:]) + bias[hq:, hq:]) * pairs[hq:, hq:]
            y_top = dot_nn(u_h[:, :hq], top)
            y_low = dot_nn(u_h[:, hq:], low.astype(BF16))
            y_h = jnp.concatenate([y_top[:, :hq], y_top[:, hq:] + y_low], axis=1)
            y_h = y_h + from_state[lo : lo + pc] * reach[h : h + 1]
            r.mixed[lo : lo + pc, here] = y_h + head[h : h + 1, 2:3] * x_h
        contrib = dot_nt(jnp.concatenate(tail_parts, axis=0), in_low)
        for h in range(nh):
            lo = h * pc
            r.state[lo : lo + pc] = keep[h : h + 1] * entering[lo : lo + pc] + contrib[lo : lo + pc]

    def out_step():
        b = block_at
        here = pl.ds(pl.multiple_of(b * q, q), q)
        gain = r.conv[0:inner, 5:6]
        if gathers:

            @pl.when(step_at == AHEAD)
            def _():
                gather.take(2)

        no, nsib, _ = normed_block(b)
        gate = dot_nt(weights[gate_at:out_at, own_cols], no) + dot_nt(
            weights[gate_at:out_at, sib_cols], nsib
        )
        r.gate[:, here] = gate.astype(BF16)
        progress(0, up_steps)
        gated = r.mixed[:, here] * (gate * sigmoid(gate))
        squares_row = jnp.sum(gated * gated, axis=0, keepdims=True)
        weighted = gated * gain
        low = weighted.astype(BF16)
        if gathers:

            @pl.when(step_at == AHEAD)
            def _():
                gather.take(3)

        send_parts(
            dot_tn(low, weights[out_at:, sib_cols]).astype(BF16),
            lambda: dot_tn(low, weights[out_at:, own_cols]),
        )
        progress(7, up_steps)
        swap(1, b).wait_recv()
        dng = dot_nt(weights[out_at:, own_cols], r.c_own[...]) + dot_nt(
            weights[out_at:, sib_cols], r.c_scr[b]
        )
        r.dng[:, here] = dng.astype(BF16)
        r.stats[me, pl.ds(b, 1)] = squares_row
        r.stats[me, pl.ds(blocks + b, 1)] = jnp.sum(dng * weighted, axis=0, keepdims=True)

    def normed_block(b):
        lanes = lax.broadcasted_iota(jnp.int32, r.scale.shape, 1)
        scaling = jnp.sum(jnp.where(lanes == b, r.scale[...], 0.0), axis=1, keepdims=True)
        no = (r.x_own[...].astype(F32) * scaling * r.gain_own[...]).astype(BF16)
        nsib = (r.x_scr[b].astype(F32) * scaling * r.gain_sib[...]).astype(BF16)
        return no, nsib, lanes

    def backward_step():
        b = block_at
        here = pl.ds(pl.multiple_of(b * q, q), q)
        aux = r.aux[:, here]
        conv = r.conv[...]
        gain = conv[0:inner, 5:6]
        head = r.head[...]
        no, nsib, lanes = normed_block(b)
        arg = conv_args(r, conv, aux, b, q)
        sig_arg = sigmoid(arg)
        act = arg * sig_arg
        r.slope[...] = sig_arg * (1.0 + arg * (1.0 - sig_arg))
        x_all = act[0:inner]
        in_low = act[inner : inner + ns].astype(BF16)
        out_low = act[inner + ns :].astype(BF16)
        step_arg, step, cumul, last, cols = block_rows(None, r.step[:, here], head, aux)
        gate = r.gate[:, here].astype(F32)
        sig = sigmoid(gate)
        silu = gate * sig
        mixed = r.mixed[:, here]
        gated = mixed * silu

        for which in range(len(TURN_AT)):
            progress(which, down_steps)

        @pl.when(step_at == 2 * blocks)
        def _():
            for k in range(group - 1):
                stat_copy(k).wait()

        square_sum, gate_dot = jnp.zeros((1, q), F32), jnp.zeros((1, q), F32)
        for k in range(group):
            square_sum = square_sum + r.stats[k, pl.ds(b, 1)]
            gate_dot = gate_dot + r.stats[k, pl.ds(blocks + b, 1)]
        gate_scale = lax.rsqrt(square_sum / inner_width + EPSILON)
        pull = gate_scale * gate_scale * gate_scale * gate_dot / inner_width
        dng_scaled = r.dng[:, here].astype(F32) * gate_scale
        d_gated = gain * dng_scaled - gated * pull
        r.acc_chan[0] += lane_fold(dng_scaled * gated)
        normed_gate = (gated * (gate_scale * gain)).astype(BF16)
        r.acc_w[out_at:, own_cols] += dot_nn(normed_gate, r.c_own[...])
        r.acc_w[out_at:, sib_cols] += dot_nn(normed_gate, r.c_scr[b])
        grad_mixed = d_gated * silu
        r.low[gate_at:out_at] = (d_gated * mixed * (sig * (1.0 + gate * (1.0 - sig)))).astype(BF16)
        progress(3, down_steps)

        t_at = lax.broadcasted_iota(jnp.int32, (q, q), 0)
        s_at = lax.broadcasted_iota(jnp.int32, (q, q), 1)
        seg_col = cols[:, STEP_ROWS + 3 : STEP_ROWS + 4]
        bias = jnp.where((s_at <= t_at) & (seg_col == aux[3:4]), 0.0, NEG)
        pairs = dot_tn(out_low, in_low)
        reach = aux[4:5] * jnp.exp(cumul)
        tails = aux[5:6] * jnp.exp(last - cumul)
        keep = aux[6:7, 0:1] * jnp.exp(last)
        entering = r.states[b]

        @pl.when(step_at == 2 * blocks)
        def _():
            r.state[...] = jnp.zeros_like(r.state)

        d_next = r.state[...]
        from_next = dot_nn(d_next.astype(BF16), in_low)
        r.acc_chan[1] += lane_fold(grad_mixed * x_all)
        d_pairs_top = jnp.zeros((hq, hq), F32)
        d_pairs_low = jnp.zeros((hq, q), F32)
        reach_parts, tail_parts = [], []
        row_sums, col_sums, x_sums, tail_sums, carry_sums = [], [], [], [], []
        for h in range(nh):
            lo = h * pc
            x_h = x_all[lo : lo + pc]
            u_h = x_h * step[h : h + 1]
            u_low = u_h.astype(BF16)
            g_h = grad_mixed[lo : lo + pc]
            g_low = g_h.astype(BF16)
            col = cols[:, h : h + 1]
            row = cumul[h : h + 1]
            reach_parts.append((g_h * reach[h : h + 1]).astype(BF16))
            tail_parts.append((u_h * tails[h : h + 1]).astype(BF16))
            e_top = jnp.exp((col[:hq] - row[:, :hq]) + bias[:hq, :hq])
            e_low = jnp.exp((col[hq:] - row) + bias[hq:])
            m_top = (e_top * pairs[:hq, :hq]).astype(BF16)
            m_low = (e_low * pairs[hq:]).astype(BF16)
            dm_top = dot_tn(g_low[:, :hq], u_low[:, :hq])
            dm_low = dot_tn(g_low[:, hq:], u_low)
            d_pairs_top = d_pairs_top + dm_top * e_top
            d_pairs_low = d_pairs_low + dm_low * e_low
            du_top = dot_nn(g_low[:, :hq], m_top)
            du_low = dot_nn(g_low[:, hq:], m_low)
            du_local = jnp.concatenate([du_top + du_low[:, :hq], du_low[:, hq:]], axis=1)
            du_next = from_next[lo : lo + pc] * tails[h : h + 1]
            du = du_local + du_next
            skip = head[h : h + 1, 2:3]
            r.work[lo : lo + pc] = du * step[h : h + 1] + skip * g_h
            u_round = u_low.astype(F32)
            y_h = mixed[lo : lo + pc] - skip * x_h
            row_sums.append(jnp.sum(g_low.astype(F32) * y_h, axis=0, keepdims=True))
            next_sum = jnp.sum(u_round * du_next, axis=0, keepdims=True)
            col_sums.append(jnp.sum(u_round * du_local, axis=0, keepdims=True) + next_sum)
            tail_sums.append(next_sum)
            x_sums.append(jnp.sum(x_h * du, axis=0, keepdims=True))
            carry_sums.append(
                jnp.sum(entering[lo : lo + pc] * d_next[lo : lo + pc], axis=0, keepdims=True)
            )
            if h in (nh // 3, 2 * nh // 3):
                progress(3 + h // (nh // 3), down_steps)
        progress(6, down_steps)
        pad_rows = [jnp.zeros((STEP_ROWS - nh, q), F32)]
        row_sum = jnp.concatenate(row_sums + pad_rows, axis=0)
        col_sum = jnp.concatenate(col_sums + pad_rows, axis=0)
        tail_sum = jnp.concatenate(tail_sums + pad_rows, axis=0)
        x_sum = jnp.concatenate(x_sums + pad_rows, axis=0)
        carry = jnp.concatenate(carry_sums + [jnp.zeros((STEP_ROWS - nh, ns), F32)], axis=0)
        d_last = jnp.sum(tail_sum, axis=1, keepdims=True) + keep * jnp.sum(
            carry, axis=1, keepdims=True
        )
        later = (t_at >= s_at).astype(F32)
        d_log = dot_nn(row_sum - col_sum, later, HIGHEST) + d_last
        d_step = x_sum + head[:, 1:2] * d_log
        d_step_arg = d_step * sigmoid(step_arg)
        r.acc_head[0] += lane_fold(d_step_arg)
        r.acc_head[1] += lane_fold(step * d_log)
        r.low[step_row:inner_at] = d_step_arg.astype(BF16)

        g_reach = jnp.concatenate(reach_parts, axis=0)
        u_tail = jnp.concatenate(tail_parts, axis=0)
        d_top_low = d_pairs_top.astype(BF16)
        d_low_low = d_pairs_low.astype(BF16)
        d_out = dot_tn(entering.astype(BF16), g_reach)
        d_out = d_out + jnp.concatenate(
            [dot_nt(in_low[:, :hq], d_top_low), dot_nt(in_low, d_low_low)], axis=1
        )
        d_in = dot_tn(d_next.astype(BF16), u_tail) + dot_nn(out_low[:, hq:], d_low_low)
        d_in_top = dot_nn(out_low[:, :hq], d_top_low)
        d_in = jnp.concatenate([d_in[:, :hq] + d_in_top, d_in[:, hq:]], axis=1)
        d_enter = dot_nt(g_reach, out_low)
        for h in range(nh):
            lo = h * pc
            r.state[lo : lo + pc] = keep[h : h + 1] * d_next[lo : lo + pc] + d_enter[lo : lo + pc]

        err = jnp.concatenate([r.work[...], d_in, d_out], axis=0) * r.slope[...]
        values = r.pre[:, pl.ds(pl.multiple_of(b * q + 128, 128), q)]
        d_pre = conv[:, 3:4] * err
        r.acc_conv[3] += lane_fold(err * values)
        r.acc_conv[4] += lane_fold(err)
        for offset in range(1, 4):
            masked = err * aux[offset - 1 : offset]
            joined = jnp.concatenate([masked, r.after[offset - 1]], axis=1)
            shifted = joined[:, offset : offset + q]
            r.after[offset - 1] = masked[:, :128]
            d_pre = d_pre + conv[:, 3 - offset : 4 - offset] * shifted
            r.acc_conv[3 - offset] += lane_fold(shifted * values)
        r.low[inner_at:gate_at] = d_pre[0:inner].astype(BF16)
        r.low[0:step_row] = d_pre[inner:].astype(BF16)
        progress(7, down_steps)
        low = r.low[...]
        dn_sib = dot_tn(low, weights[0:out_at, sib_cols])
        dn_own = send_parts(
            dn_sib.astype(BF16), lambda: dot_tn(low, weights[0:out_at, own_cols])
        )
        token_dot = jnp.zeros((q, 1), F32)
        for which, (part, seen) in enumerate(((dn_own, no), (dn_sib, nsib))):
            product = part * seen.astype(F32)
            token_dot = token_dot + jnp.sum(product, axis=1, keepdims=True)
            r.acc_norm[which] += jnp.sum(product.reshape(q // 8, 8, half), axis=0)
        r.acc_dot[...] = jnp.where(lanes == b, token_dot, r.acc_dot[...])
        r.acc_w[0:out_at, own_cols] += dot_nn(low, no)
        r.acc_w[0:out_at, sib_cols] += dot_nn(low, nsib)

    def ending():
        lane = 2 * ns
        if gathers:
            weights[0:inner_at] = r.acc_w[0:inner_at].astype(BF16)
            early.start()
        else:
            r.grad_w[...] = r.acc_w[...].astype(BF16)
        for u in range(units):
            chain.stage_first((2 * blocks - 1) * units + u)
        zeros = jnp.zeros((1, 128), F32)
        conv_vec, chan_vec, head_vec = (
            rows_of(ref) for ref in (r.acc_conv, r.acc_chan, r.acc_head)
        )
        norm_vec = [jnp.sum(r.acc_norm[which], axis=0, keepdims=True) for which in range(2)]
        skip = chan_vec[1:2]
        r.group_vec[me] = jnp.concatenate(
            [
                conv_vec[0:5, inner:],
                skip[:, 0:lane],
                jnp.concatenate([skip[:, lane:], head_vec[0:1]], axis=1),
                jnp.concatenate([head_vec[1:2], zeros], axis=1),
                r.acc_dot[...].T[0:blocks],
            ]
            + [vec[:, at : at + lane] for vec in norm_vec for at in range(0, half, lane)]
            + [jnp.zeros((2, lane), F32)],
            axis=0,
        )

        def group_copy(k):
            sems = (r.group_sems.at[0], r.group_sems.at[1])
            return send(r.group_vec.at[me], r.group_vec.at[me], sems, k, **peers[k])

        for k in range(group - 1):
            group_copy(k).start()

        n_pair, n_cross, n_done = (
            plan.left(table) for table in (plan.pair, plan.cross, plan.done)
        )

        def late_cross(m, _):
            chain.stage_cross(m)
            return 0

        lax.fori_loop(n_cross, max(n_cross, n_pair - 1), late_cross, 0)
        n_cross = max(n_cross, n_pair - 1)
        drained = [n_pair]

        def drain(count=None):
            lo = drained[0]
            hi = plan.total + 1 if count is None else min(plan.total, n_pair + count)
            drained[0] = max(lo, hi)

            def one(m, _):
                @pl.when((m - chain.slots >= n_done) & (m < plan.total))
                def _():
                    chain.stage_done(m - chain.slots)

                @pl.when(m < plan.total)
                def _():
                    chain.stage_pair(m)

                @pl.when(m - 1 >= n_cross)
                def _():
                    chain.stage_cross(m - 1)

                return 0

            lax.fori_loop(lo, max(lo, hi), one, 0)

        if gathers:
            middle = (inner_at + rows) // 2
            for at, (lo, hi) in enumerate(((inner_at, middle), (middle, rows))):
                drain(cfg.stops[at])
                weights[lo:hi] = r.acc_w[lo:hi].astype(BF16)
            drain(cfg.stops[2])
            early.middle()
            late.start()
            drain(cfg.stops[3])
            early.end()
            slice_rows = 2 * ns // group
            for k in range(group):
                lo = k * slice_rows
                r.state_send[k] = r.acc_w[lo : lo + slice_rows, mine].astype(BF16)
            r.step_swap[0] = r.acc_w[step_row:inner_at, mine]

            def state_copy(phase, k):
                peer = peers[k]
                sems = (r.state_sems.at[2 * phase], r.state_sems.at[2 * phase + 1])
                to = peer["row"] * cfg.col_count + peer["col"]
                if phase == 0:
                    return send(r.state_send.at[to], r.state_recv.at[me], sems, k, **peer)
                return send(r.state_all.at[me], r.state_all.at[me], sems, k, **peer)

            step_copy = send(
                r.step_swap.at[0],
                r.step_swap.at[1],
                (r.state_sems.at[0], r.state_sems.at[1]),
                group - 1,
                row=1 - row_at,
            )
            for k in range(group - 1):
                state_copy(0, k).start()
            step_copy.start()
            r.state_recv[me] = r.state_send[me]
        drain(cfg.stops[4])

        for k in range(group - 1):
            group_copy(k).wait()
        shared = r.group_vec[0]
        for k in range(1, group):
            shared = shared + r.group_vec[k]
        by_row, by_head = jnp.zeros((3, lane), F32), jnp.zeros((3, lane), F32)
        for k in range(group):
            one = r.group_vec[k]
            same_row, same_col = (k // cfg.col_count) == row_at, (k % cfg.col_count) == col_at
            by_row = by_row + jnp.where(same_row, one[16:19], one[19:22])
            by_head = by_head + jnp.where(same_col, one[5:8], 0.0)
        scale = r.scale[...].T[0:blocks]
        square_sum = r.stats[0, 0:blocks]
        for k in range(1, group):
            square_sum = square_sum + r.stats[k, 0:blocks]
        gate_scale = lax.rsqrt(square_sum / inner_width + EPSILON)
        r.token_out[...] = jnp.concatenate(
            [scale, shared[8:16] * scale * scale / width, gate_scale], axis=0
        )
        norm_sum = jnp.concatenate([by_row[at : at + 1] for at in range(half // lane)], axis=1)
        norm_sum = norm_sum / r.gain_own[...]
        skip_sum = jnp.concatenate([by_head[0:1], by_head[1:2, 0:128]], axis=1)
        r.dp_vec[0] = jnp.concatenate(
            [
                jnp.concatenate([conv_vec[0:5, 0:inner], shared[0:5]], axis=1),
                jnp.concatenate([chan_vec[0:1], by_head[1:2, 128:], by_head[2:3, 0:128]], axis=1),
                jnp.concatenate([skip_sum, norm_sum[:, 0:lane]], axis=1),
                jnp.concatenate([norm_sum[:, lane:], zeros], axis=1),
            ],
            axis=0,
        )

        def dp_copy(k):
            sems = (r.dp_sems.at[0], r.dp_sems.at[1])
            return send(r.dp_vec.at[0], r.dp_vec.at[k], sems, k - 1, **friends[k - 1])

        if not gathers:
            r.vec_out[...] = r.dp_vec[0]
            drain()
        else:
            for k in range(1, 4):
                dp_copy(k).start()
            drain(cfg.stops[5])
            for k in range(group - 1):
                state_copy(0, k).wait()
            summed = r.state_recv[0].astype(F32)
            for k in range(1, group):
                summed = summed + r.state_recv[k].astype(F32)
            r.state_all[me] = summed.astype(BF16)
            for k in range(group - 1):
                state_copy(1, k).start()
            step_copy.wait()
            r.g_step[...] = r.step_swap[0] + r.step_swap[1]
            drain(cfg.stops[6])
            late.middle()
            drain(cfg.stops[7])
            for k in range(1, 4):
                dp_copy(k).wait()
            ordered = [lax.rem(dp_at - k + 4, 4) for k in range(4)]
            total = r.dp_vec[ordered[0]]
            for k in range(1, 4):
                total = total + r.dp_vec[ordered[k]]
            r.vec_out[...] = total
            drain(cfg.stops[8])
            late.end()
            r.g_inner[...] = r.acc_w[inner_at:gate_at, mine]
            r.g_gate[...] = r.acc_w[gate_at:out_at, mine]
            r.g_out[...] = r.acc_w[out_at:, mine]
            drain()
            for k in range(group - 1):
                state_copy(1, k).wait()
            whole_state = [r.state_all[k].astype(F32) for k in range(group)]
            r.g_state[...] = jnp.concatenate(whole_state, axis=0).T
            early.finish()
            late.finish()
        last_done = max(n_done, plan.total - chain.slots)

        def settle(m, _):
            chain.stage_done(m)
            return 0

        lax.fori_loop(last_done, plan.total, settle, 0)
        chain.totals()
        for m in range(plan.total - chain.out_slots, plan.total):
            chain.exchange(m).wait_send()

    @pl.when(scans == 1)
    def _():
        scan_step()

    if gathers:
        for g, at in ((2, FORWARD_AT[0]), (3, FORWARD_AT[1])):

            @pl.when(step_at == at)
            def _(g=g):
                gather.forward(g)

    @pl.when((scans == 0) & ~goes_down)
    def _():
        out_step()

    @pl.when(step_at == 2 * blocks - 1)
    def _():
        for k in range(group - 1):
            stat_copy(k).start()
        gain_swap.wait_send()
        for b in range(blocks):
            swap(0, b).wait_send()
            swap(1, b).wait_send()
        if gathers:
            gather.finish()

    @pl.when(step_at >= 2 * blocks)
    def _():
        backward_step()

    @pl.when(step_at == 3 * blocks - 1)
    def _():
        ending()


def walk(step, blocks):
    def flag(test):
        return test.astype(jnp.int32)

    mixed = blocks - AHEAD
    at = step - AHEAD
    early = flag(at < 0)
    late = flag(at >= 2 * mixed)
    down = flag(step >= 2 * blocks)
    turn = (1 - early) * (1 - late)
    ahead = at + early * AHEAD
    odd = turn * lax.rem(ahead, 2)
    pair = lax.div(ahead, 2)
    block = (
        early * step
        + turn * (pair + odd * AHEAD)
        + late * (1 - down) * (step - blocks)
        + down * (3 * blocks - 1 - step)
    )
    return early + odd, block


def conv_args(r, conv, aux, b, q):
    rows = conv.shape[0]
    joined = r.pre[:, pl.ds(pl.multiple_of(b * q, q), q + 128)]
    arg = conv[:, 4:5] + conv[:, 3:4] * joined[:, 128:]
    for offset in range(1, 4):
        arg = arg + conv[:, 3 - offset : 4 - offset] * (
            aux[offset - 1 : offset] * joined[:, 128 - offset : 128 - offset + q]
        )
    return arg


def finish_kernel(
    nh,
    x_ref,
    c_ref,
    out_total,
    dn_total,
    tokens,
    gain_own,
    vectors,
    decay_log,
    g_inner,
    g_gate,
    g_out,
    g_state,
    g_step,
    output,
    grad_inputs,
    inner_grad,
    gate_grad,
    out_grad,
    state_grad,
    step_grad,
    norm_grad,
    conv_inner,
    bias_inner,
    conv_state,
    bias_state,
    head_grad,
    gate_norm,
):
    at = pl.program_id(0)
    blocks = tokens.shape[0] // 3
    steps = pl.num_programs(0)
    cols = []
    for part in range(blocks // steps):
        b = at * (blocks // steps) + part
        rows = [tokens[pl.ds(k * blocks + b, 1)] for k in range(3)]
        cols.append(columns_of(jnp.concatenate(rows, axis=0)))
    cols = jnp.concatenate(cols, axis=0)
    scale, pull, gate_scale = (cols[:, k : k + 1] for k in range(3))
    plain = x_ref[...].astype(F32)
    output[...] = (plain + gate_scale * out_total[...].astype(F32)).astype(BF16)
    weighted = dn_total[...].astype(F32) * gain_own[...]
    grad_inputs[...] = c_ref[...].astype(F32) + scale * weighted - plain * pull
    inner_grad[...] = g_inner[...]
    gate_grad[...] = g_gate[...]
    out_grad[...] = g_out[...]
    state_grad[...] = g_state[...]

    @pl.when(at == 0)
    def _():
        inner = g_inner.shape[0] * steps
        pc = inner // nh
        lane = vectors.shape[1] - inner
        half = gain_own.shape[1]
        vec = vectors[...]
        step_grad[...] = g_step[0:nh]
        norm_grad[...] = jnp.concatenate([vec[6:7, inner:], vec[7:8, 0 : half - lane]], axis=1)
        conv_state[...] = vec[0:4, inner:]
        bias_state[...] = vec[4:5, inner:]
        skips = []
        for h in range(nh):
            part = vec[:, h * pc : (h + 1) * pc]
            conv_inner[h] = part[0:4]
            bias_inner[h : h + 1] = part[4:5]
            gate_norm[h : h + 1] = part[5:6]
            skips.append(jnp.sum(part[6:7], axis=1, keepdims=True))
        decay = -vec[5:6, inner + 128 : inner + 128 + nh] * jnp.exp(decay_log[...])
        head_grad[0:1] = vec[5:6, inner : inner + nh]
        head_grad[1:2] = decay
        head_grad[2:3] = jnp.concatenate(skips, axis=1)


def per_device(
    inputs,
    segments,
    cotangent,
    norm_gain,
    gate_proj,
    inner_proj,
    state_proj,
    step_proj,
    conv_inner,
    bias_inner,
    conv_state,
    bias_state,
    step_bias,
    decay_log,
    skip_gain,
    gate_norm,
    out_proj,
):
    length, half = inputs.shape
    row_count = lax.axis_size("row")
    col_count = lax.axis_size("col")
    col_at = lax.axis_index("col")
    width = half * row_count
    share, nh, pc = gate_proj.shape
    inner = nh * pc
    state_width = state_proj.shape[1]
    ns = state_width // 2
    conv_rows = inner + state_width
    gate_at = conv_rows + STEP_ROWS
    out_at = gate_at + inner
    rows = out_at + inner
    q = BLOCK_LEN
    blocks = length // q

    def channel_rows(w):
        return jnp.transpose(w, (1, 2, 0)).reshape(inner, share)

    gathers = lax.axis_size("dp") == 4 and share % 128 == 0
    parts = [
        channel_rows(inner_proj),
        state_proj,
        step_proj.T,
        channel_rows(gate_proj),
        channel_rows(out_proj),
    ]
    if not gathers:
        step_rows = jnp.pad(step_proj.T, ((0, STEP_ROWS - nh), (0, 0)))
        parts = [state_proj.T, step_rows, parts[0], parts[3], parts[4]]
        stacked = jnp.concatenate(parts, axis=0).astype(BF16)
        parts = [lax.all_gather(stacked, "dp", axis=1, tiled=True)]
    gain_own = norm_gain[None, :]
    group = row_count * col_count

    units = UNITS
    slots = blocks * units
    cfg = types.SimpleNamespace(
        nh=nh,
        pc=pc,
        ns=ns,
        width=width,
        row_count=row_count,
        col_count=col_count,
        gathers=gathers,
        blocks=blocks,
        units=units,
        early_split=144,
        stops=STOPS,
    )
    plan = Plan(blocks, units, slots, *MODEL)

    def fold(i):
        return walk(i, blocks)[1]

    def whole(*shape):
        return pl.BlockSpec(shape, lambda i: (0,) * len(shape), pipeline_mode=pl.Buffered(1))

    sds, dma, vmem = jax.ShapeDtypeStruct, pltpu.SemaphoreType.DMA, pltpu.VMEM
    anywhere = pl.BlockSpec(memory_space=pl.ANY)
    token_block = pl.BlockSpec((q, half), lambda i: (fold(i), 0))
    ins = {
        "x_own": (inputs, token_block),
        "c_own": (cotangent, token_block),
        "x_any": (inputs, anywhere),
        "c_any": (cotangent, anywhere),
        "gain_own": (gain_own, whole(1, half)),
        "seg": (segments, pl.BlockSpec((1, q), lambda i: (0, fold(i)))),
        "conv_in": (jnp.transpose(conv_inner, (1, 0, 2)), whole(nh, 4, pc)),
        "bias_in": (bias_inner, whole(nh, pc)),
        "gate_gain": (gate_norm, whole(nh, pc)),
        "conv_st": (conv_state, whole(4, state_width)),
        "bias_st": (bias_state[None], whole(1, state_width)),
        "step_bias": (step_bias[None], whole(1, nh)),
        "decay_log": (decay_log[None], whole(1, nh)),
        "skip_gain": (skip_gain[None], whole(1, nh)),
    }
    outs = {
        "out_total": (sds((length, half), BF16), anywhere),
        "dn_total": (sds((length, half), BF16), anywhere),
        "token_out": (sds((3 * blocks, q), F32), whole(3 * blocks, q)),
        "vec_out": (sds((8, conv_rows), F32), whole(8, conv_rows)),
    }
    scratch = {
        "acc_w": vmem((rows, width), F32),
        "x_scr": vmem((blocks, q, half), BF16),
        "c_scr": vmem((blocks, q, half), BF16),
        "gain_sib": vmem((1, half), F32),
        "conv": vmem((conv_rows, 128), F32),
        "head": vmem((STEP_ROWS, 128), F32),
        "prev_seg": vmem((1, 128), F32),
        "pre": vmem((conv_rows, length + 128), F32),
        "step": vmem((STEP_ROWS, length), F32),
        "gate": vmem((inner, length), BF16),
        "mixed": vmem((inner, length), F32),
        "dng": vmem((inner, length), BF16),
        "aux": vmem((8, length), F32),
        "scale": vmem((q, 128), F32),
        "states": vmem((blocks, inner, ns), F32),
        "state": vmem((inner, ns), F32),
        "stats": vmem((group, 2 * blocks, q), F32),
        "work": vmem((inner, q), F32),
        "slope": vmem((conv_rows, q), F32),
        "low": vmem((out_at, q), BF16),
        "after": vmem((3, conv_rows, 128), F32),
        "acc_conv": vmem((5, conv_rows, 128), F32),
        "acc_chan": vmem((2, inner, 128), F32),
        "acc_head": vmem((2, STEP_ROWS, 128), F32),
        "acc_norm": vmem((2, 8, half), F32),
        "acc_dot": vmem((q, 128), F32),
        "group_vec": vmem((group, 24, 2 * ns), F32),
        "dp_vec": vmem((4, 8, conv_rows), F32),
        "ch_own": vmem((2 * units, q // units, half), BF16),
        "ch_sib": vmem((2 * units, q // units, half), BF16),
        "ch_first": vmem((slots, q // units, half), BF16),
        "ch_pair": vmem((slots, q // units, half), BF16),
        "ch_cross": vmem((slots, q // units, half), BF16),
        "cs_send": dma((3, slots)),
        "cs_recv": dma((3, slots)),
        "cs_out": dma((2, plan.total)),
        "cs_keep": dma((slots,)),
        "ch_free": pltpu.SemaphoreType.REGULAR((3,)),
        "swap_sems": dma((4, blocks + 1)),
        "stat_sems": dma((2, group - 1)),
        "group_sems": dma((2, group - 1)),
        "dp_sems": dma((2, 3)),
    }
    if gathers:
        for name, part in zip(("inner_w", "state_w", "step_w", "gate_w", "out_w"), parts):
            ins[name] = (part, whole(*part.shape) if name == "step_w" else anywhere)
        grad_shape = sds((inner, share), F32)
        outs["g_inner"] = (grad_shape, whole(inner, share))
        outs["g_gate"] = (grad_shape, whole(inner, share))
        outs["g_out"] = (grad_shape, whole(inner, share))
        outs["g_state"] = (sds((share, state_width), F32), whole(share, state_width))
        outs["g_step"] = (sds((STEP_ROWS, share), F32), whole(STEP_ROWS, share))
        pieces = (group, state_width // group, share)
        early_rows = state_width + STEP_ROWS
        late_half = (rows - early_rows) // 2
        scratch.update(
            weights=vmem((rows, width), BF16),
            gather_sems=dma((8, 4)),
            raw_sems=dma((4,)),
            ea_top=vmem((2, cfg.early_split, share), BF16),
            ea_low=vmem((2, early_rows - cfg.early_split, share), BF16),
            ea_top_last=vmem((cfg.early_split, share), BF16),
            ea_low_last=vmem((early_rows - cfg.early_split, share), BF16),
            ea_sems=dma((4, 3)),
            rs_top=vmem((2, late_half, share), BF16),
            rs_low=vmem((2, late_half, share), BF16),
            rs_top_last=vmem((late_half, share), BF16),
            rs_low_last=vmem((late_half, share), BF16),
            rs_sems=dma((4, 3)),
            step_swap=vmem((2, STEP_ROWS, share), F32),
            state_send=vmem(pieces, BF16),
            state_recv=vmem(pieces, BF16),
            state_all=vmem(pieces, BF16),
            state_sems=dma((4, group)),
        )
    else:
        ins["weights"] = (parts[0], whole(rows, width))
        outs["grad_w"] = (sds((rows, width), BF16), whole(rows, width))
    names = (*ins, *outs, *scratch)
    results = pl.pallas_call(
        functools.partial(layer_kernel, cfg, plan, names),
        name="layer",
        grid=(3 * blocks,),
        in_specs=[spec for _, spec in ins.values()],
        out_specs=[spec for _, spec in outs.values()],
        out_shape=[shape for shape, _ in outs.values()],
        scratch_shapes=list(scratch.values()),
        compiler_params=pltpu.CompilerParams(
            vmem_limit_bytes=VMEM_LIMIT, collective_id=1, has_side_effects=True
        ),
        cost_estimate=pl.CostEstimate(
            flops=6 * length * width * rows,
            bytes_accessed=60 << 20,
            transcendentals=2 * nh * length * q,
        ),
    )(*(array for array, _ in ins.values()))
    made = types.SimpleNamespace(**dict(zip(outs, results, strict=True)))
    if gathers:
        return finish(nh, blocks, made, inputs, cotangent, gain_own, decay_log[None], ns)
    tokens = made.token_out.reshape(3, length)
    scale, pull, gate_scale = (tokens[k][:, None] for k in range(3))
    plain = inputs.astype(F32)
    output = (plain + gate_scale * made.out_total.astype(F32)).astype(BF16)
    weighted = made.dn_total.astype(F32) * gain_own
    grad_inputs = cotangent.astype(F32) + scale * weighted - plain * pull
    vectors = made.vec_out
    grads = lax.psum_scatter(made.grad_w, "dp", scatter_dimension=1, tiled=True)
    grads = grads.astype(F32)
    vectors = lax.psum(vectors, "dp")
    g_state = lax.psum(grads[0:state_width], ("row", "col")).T
    g_step = lax.psum(grads[state_width : state_width + STEP_ROWS], "row")
    g_inner = grads[state_width + STEP_ROWS : gate_at]
    g_gate = grads[gate_at:out_at]
    g_out = grads[out_at:]

    def feature_rows(w):
        return jnp.transpose(w.reshape(nh, pc, share), (2, 0, 1))

    channel_vecs = vectors[:, 0:inner].reshape(8, nh, pc)
    grad_norm = jnp.concatenate([vectors[6, inner:], vectors[7, : half - 2 * ns]])
    return (
        output,
        grad_inputs,
        grad_norm,
        feature_rows(g_gate),
        feature_rows(g_inner),
        g_state,
        g_step[:nh].T,
        channel_vecs[0:4],
        channel_vecs[4],
        vectors[0:4, inner:],
        vectors[4, inner:],
        vectors[5, inner : inner + nh],
        -vectors[5, inner + 128 : inner + 128 + nh] * jnp.exp(decay_log),
        jnp.sum(channel_vecs[6], axis=1),
        channel_vecs[5],
        feature_rows(g_out),
    )


def finish(nh, blocks, made, inputs, cotangent, gain_own, decay_log, ns):
    length, half = inputs.shape
    inner, share = made.g_inner.shape
    pc = inner // nh
    q = length // blocks
    steps = FINISH_STEPS
    sds = jax.ShapeDtypeStruct

    def whole(*shape):
        return pl.BlockSpec(shape, lambda i: (0,) * len(shape))

    tokens = pl.BlockSpec((length // steps, half), lambda i: (i, 0))
    rows = pl.BlockSpec((inner // steps, share), lambda i: (i, 0))
    state_rows = pl.BlockSpec((share // steps, 2 * ns), lambda i: (i, 0))
    grad = sds((inner, share), F32)
    (
        output,
        grad_inputs,
        g_inner,
        g_gate,
        g_out,
        g_state,
        g_step,
        norm,
        conv_inner,
        bias_inner,
        conv_state,
        bias_state,
        heads,
        gate_norm,
    ) = pl.pallas_call(
        functools.partial(finish_kernel, nh),
        name="finish",
        grid=(steps,),
        in_specs=[
            tokens,
            tokens,
            tokens,
            tokens,
            whole(3 * blocks, q),
            whole(1, half),
            whole(*made.vec_out.shape),
            whole(1, nh),
            rows,
            rows,
            rows,
            state_rows,
            whole(STEP_ROWS, share),
        ],
        out_specs=[
            tokens,
            tokens,
            rows,
            rows,
            rows,
            state_rows,
            whole(nh, share),
            whole(1, half),
            whole(nh, 4, pc),
            whole(nh, pc),
            whole(4, 2 * ns),
            whole(1, 2 * ns),
            whole(3, nh),
            whole(nh, pc),
        ],
        out_shape=[
            sds((length, half), BF16),
            sds((length, half), F32),
            grad,
            grad,
            grad,
            sds((share, 2 * ns), F32),
            sds((nh, share), F32),
            sds((1, half), F32),
            sds((nh, 4, pc), F32),
            sds((nh, pc), F32),
            sds((4, 2 * ns), F32),
            sds((1, 2 * ns), F32),
            sds((3, nh), F32),
            sds((nh, pc), F32),
        ],
        compiler_params=pltpu.CompilerParams(vmem_limit_bytes=VMEM_LIMIT),
    )(
        inputs,
        cotangent,
        made.out_total,
        made.dn_total,
        made.token_out,
        gain_own,
        made.vec_out,
        decay_log,
        made.g_inner,
        made.g_gate,
        made.g_out,
        made.g_state,
        made.g_step,
    )

    def feature_rows(w):
        return jnp.transpose(w.reshape(nh, pc, share), (2, 0, 1))

    return (
        output,
        grad_inputs,
        norm[0],
        feature_rows(g_gate),
        feature_rows(g_inner),
        g_state,
        g_step.T,
        jnp.transpose(conv_inner, (1, 0, 2)),
        bias_inner,
        conv_state,
        bias_state[0],
        heads[0],
        heads[1],
        heads[2],
        gate_norm,
        feature_rows(g_out),
    )


def solution(mesh):
    return jax.shard_map(
        per_device,
        mesh=mesh,
        in_specs=(
            P("dp", "row"),
            P("dp", None),
            P("dp", "row"),
            P("row"),
            P("dp", "col", "row"),
            P("dp", "col", "row"),
            P("dp", None),
            P("dp", "col"),
            P(None, "col", "row"),
            P("col", "row"),
            P(),
            P(),
            P("col"),
            P("col"),
            P("col"),
            P("col", "row"),
            P("dp", "col", "row"),
        ),
        out_specs=(
            P("dp", "row"),
            P("dp", "row"),
            P("row"),
            P("dp", "col", "row"),
            P("dp", "col", "row"),
            P("dp", None),
            P("dp", "col"),
            P(None, "col", "row"),
            P("col", "row"),
            P(),
            P(),
            P("col"),
            P("col"),
            P("col"),
            P("col", "row"),
            P("dp", "col", "row"),
        ),
        check_vma=False,
    )
```

```python
import functools
import types

import jax
import jax.numpy as jnp
from jax import lax
from jax.experimental import pallas as pl
from jax.experimental.pallas import tpu as pltpu
from jax.sharding import PartitionSpec as P

H = 48
P_SIZE = 64
BLOCK_LEN = 256
EPSILON = 1e-05
NEG = -1e30
STEP_ROWS = 16
UNITS = 2
UP_AT = (0.45, None, None, None, None, None, None, 0.8)
DOWN_AT = (None, None, None, 0.22, 0.35, 0.5, 0.65, 0.78)
TURN_AT = (0.3, 0.6, 0.9)
AHEAD = 5
MODEL = (2.4, 3.7, 10.0, 8.2, 8.0, 0.5)
FORWARD_AT = (2, 4)
STOPS = (1, 1, 2, 3, 4, 7, 7, 8, 10)
DEPTH = 2
VMEM_LIMIT = 63 << 20
FINISH_STEPS = 2
F32 = jnp.float32
BF16 = jnp.bfloat16
HIGHEST = lax.Precision.HIGHEST


def dot_nn(left, right, precision=None):
    return lax.dot_general(
        left, right, (((1,), (0,)), ((), ())), preferred_element_type=F32, precision=precision
    )


def dot_nt(left, right, precision=None):
    return lax.dot_general(
        left, right, (((1,), (1,)), ((), ())), preferred_element_type=F32, precision=precision
    )


def dot_tn(left, right):
    return lax.dot_general(left, right, (((0,), (0,)), ((), ())), preferred_element_type=F32)


def sigmoid(values):
    return 0.5 * jnp.tanh(0.5 * values) + 0.5


def softplus(values):
    return jnp.maximum(values, 0.0) + jnp.log1p(jnp.exp(-jnp.abs(values)))


def lane_fold(values):
    total = values[:, :128]
    for at in range(128, values.shape[1], 128):
        total = total + values[:, at : at + 128]
    return total


def columns_of(rows):
    padded = jnp.concatenate([rows, jnp.zeros((128 - rows.shape[0], rows.shape[1]), F32)], axis=0)
    return padded.T


def rows_of(ref):
    lanes = lax.broadcasted_iota(jnp.int32, ref.shape[1:], 1)
    total = jnp.zeros(ref.shape[1:], F32)
    for at in range(ref.shape[0]):
        total = jnp.where(lanes == at, jnp.sum(ref[at], axis=1, keepdims=True), total)
    if total.shape[0] % 128:
        total = jnp.concatenate([total, jnp.zeros((128 - total.shape[0], 128), F32)], axis=0)
    return total.T[0:8]


def pad_lanes(rows):
    return jnp.concatenate([rows, jnp.zeros((rows.shape[0], 128 - rows.shape[1]), F32)], axis=1)


def load_columns(r):
    nh, taps, pc = r.conv_in.shape
    rows = []
    for h in range(nh):
        rows += [r.conv_in[h], r.bias_in[h : h + 1], r.gate_gain[h : h + 1]]
        rows += [jnp.zeros((2, pc), F32)]
    cols = columns_of(pad_lanes(jnp.concatenate(rows, axis=0)))[0:pc]
    for h in range(nh):
        turned = pltpu.roll(cols, 128 - 8 * h, axis=1) if h else cols
        r.conv[h * pc : (h + 1) * pc] = turned
    state_rows = jnp.concatenate([r.conv_st[...], r.bias_st[...]], axis=0)
    r.conv[nh * pc :] = columns_of(state_rows)
    head_rows = jnp.concatenate([r.step_bias[...], r.decay_log[...], r.skip_gain[...]], axis=0)
    heads = columns_of(pad_lanes(head_rows))[0:STEP_ROWS]
    lanes = lax.broadcasted_iota(jnp.int32, heads.shape, 1)
    r.head[...] = jnp.where(lanes == 1, -jnp.exp(heads), heads)


def block_rows(dims, step_pre, hrow, aux):
    q = step_pre.shape[1]
    step_arg = step_pre + hrow[:, 0:1]
    step = softplus(step_arg)
    log_decay = step * hrow[:, 1:2]
    source = lax.broadcasted_iota(jnp.int32, (q, q), 0)
    target = lax.broadcasted_iota(jnp.int32, (q, q), 1)
    upper = (source <= target).astype(F32)
    cumul = dot_nn(log_decay, upper, HIGHEST)
    last = cumul[:, q - 1 : q]
    cols = columns_of(jnp.concatenate([cumul, aux], axis=0))
    return step_arg, step, cumul, last, cols


MESH = pl.DeviceIdType.MESH


def send(src, dst, sems, at, **device):
    return pltpu.make_async_remote_copy(
        src_ref=src,
        dst_ref=dst,
        send_sem=sems[0].at[at],
        recv_sem=sems[1].at[at],
        device_id=device,
        device_id_type=MESH,
    )


def group_peers(row_count, col_count):
    row_at, col_at = lax.axis_index("row"), lax.axis_index("col")
    return [
        dict(row=lax.rem(row_at + j, row_count), col=lax.rem(col_at + k, col_count))
        for k in range(col_count)
        for j in range(row_count)
        if (j, k) != (0, 0)
    ]


def greet(peers):
    barrier = pltpu.get_barrier_semaphore()
    for peer in peers:
        pl.semaphore_signal(barrier, inc=1, device_id=peer, device_id_type=MESH)


def greeted(peers):
    pl.semaphore_wait(pltpu.get_barrier_semaphore(), len(peers))


def add_low(left, right):
    return left + right


class Chain:
    def __init__(self, r, total, turn, first_rows, second_rows):
        self.total, self.turn = total, turn
        self.own, self.sib = r.ch_own, r.ch_sib
        self.first, self.pair, self.cross = r.ch_first, r.ch_pair, r.ch_cross
        self.slots = self.first.shape[0]
        self.out_slots = self.own.shape[0]
        self.sems = [(r.cs_send.at[k], r.cs_recv.at[k]) for k in range(3)]
        self.sems.append((r.cs_out.at[0], r.cs_out.at[1]))
        self.keep_sems = r.cs_keep
        self.free = r.ch_free
        self.first_rows, self.second_rows = first_rows, second_rows
        self.row_at, self.col_at = lax.axis_index("row"), lax.axis_index("col")
        self.is_outer = (self.col_at == 0) | (self.col_at == 3)
        self.inward = 1 + lax.div(self.col_at, 2)
        self.outward = 3 * lax.div(self.col_at, 2)

    def slot(self, m):
        return lax.rem(m, self.slots)

    def out_slot(self, m):
        return lax.rem(m, self.out_slots)

    def exchange(self, m):
        return send(
            self.sib.at[self.out_slot(m)],
            self.first.at[self.slot(m)],
            self.sems[0],
            self.slot(m),
            row=1 - self.row_at,
        )

    def to_inner(self, m):
        at = self.slot(m)
        return send(self.first.at[at], self.pair.at[at], self.sems[1], at, col=self.inward)

    def across(self, m):
        at = self.slot(m)
        return send(self.pair.at[at], self.cross.at[at], self.sems[2], at, col=3 - self.col_at)

    def to_outer(self, m, rows):
        return send(self.cross.at[self.slot(m)], rows, self.sems[3], m, col=self.outward)

    def keep(self, m, rows):
        at = self.slot(m)
        return pltpu.make_async_copy(self.cross.at[at], rows, self.keep_sems.at[at])

    def credit(self, which, m, **device):
        @pl.when(m < self.total - self.slots)
        def _():
            pl.semaphore_signal(
                self.free.at[which], inc=1, device_id=device, device_id_type=MESH
            )

    def spend(self, which, m):
        @pl.when(m >= self.slots)
        def _():
            pl.semaphore_wait(self.free.at[which], 1)

    def begin(self, m, sib_part):
        @pl.when(m >= self.out_slots)
        def _():
            self.exchange(m - self.out_slots).wait_send()

        self.sib[self.out_slot(m)] = sib_part
        self.spend(0, m)
        self.exchange(m).start()

    def put_own(self, m, own_part):
        self.own[self.out_slot(m)] = own_part

    def stage_first(self, m):
        at = self.slot(m)
        self.exchange(m).wait_recv()
        self.first[at] = add_low(self.own[self.out_slot(m)], self.first[at])

        @pl.when(self.is_outer & (m < DEPTH))
        def _():
            self.to_inner(m).start()

    def stage_pair(self, m):
        at = self.slot(m)

        @pl.when(self.is_outer)
        def _():
            self.to_inner(m).wait_send()

            @pl.when(m + DEPTH < self.total)
            def _():
                self.spend(1, m + DEPTH)
                self.to_inner(m + DEPTH).start()

        @pl.when(~self.is_outer)
        def _():
            self.to_inner(m).wait_recv()
            self.pair[at] = add_low(self.first[at], self.pair[at])
            self.spend(2, m)
            self.across(m).start()

        self.credit(0, m, row=1 - self.row_at)

    def stage_cross(self, m):
        at = self.slot(m)

        @pl.when(~self.is_outer)
        def _():
            self.across(m).wait()
            self.cross[at] = add_low(self.pair[at], self.cross[at])
            self.credit(1, m, col=self.outward)

            @pl.when(m < self.turn)
            def _():
                self.keep(m, self.first_rows(m)).start()
                self.to_outer(m, self.first_rows(m)).start()

            @pl.when(m >= self.turn)
            def _():
                self.keep(m, self.second_rows(m)).start()
                self.to_outer(m, self.second_rows(m)).start()

    def stage_done(self, m):
        @pl.when(~self.is_outer)
        def _():
            rows = self.first_rows(0)
            self.keep(m, rows).wait()
            self.to_outer(m, rows).wait_send()
            self.credit(2, m, col=3 - self.col_at)

    def totals(self):
        @pl.when(self.is_outer)
        def _():
            def one(m, _):
                self.to_outer(m, self.first_rows(0)).wait_recv()
                return 0

            lax.fori_loop(0, self.total, one, 0)


class Plan:
    def __init__(self, blocks, units, slots, up_us, scan_us, gap, down_us, hop, lag):
        steps = 2 * blocks
        self.total = steps * units
        self.per_step = len(UP_AT)
        self.points = steps * self.per_step
        hop = hop / units
        mixed = blocks - AHEAD
        lengths = [up_us + scan_us] * mixed + [up_us] * AHEAD + [down_us] * blocks
        starts = [0.0]
        for step in range(1, steps):
            pause = gap if step == blocks else 0.0
            starts.append(starts[-1] + lengths[step - 1] + pause)
        times = []
        for step in range(steps):
            if step < blocks:
                times += [None if at is None else starts[step] + at * up_us for at in UP_AT]
            else:
                times += [
                    None if at is None else starts[step] + at * down_us for at in DOWN_AT
                ]
        for which, at in enumerate(TURN_AT):
            times[self.per_step * blocks + which] = starts[blocks] - gap * (1.0 - at)
        ends = [at + up_us for at in starts[:blocks]]
        ends += [at + down_us for at in starts[blocks:]]

        def point_after(when):
            fits = [p for p, at in enumerate(times) if at is not None and at >= when]
            return fits[0] if fits else self.points

        def exact(point, when):
            known = point < len(times) and times[point] is not None
            return times[point] if known else when

        self.pair, self.cross, self.done = [], [], []
        one = two = three = 0.0
        for m in range(self.total):
            ready = ends[m // units] + 2.0
            if m >= DEPTH:
                ready = max(ready, taken[m - DEPTH])
            else:
                taken = taken if m else []
            one = max(one, ready) + hop
            point = point_after(one + lag)
            if m + DEPTH < self.total:
                point = max(point, self.per_step * ((m + DEPTH) // units + 1))
            if m + slots < self.total:
                point = min(point, self.per_step * ((m + slots) // units + 1) - 1)
            point = min(point, self.points)
            self.pair.append(point)
            taken_at = exact(point, one + lag)
            taken.append(taken_at)
            two = max(two, taken_at) + hop
            point = max(point_after(two + lag), point)
            self.cross.append(point)
            three = max(three, exact(point, two + lag)) + hop
            self.done.append(point_after(three + lag))
        for m in range(self.total - slots):
            self.done[m] = max(min(self.done[m], self.pair[m + slots]), self.cross[m])
        self.end = three + lag

    def span(self, table, which, step, steps):
        first = count = 0
        for point in sorted(set(table)):
            on = point // self.per_step
            if on in steps and point % self.per_step == which:
                hit = (step == on).astype(jnp.int32)
                first = first + table.index(point) * hit
                count = count + table.count(point) * hit
        return first, first + count

    def left(self, table):
        return sum(1 for at in table if at < self.points)


class Gather:
    def __init__(self, whole, sems, groups):
        self.whole, self.groups = whole, groups
        self.sems = sems
        at = lax.axis_index("dp")
        self.at = at
        self.near = at + 1 - 2 * lax.rem(at, 2)
        self.far = lax.rem(at + 2, 4)
        self.share = whole.shape[1] // 4

    def part(self, shard, lo, hi):
        return self.whole.at[
            lo:hi, pl.ds(pl.multiple_of(shard * self.share, 128), self.share)
        ]

    def direct(self, g, to_near):
        lo, _, hi = self.groups[g]
        return send(
            self.part(self.at, lo, hi),
            self.part(self.at, lo, hi),
            self.sems[0 if to_near else 1],
            g,
            dp=self.near if to_near else self.far,
        )

    def onward(self, g, from_near):
        lo, mid, hi = self.groups[g]
        lo, hi = (lo, mid) if from_near else (mid, hi)
        part = self.part(self.near if from_near else self.far, lo, hi)
        return send(
            part,
            part,
            self.sems[2 if from_near else 3],
            g,
            dp=self.far if from_near else self.near,
        )

    def start(self, g):
        self.direct(g, True).start()
        self.direct(g, False).start()

    def forward(self, g):
        for which in (True, False):
            self.direct(g, which).wait_recv()
            self.onward(g, which).start()

    def take(self, g):
        self.onward(g, True).wait_recv()
        self.onward(g, False).wait_recv()

    def finish(self):
        for g in range(len(self.groups)):
            for which in (True, False):
                self.direct(g, which).wait_send()
                self.onward(g, which).wait_send()


class Reduce:
    def __init__(self, acc, stage, bounds, bufs, sems):
        self.acc, self.stage = acc, stage
        self.halves = (bounds[0:2], bounds[1:3])
        self.bufs, self.sems = bufs, sems
        at = lax.axis_index("dp")
        self.at = at
        self.near = at + 1 - 2 * lax.rem(at, 2)
        self.far = lax.rem(at + 2, 4)
        self.share = acc.shape[1] // 4

    def cols(self, shard):
        return pl.ds(pl.multiple_of(shard * self.share, 128), self.share)

    def first(self, half, slot):
        lo, hi = self.halves[half]
        to = (self.near, self.far)[half]
        shard = to if slot == 0 else 3 - self.at
        return send(
            self.stage.at[lo:hi, self.cols(shard)],
            self.bufs[half].at[slot],
            self.sems[half],
            slot,
            dp=to,
        )

    def second(self, half):
        return send(
            self.bufs[half].at[1],
            self.bufs[2 + half],
            self.sems[half],
            2,
            dp=(self.far, self.near)[half],
        )

    def start(self):
        for slot in (1, 0):
            for half in range(2):
                self.first(half, slot).start()

    def middle(self):
        for half in range(2):
            lo, hi = self.halves[half]
            other = (self.far, self.near)[half]
            self.first(half, 1).wait_recv()
            self.bufs[half][1] = (
                self.acc[lo:hi, self.cols(other)] + self.bufs[half][1].astype(F32)
            ).astype(BF16)
            self.second(half).start()

    def end(self):
        for half in range(2):
            lo, hi = self.halves[half]
            self.first(half, 0).wait_recv()
            self.second(half).wait_recv()
            mine = self.cols(self.at)
            self.acc[lo:hi, mine] = (
                self.acc[lo:hi, mine]
                + self.bufs[half][0].astype(F32)
                + self.bufs[2 + half][...].astype(F32)
            )

    def finish(self):
        for half in range(2):
            self.first(half, 0).wait_send()
            self.first(half, 1).wait_send()
            self.second(half).wait_send()


def layer_kernel(cfg, plan, names, *refs):
    r = types.SimpleNamespace(**dict(zip(names, refs, strict=True)))
    nh, pc, ns, width = cfg.nh, cfg.pc, cfg.ns, cfg.width
    gathers, blocks, units = cfg.gathers, cfg.blocks, cfg.units
    inner = nh * pc
    conv_rows = inner + 2 * ns
    step_row = 2 * ns
    inner_at = step_row + STEP_ROWS
    gate_at = inner_at + inner
    out_at = gate_at + inner
    rows = out_at + inner
    q, half = r.x_own.shape
    hq = q // 2
    unit_rows = q // units
    inner_width = H * P_SIZE
    step_at = pl.program_id(0)
    scans, block_at = walk(step_at, blocks)
    goes_down = step_at >= 2 * blocks
    chain_step = jnp.where(goes_down, step_at - blocks, block_at)
    row_at, col_at, dp_at = (lax.axis_index(name) for name in ("row", "col", "dp"))
    own_at = pl.multiple_of(row_at * half, 128)
    sib_at = pl.multiple_of((1 - row_at) * half, 128)
    own_cols, sib_cols = pl.ds(own_at, half), pl.ds(sib_at, half)
    group = cfg.row_count * cfg.col_count
    me = row_at * cfg.col_count + col_at
    peers = group_peers(cfg.row_count, cfg.col_count)
    friends = [dict(dp=lax.rem(dp_at + k, 4)) for k in range(1, 4)] if gathers else []
    weights = r.weights

    def out_rows(m):
        return r.out_total.at[pl.ds(pl.multiple_of(m * unit_rows, unit_rows), unit_rows)]

    def dn_rows(m):
        at = (2 * blocks - 1 - lax.div(m, units)) * q + lax.rem(m, units) * unit_rows
        return r.dn_total.at[pl.ds(pl.multiple_of(at, unit_rows), unit_rows)]

    chain = Chain(r, plan.total, blocks * units, out_rows, dn_rows)

    def send_parts(sib_part, own_part):
        for u in range(units):
            lo = u * unit_rows
            chain.begin(chain_step * units + u, sib_part[lo : lo + unit_rows])
        own = own_part()
        for u in range(units):
            lo = u * unit_rows
            chain.put_own(chain_step * units + u, own[lo : lo + unit_rows].astype(BF16))
        return own

    def progress(which, steps):
        if which == 0:

            @pl.when(chain_step > 0)
            def _():
                for u in range(units):
                    chain.stage_first((chain_step - 1) * units + u)

        for table, stage in (
            (plan.done, chain.stage_done),
            (plan.pair, chain.stage_pair),
            (plan.cross, chain.stage_cross),
        ):

            def one(m, _, stage=stage):
                stage(m)
                return 0

            lo, hi = plan.span(table, which, chain_step, steps)
            if lo is not hi:
                lax.fori_loop(lo, hi, one, 0)

    up_steps, down_steps = range(blocks), range(blocks, 2 * blocks)

    def token_rows(ref, b):
        return ref.at[pl.ds(pl.multiple_of(b * q, q), q)]

    def swap(which, b):
        src, dst = ((r.x_any, r.x_scr), (r.c_any, r.c_scr))[which]
        sems = (r.swap_sems.at[2 * which], r.swap_sems.at[2 * which + 1])
        return send(token_rows(src, b), dst.at[b], sems, b, row=1 - row_at)

    gain_swap = send(
        r.gain_own,
        r.gain_sib,
        (r.swap_sems.at[0], r.swap_sems.at[1]),
        blocks,
        row=1 - row_at,
    )

    def stat_copy(k):
        sems = (r.stat_sems.at[0], r.stat_sems.at[1])
        return send(r.stats.at[me], r.stats.at[me], sems, k, **peers[k])

    if gathers:
        bounds = (
            (0, cfg.early_split, inner_at),
            (inner_at, inner_at + inner // 2, gate_at),
            (gate_at, gate_at + inner // 2, out_at),
            (out_at, out_at + inner // 2, rows),
        )
        sems = [(r.gather_sems.at[2 * k], r.gather_sems.at[2 * k + 1]) for k in range(4)]
        gather = Gather(weights, sems, bounds)
        early = Reduce(
            r.acc_w,
            weights,
            (0, cfg.early_split, inner_at),
            (r.ea_top, r.ea_low, r.ea_top_last, r.ea_low_last),
            [(r.ea_sems.at[2 * k], r.ea_sems.at[2 * k + 1]) for k in range(2)],
        )
        late = Reduce(
            r.acc_w,
            weights,
            (inner_at, (inner_at + rows) // 2, rows),
            (r.rs_top, r.rs_low, r.rs_top_last, r.rs_low_last),
            [(r.rs_sems.at[2 * k], r.rs_sems.at[2 * k + 1]) for k in range(2)],
        )
        share = width // 4
        mine = early.cols(dp_at)
        raw = (
            (r.inner_w, 0, inner, 0, share),
            (r.state_w, 0, share, share, 2 * ns),
            (r.gate_w, inner, inner, 0, share),
            (r.out_w, 2 * inner, inner, 0, share),
        )

        def raw_copy(k):
            src, lo, count, at, size = raw[k]
            return pltpu.make_async_copy(
                src, r.acc_w.at[lo : lo + count, at : at + size], r.raw_sems.at[k]
            )

        def raw_value(k):
            _, lo, count, at, size = raw[k]
            return r.acc_w[lo : lo + count, at : at + size]

    @pl.when(step_at == 0)
    def _():
        greet(peers + friends)
        r.gain_own[...] = r.gain_in[...].reshape(1, half)
        if gathers:
            for k in range(len(raw)):
                raw_copy(k).start()
            for k in range(len(raw)):
                raw_copy(k).wait()
            step_rows = jnp.concatenate(
                [r.step_w[...], jnp.zeros((STEP_ROWS - nh, share), F32)], axis=0
            )
            weights[0:step_row, mine] = raw_value(1).T.astype(BF16)
            weights[step_row:inner_at, mine] = step_rows.astype(BF16)
            weights[inner_at:gate_at, mine] = raw_value(0).astype(BF16)
            weights[gate_at:out_at, mine] = raw_value(2).astype(BF16)
            weights[out_at:, mine] = raw_value(3).astype(BF16)
        greeted(peers + friends)
        if gathers:
            gather.start(0)
            gather.start(1)
        gain_swap.start()
        for b in range(blocks):
            swap(0, b).start()
            swap(1, b).start()
        load_columns(r)
        for ref in (r.acc_w, r.state, r.after, r.acc_conv, r.acc_chan, r.acc_head):
            ref[...] = jnp.zeros_like(ref)
        for ref in (r.acc_norm, r.acc_dot, r.scale):
            ref[...] = jnp.zeros_like(ref)
        r.pre[:, 0:128] = jnp.zeros((conv_rows, 128), F32)
        r.prev_seg[...] = jnp.full_like(r.prev_seg, -1.0)
        gain_swap.wait_recv()
        if gathers:
            gather.forward(0)
            gather.forward(1)
            gather.start(2)
            gather.start(3)
            gather.take(0)
            gather.take(1)

    def scan_step():
        b = block_at
        here = pl.ds(pl.multiple_of(b * q, q), q)
        swap(0, b).wait_recv()
        xo = r.x_own[...].astype(F32)
        xs = r.x_scr[b].astype(F32)
        squares = jnp.sum(xo * xo, axis=1, keepdims=True) + jnp.sum(
            xs * xs, axis=1, keepdims=True
        )
        scaling = lax.rsqrt(squares / width + EPSILON)
        lanes = lax.broadcasted_iota(jnp.int32, r.scale.shape, 1)
        r.scale[...] = jnp.where(lanes == b, scaling, r.scale[...])
        no = (xo * scaling * r.gain_own[...]).astype(BF16)
        nsib = (xs * scaling * r.gain_sib[...]).astype(BF16)
        pre = dot_nt(weights[0:gate_at, own_cols], no) + dot_nt(weights[0:gate_at, sib_cols], nsib)
        values = jnp.concatenate([pre[inner_at:gate_at], pre[0:step_row]], axis=0)
        step_pre = pre[step_row:inner_at]
        r.pre[:, pl.ds(pl.multiple_of(b * q + 128, 128), q)] = values
        r.step[:, here] = step_pre
        seg = r.seg[...].astype(F32)
        seg_before = r.prev_seg[...]
        seg_joined = jnp.concatenate([seg_before, seg], axis=1)
        before, final = seg_before[:, 127:128], seg[:, q - 1 : q]
        aux = jnp.concatenate(
            [
                (seg_joined[:, 128 - offset : 128 - offset + q] == seg).astype(F32)
                for offset in range(1, 4)
            ]
            + [
                seg,
                (seg == before).astype(F32),
                (seg == final).astype(F32),
                jnp.broadcast_to((before == final).astype(F32), (1, q)),
                jnp.zeros((1, q), F32),
            ],
            axis=0,
        )
        r.prev_seg[...] = seg[:, q - 128 :]
        r.aux[:, here] = aux
        conv = r.conv[...]
        head = r.head[...]
        arg = conv_args(r, conv, aux, b, q)
        act = arg * sigmoid(arg)
        r.work[...] = act[0:inner]
        in_low = act[inner : inner + ns].astype(BF16)
        out_low = act[inner + ns :].astype(BF16)

        _, step, cumul, last, cols = block_rows(None, step_pre, head, aux)
        source = lax.broadcasted_iota(jnp.int32, (q, q), 0)
        target = lax.broadcasted_iota(jnp.int32, (q, q), 1)
        seg_col = cols[:, STEP_ROWS + 3 : STEP_ROWS + 4]
        bias = jnp.where((source <= target) & (seg_col == aux[3:4]), 0.0, NEG)
        pairs = dot_tn(in_low, out_low)
        entering = r.state[...]
        r.states[b] = entering
        from_state = dot_nn(entering.astype(BF16), out_low)
        reach = aux[4:5] * jnp.exp(cumul)
        tails = aux[5:6] * jnp.exp(last - cumul)
        keep = aux[6:7, 0:1] * jnp.exp(last)
        tail_parts = []
        for h in range(nh):
            lo = h * pc
            x_h = r.work[lo : lo + pc]
            u_h = (x_h * step[h : h + 1]).astype(BF16)
            tail_parts.append((x_h * (step[h : h + 1] * tails[h : h + 1])).astype(BF16))
            col = cols[:, h : h + 1]
            row = cumul[h : h + 1]
            top = (jnp.exp((row - col[:hq]) + bias[:hq]) * pairs[:hq]).astype(BF16)
            low = jnp.exp((row[:, hq:] - col[hq:]) + bias[hq:, hq:]) * pairs[hq:, hq:]
            y_top = dot_nn(u_h[:, :hq], top)
            y_low = dot_nn(u_h[:, hq:], low.astype(BF16))
            y_h = jnp.concatenate([y_top[:, :hq], y_top[:, hq:] + y_low], axis=1)
            y_h = y_h + from_state[lo : lo + pc] * reach[h : h + 1]
            r.mixed[lo : lo + pc, here] = y_h + head[h : h + 1, 2:3] * x_h
        contrib = dot_nt(jnp.concatenate(tail_parts, axis=0), in_low)
        for h in range(nh):
            lo = h * pc
            r.state[lo : lo + pc] = keep[h : h + 1] * entering[lo : lo + pc] + contrib[lo : lo + pc]

    def out_step():
        b = block_at
        here = pl.ds(pl.multiple_of(b * q, q), q)
        gain = r.conv[0:inner, 5:6]
        if gathers:

            @pl.when(step_at == AHEAD)
            def _():
                gather.take(2)

        no, nsib, _ = normed_block(b)
        gate = dot_nt(weights[gate_at:out_at, own_cols], no) + dot_nt(
            weights[gate_at:out_at, sib_cols], nsib
        )
        r.gate[:, here] = gate.astype(BF16)
        progress(0, up_steps)
        gated = r.mixed[:, here] * (gate * sigmoid(gate))
        squares_row = jnp.sum(gated * gated, axis=0, keepdims=True)
        weighted = gated * gain
        low = weighted.astype(BF16)
        if gathers:

            @pl.when(step_at == AHEAD)
            def _():
                gather.take(3)

        send_parts(
            dot_tn(low, weights[out_at:, sib_cols]).astype(BF16),
            lambda: dot_tn(low, weights[out_at:, own_cols]),
        )
        progress(7, up_steps)
        swap(1, b).wait_recv()
        dng = dot_nt(weights[out_at:, own_cols], r.c_own[...]) + dot_nt(
            weights[out_at:, sib_cols], r.c_scr[b]
        )
        r.dng[:, here] = dng.astype(BF16)
        r.stats[me, pl.ds(b, 1)] = squares_row
        r.stats[me, pl.ds(blocks + b, 1)] = jnp.sum(dng * weighted, axis=0, keepdims=True)

    def normed_block(b):
        lanes = lax.broadcasted_iota(jnp.int32, r.scale.shape, 1)
        scaling = jnp.sum(jnp.where(lanes == b, r.scale[...], 0.0), axis=1, keepdims=True)
        no = (r.x_own[...].astype(F32) * scaling * r.gain_own[...]).astype(BF16)
        nsib = (r.x_scr[b].astype(F32) * scaling * r.gain_sib[...]).astype(BF16)
        return no, nsib, lanes

    def backward_step():
        b = block_at
        here = pl.ds(pl.multiple_of(b * q, q), q)
        aux = r.aux[:, here]
        conv = r.conv[...]
        gain = conv[0:inner, 5:6]
        head = r.head[...]
        no, nsib, lanes = normed_block(b)
        arg = conv_args(r, conv, aux, b, q)
        sig_arg = sigmoid(arg)
        act = arg * sig_arg
        r.slope[...] = sig_arg * (1.0 + arg * (1.0 - sig_arg))
        x_all = act[0:inner]
        in_low = act[inner : inner + ns].astype(BF16)
        out_low = act[inner + ns :].astype(BF16)
        step_arg, step, cumul, last, cols = block_rows(None, r.step[:, here], head, aux)
        gate = r.gate[:, here].astype(F32)
        sig = sigmoid(gate)
        silu = gate * sig
        mixed = r.mixed[:, here]
        gated = mixed * silu

        for which in range(len(TURN_AT)):
            progress(which, down_steps)

        @pl.when(step_at == 2 * blocks)
        def _():
            for k in range(group - 1):
                stat_copy(k).wait()

        square_sum, gate_dot = jnp.zeros((1, q), F32), jnp.zeros((1, q), F32)
        for k in range(group):
            square_sum = square_sum + r.stats[k, pl.ds(b, 1)]
            gate_dot = gate_dot + r.stats[k, pl.ds(blocks + b, 1)]
        gate_scale = lax.rsqrt(square_sum / inner_width + EPSILON)
        pull = gate_scale * gate_scale * gate_scale * gate_dot / inner_width
        dng_scaled = r.dng[:, here].astype(F32) * gate_scale
        d_gated = gain * dng_scaled - gated * pull
        r.acc_chan[0] += lane_fold(dng_scaled * gated)
        normed_gate = (gated * (gate_scale * gain)).astype(BF16)
        r.acc_w[out_at:, own_cols] += dot_nn(normed_gate, r.c_own[...])
        r.acc_w[out_at:, sib_cols] += dot_nn(normed_gate, r.c_scr[b])
        grad_mixed = d_gated * silu
        r.low[gate_at:out_at] = (d_gated * mixed * (sig * (1.0 + gate * (1.0 - sig)))).astype(BF16)
        progress(3, down_steps)

        t_at = lax.broadcasted_iota(jnp.int32, (q, q), 0)
        s_at = lax.broadcasted_iota(jnp.int32, (q, q), 1)
        seg_col = cols[:, STEP_ROWS + 3 : STEP_ROWS + 4]
        bias = jnp.where((s_at <= t_at) & (seg_col == aux[3:4]), 0.0, NEG)
        pairs = dot_tn(out_low, in_low)
        reach = aux[4:5] * jnp.exp(cumul)
        tails = aux[5:6] * jnp.exp(last - cumul)
        keep = aux[6:7, 0:1] * jnp.exp(last)
        entering = r.states[b]

        @pl.when(step_at == 2 * blocks)
        def _():
            r.state[...] = jnp.zeros_like(r.state)

        d_next = r.state[...]
        from_next = dot_nn(d_next.astype(BF16), in_low)
        r.acc_chan[1] += lane_fold(grad_mixed * x_all)
        d_pairs_top = jnp.zeros((hq, hq), F32)
        d_pairs_low = jnp.zeros((hq, q), F32)
        reach_parts, tail_parts = [], []
        row_sums, col_sums, x_sums, tail_sums, carry_sums = [], [], [], [], []
        for h in range(nh):
            lo = h * pc
            x_h = x_all[lo : lo + pc]
            u_h = x_h * step[h : h + 1]
            u_low = u_h.astype(BF16)
            g_h = grad_mixed[lo : lo + pc]
            g_low = g_h.astype(BF16)
            col = cols[:, h : h + 1]
            row = cumul[h : h + 1]
            reach_parts.append((g_h * reach[h : h + 1]).astype(BF16))
            tail_parts.append((u_h * tails[h : h + 1]).astype(BF16))
            e_top = jnp.exp((col[:hq] - row[:, :hq]) + bias[:hq, :hq])
            e_low = jnp.exp((col[hq:] - row) + bias[hq:])
            m_top = (e_top * pairs[:hq, :hq]).astype(BF16)
            m_low = (e_low * pairs[hq:]).astype(BF16)
            dm_top = dot_tn(g_low[:, :hq], u_low[:, :hq])
            dm_low = dot_tn(g_low[:, hq:], u_low)
            d_pairs_top = d_pairs_top + dm_top * e_top
            d_pairs_low = d_pairs_low + dm_low * e_low
            du_top = dot_nn(g_low[:, :hq], m_top)
            du_low = dot_nn(g_low[:, hq:], m_low)
            du_local = jnp.concatenate([du_top + du_low[:, :hq], du_low[:, hq:]], axis=1)
            du_next = from_next[lo : lo + pc] * tails[h : h + 1]
            du = du_local + du_next
            skip = head[h : h + 1, 2:3]
            r.work[lo : lo + pc] = du * step[h : h + 1] + skip * g_h
            u_round = u_low.astype(F32)
            y_h = mixed[lo : lo + pc] - skip * x_h
            row_sums.append(jnp.sum(g_low.astype(F32) * y_h, axis=0, keepdims=True))
            next_sum = jnp.sum(u_round * du_next, axis=0, keepdims=True)
            col_sums.append(jnp.sum(u_round * du_local, axis=0, keepdims=True) + next_sum)
            tail_sums.append(next_sum)
            x_sums.append(jnp.sum(x_h * du, axis=0, keepdims=True))
            carry_sums.append(
                jnp.sum(entering[lo : lo + pc] * d_next[lo : lo + pc], axis=0, keepdims=True)
            )
            if h in (nh // 3, 2 * nh // 3):
                progress(3 + h // (nh // 3), down_steps)
        progress(6, down_steps)
        pad_rows = [jnp.zeros((STEP_ROWS - nh, q), F32)]
        row_sum = jnp.concatenate(row_sums + pad_rows, axis=0)
        col_sum = jnp.concatenate(col_sums + pad_rows, axis=0)
        tail_sum = jnp.concatenate(tail_sums + pad_rows, axis=0)
        x_sum = jnp.concatenate(x_sums + pad_rows, axis=0)
        carry = jnp.concatenate(carry_sums + [jnp.zeros((STEP_ROWS - nh, ns), F32)], axis=0)
        d_last = jnp.sum(tail_sum, axis=1, keepdims=True) + keep * jnp.sum(
            carry, axis=1, keepdims=True
        )
        later = (t_at >= s_at).astype(F32)
        d_log = dot_nn(row_sum - col_sum, later, HIGHEST) + d_last
        d_step = x_sum + head[:, 1:2] * d_log
        d_step_arg = d_step * sigmoid(step_arg)
        r.acc_head[0] += lane_fold(d_step_arg)
        r.acc_head[1] += lane_fold(step * d_log)
        r.low[step_row:inner_at] = d_step_arg.astype(BF16)

        g_reach = jnp.concatenate(reach_parts, axis=0)
        u_tail = jnp.concatenate(tail_parts, axis=0)
        d_top_low = d_pairs_top.astype(BF16)
        d_low_low = d_pairs_low.astype(BF16)
        d_out = dot_tn(entering.astype(BF16), g_reach)
        d_out = d_out + jnp.concatenate(
            [dot_nt(in_low[:, :hq], d_top_low), dot_nt(in_low, d_low_low)], axis=1
        )
        d_in = dot_tn(d_next.astype(BF16), u_tail) + dot_nn(out_low[:, hq:], d_low_low)
        d_in_top = dot_nn(out_low[:, :hq], d_top_low)
        d_in = jnp.concatenate([d_in[:, :hq] + d_in_top, d_in[:, hq:]], axis=1)
        d_enter = dot_nt(g_reach, out_low)
        for h in range(nh):
            lo = h * pc
            r.state[lo : lo + pc] = keep[h : h + 1] * d_next[lo : lo + pc] + d_enter[lo : lo + pc]

        err = jnp.concatenate([r.work[...], d_in, d_out], axis=0) * r.slope[...]
        values = r.pre[:, pl.ds(pl.multiple_of(b * q + 128, 128), q)]
        d_pre = conv[:, 3:4] * err
        r.acc_conv[3] += lane_fold(err * values)
        r.acc_conv[4] += lane_fold(err)
        for offset in range(1, 4):
            masked = err * aux[offset - 1 : offset]
            joined = jnp.concatenate([masked, r.after[offset - 1]], axis=1)
            shifted = joined[:, offset : offset + q]
            r.after[offset - 1] = masked[:, :128]
            d_pre = d_pre + conv[:, 3 - offset : 4 - offset] * shifted
            r.acc_conv[3 - offset] += lane_fold(shifted * values)
        r.low[inner_at:gate_at] = d_pre[0:inner].astype(BF16)
        r.low[0:step_row] = d_pre[inner:].astype(BF16)
        progress(7, down_steps)
        low = r.low[...]
        dn_sib = dot_tn(low, weights[0:out_at, sib_cols])
        dn_own = send_parts(
            dn_sib.astype(BF16), lambda: dot_tn(low, weights[0:out_at, own_cols])
        )
        token_dot = jnp.zeros((q, 1), F32)
        for which, (part, seen) in enumerate(((dn_own, no), (dn_sib, nsib))):
            product = part * seen.astype(F32)
            token_dot = token_dot + jnp.sum(product, axis=1, keepdims=True)
            r.acc_norm[which] += jnp.sum(product.reshape(q // 8, 8, half), axis=0)
        r.acc_dot[...] = jnp.where(lanes == b, token_dot, r.acc_dot[...])
        r.acc_w[0:out_at, own_cols] += dot_nn(low, no)
        r.acc_w[0:out_at, sib_cols] += dot_nn(low, nsib)

    def ending():
        lane = 2 * ns
        if gathers:
            weights[0:inner_at] = r.acc_w[0:inner_at].astype(BF16)
            early.start()
        else:
            r.grad_w[...] = r.acc_w[...].astype(BF16)
        for u in range(units):
            chain.stage_first((2 * blocks - 1) * units + u)
        zeros = jnp.zeros((1, 128), F32)
        conv_vec, chan_vec, head_vec = (
            rows_of(ref) for ref in (r.acc_conv, r.acc_chan, r.acc_head)
        )
        norm_vec = [jnp.sum(r.acc_norm[which], axis=0, keepdims=True) for which in range(2)]
        skip = chan_vec[1:2]
        r.group_vec[me] = jnp.concatenate(
            [
                conv_vec[0:5, inner:],
                skip[:, 0:lane],
                jnp.concatenate([skip[:, lane:], head_vec[0:1]], axis=1),
                jnp.concatenate([head_vec[1:2], zeros], axis=1),
                r.acc_dot[...].T[0:blocks],
            ]
            + [vec[:, at : at + lane] for vec in norm_vec for at in range(0, half, lane)]
            + [jnp.zeros((2, lane), F32)],
            axis=0,
        )

        def group_copy(k):
            sems = (r.group_sems.at[0], r.group_sems.at[1])
            return send(r.group_vec.at[me], r.group_vec.at[me], sems, k, **peers[k])

        for k in range(group - 1):
            group_copy(k).start()

        n_pair, n_cross, n_done = (
            plan.left(table) for table in (plan.pair, plan.cross, plan.done)
        )

        def late_cross(m, _):
            chain.stage_cross(m)
            return 0

        lax.fori_loop(n_cross, max(n_cross, n_pair - 1), late_cross, 0)
        n_cross = max(n_cross, n_pair - 1)
        drained = [n_pair]

        def drain(count=None):
            lo = drained[0]
            hi = plan.total + 1 if count is None else min(plan.total, n_pair + count)
            drained[0] = max(lo, hi)

            def one(m, _):
                @pl.when((m - chain.slots >= n_done) & (m < plan.total))
                def _():
                    chain.stage_done(m - chain.slots)

                @pl.when(m < plan.total)
                def _():
                    chain.stage_pair(m)

                @pl.when(m - 1 >= n_cross)
                def _():
                    chain.stage_cross(m - 1)

                return 0

            lax.fori_loop(lo, max(lo, hi), one, 0)

        if gathers:
            middle = (inner_at + rows) // 2
            for at, (lo, hi) in enumerate(((inner_at, middle), (middle, rows))):
                drain(cfg.stops[at])
                weights[lo:hi] = r.acc_w[lo:hi].astype(BF16)
            drain(cfg.stops[2])
            early.middle()
            late.start()
            drain(cfg.stops[3])
            early.end()
            slice_rows = 2 * ns // group
            for k in range(group):
                lo = k * slice_rows
                r.state_send[k] = r.acc_w[lo : lo + slice_rows, mine].astype(BF16)
            r.step_swap[0] = r.acc_w[step_row:inner_at, mine]

            def state_copy(phase, k):
                peer = peers[k]
                sems = (r.state_sems.at[2 * phase], r.state_sems.at[2 * phase + 1])
                to = peer["row"] * cfg.col_count + peer["col"]
                if phase == 0:
                    return send(r.state_send.at[to], r.state_recv.at[me], sems, k, **peer)
                return send(r.state_all.at[me], r.state_all.at[me], sems, k, **peer)

            step_copy = send(
                r.step_swap.at[0],
                r.step_swap.at[1],
                (r.state_sems.at[0], r.state_sems.at[1]),
                group - 1,
                row=1 - row_at,
            )
            for k in range(group - 1):
                state_copy(0, k).start()
            step_copy.start()
            r.state_recv[me] = r.state_send[me]
        drain(cfg.stops[4])

        for k in range(group - 1):
            group_copy(k).wait()
        shared = r.group_vec[0]
        for k in range(1, group):
            shared = shared + r.group_vec[k]
        by_row, by_head = jnp.zeros((3, lane), F32), jnp.zeros((3, lane), F32)
        for k in range(group):
            one = r.group_vec[k]
            same_row, same_col = (k // cfg.col_count) == row_at, (k % cfg.col_count) == col_at
            by_row = by_row + jnp.where(same_row, one[16:19], one[19:22])
            by_head = by_head + jnp.where(same_col, one[5:8], 0.0)
        scale = r.scale[...].T[0:blocks]
        square_sum = r.stats[0, 0:blocks]
        for k in range(1, group):
            square_sum = square_sum + r.stats[k, 0:blocks]
        gate_scale = lax.rsqrt(square_sum / inner_width + EPSILON)
        r.token_out[...] = jnp.concatenate(
            [scale, shared[8:16] * scale * scale / width, gate_scale], axis=0
        )
        norm_sum = jnp.concatenate([by_row[at : at + 1] for at in range(half // lane)], axis=1)
        norm_sum = norm_sum / r.gain_own[...]
        skip_sum = jnp.concatenate([by_head[0:1], by_head[1:2, 0:128]], axis=1)
        r.dp_vec[0] = jnp.concatenate(
            [
                jnp.concatenate([conv_vec[0:5, 0:inner], shared[0:5]], axis=1),
                jnp.concatenate([chan_vec[0:1], by_head[1:2, 128:], by_head[2:3, 0:128]], axis=1),
                jnp.concatenate([skip_sum, norm_sum[:, 0:lane]], axis=1),
                jnp.concatenate([norm_sum[:, lane:], zeros], axis=1),
            ],
            axis=0,
        )

        def dp_copy(k):
            sems = (r.dp_sems.at[0], r.dp_sems.at[1])
            return send(r.dp_vec.at[0], r.dp_vec.at[k], sems, k - 1, **friends[k - 1])

        if not gathers:
            r.vec_out[...] = r.dp_vec[0]
            drain()
        else:
            for k in range(1, 4):
                dp_copy(k).start()
            drain(cfg.stops[5])
            for k in range(group - 1):
                state_copy(0, k).wait()
            summed = r.state_recv[0].astype(F32)
            for k in range(1, group):
                summed = summed + r.state_recv[k].astype(F32)
            r.state_all[me] = summed.astype(BF16)
            for k in range(group - 1):
                state_copy(1, k).start()
            step_copy.wait()
            r.g_step[...] = r.step_swap[0] + r.step_swap[1]
            drain(cfg.stops[6])
            late.middle()
            drain(cfg.stops[7])
            for k in range(1, 4):
                dp_copy(k).wait()
            ordered = [lax.rem(dp_at - k + 4, 4) for k in range(4)]
            total = r.dp_vec[ordered[0]]
            for k in range(1, 4):
                total = total + r.dp_vec[ordered[k]]
            r.vec_out[...] = total
            drain(cfg.stops[8])
            late.end()
            r.g_inner[...] = r.acc_w[inner_at:gate_at, mine]
            r.g_gate[...] = r.acc_w[gate_at:out_at, mine]
            r.g_out[...] = r.acc_w[out_at:, mine]
            drain()
            for k in range(group - 1):
                state_copy(1, k).wait()
            whole_state = [r.state_all[k].astype(F32) for k in range(group)]
            r.g_state[...] = jnp.concatenate(whole_state, axis=0).T
            early.finish()
            late.finish()
        last_done = max(n_done, plan.total - chain.slots)

        def settle(m, _):
            chain.stage_done(m)
            return 0

        lax.fori_loop(last_done, plan.total, settle, 0)
        chain.totals()
        for m in range(plan.total - chain.out_slots, plan.total):
            chain.exchange(m).wait_send()

    @pl.when(scans == 1)
    def _():
        scan_step()

    if gathers:
        for g, at in ((2, FORWARD_AT[0]), (3, FORWARD_AT[1])):

            @pl.when(step_at == at)
            def _(g=g):
                gather.forward(g)

    @pl.when((scans == 0) & ~goes_down)
    def _():
        out_step()

    @pl.when(step_at == 2 * blocks - 1)
    def _():
        for k in range(group - 1):
            stat_copy(k).start()
        gain_swap.wait_send()
        for b in range(blocks):
            swap(0, b).wait_send()
            swap(1, b).wait_send()
        if gathers:
            gather.finish()

    @pl.when(step_at >= 2 * blocks)
    def _():
        backward_step()

    @pl.when(step_at == 3 * blocks - 1)
    def _():
        ending()


def walk(step, blocks):
    def flag(test):
        return test.astype(jnp.int32)

    mixed = blocks - AHEAD
    at = step - AHEAD
    early = flag(at < 0)
    late = flag(at >= 2 * mixed)
    down = flag(step >= 2 * blocks)
    turn = (1 - early) * (1 - late)
    ahead = at + early * AHEAD
    odd = turn * lax.rem(ahead, 2)
    pair = lax.div(ahead, 2)
    block = (
        early * step
        + turn * (pair + odd * AHEAD)
        + late * (1 - down) * (step - blocks)
        + down * (3 * blocks - 1 - step)
    )
    return early + odd, block


def conv_args(r, conv, aux, b, q):
    rows = conv.shape[0]
    joined = r.pre[:, pl.ds(pl.multiple_of(b * q, q), q + 128)]
    arg = conv[:, 4:5] + conv[:, 3:4] * joined[:, 128:]
    for offset in range(1, 4):
        arg = arg + conv[:, 3 - offset : 4 - offset] * (
            aux[offset - 1 : offset] * joined[:, 128 - offset : 128 - offset + q]
        )
    return arg


def finish_kernel(
    nh,
    x_ref,
    c_ref,
    out_total,
    dn_total,
    tokens,
    gain_own,
    vectors,
    decay_log,
    g_inner,
    g_gate,
    g_out,
    g_state,
    g_step,
    output,
    grad_inputs,
    inner_grad,
    gate_grad,
    out_grad,
    state_grad,
    step_grad,
    norm_grad,
    conv_inner,
    bias_inner,
    conv_state,
    bias_state,
    step_bias,
    decay_grad,
    skip_grad,
    gate_norm,
):
    at = pl.program_id(0)
    blocks = tokens.shape[0] // 3
    steps = pl.num_programs(0)
    cols = []
    for part in range(blocks // steps):
        b = at * (blocks // steps) + part
        rows = [tokens[pl.ds(k * blocks + b, 1)] for k in range(3)]
        cols.append(columns_of(jnp.concatenate(rows, axis=0)))
    cols = jnp.concatenate(cols, axis=0)
    scale, pull, gate_scale = (cols[:, k : k + 1] for k in range(3))
    plain = x_ref[...].astype(F32)
    output[...] = (plain + gate_scale * out_total[...].astype(F32)).astype(BF16)
    weighted = dn_total[...].astype(F32) * gain_own[...].reshape(1, -1)
    grad_inputs[...] = c_ref[...].astype(F32) + scale * weighted - plain * pull
    inner_grad[...] = g_inner[...]
    gate_grad[...] = g_gate[...]
    out_grad[...] = g_out[...]
    state_grad[...] = g_state[...]

    @pl.when(at == 0)
    def _():
        inner = g_inner.shape[0] * steps
        pc = inner // nh
        lane = vectors.shape[1] - inner
        half = gain_own.shape[0]
        vec = vectors[...]
        step_grad[...] = g_step[0:nh]
        norm_grad[...] = jnp.concatenate([vec[6:7, inner:], vec[7:8, 0 : half - lane]], axis=1)[0]
        conv_state[...] = vec[0:4, inner:]
        bias_state[...] = vec[4, inner:]
        skips = []
        for h in range(nh):
            part = vec[:, h * pc : (h + 1) * pc]
            conv_inner[h] = part[0:4]
            bias_inner[h : h + 1] = part[4:5]
            gate_norm[h : h + 1] = part[5:6]
            skips.append(jnp.sum(part[6:7], axis=1, keepdims=True))
        decay = -vec[5:6, inner + 128 : inner + 128 + nh] * jnp.exp(decay_log[...])
        step_bias[...] = vec[5, inner : inner + nh]
        decay_grad[...] = decay[0]
        skip_grad[...] = jnp.concatenate(skips, axis=1)[0]


def per_device(
    inputs,
    segments,
    cotangent,
    norm_gain,
    gate_proj,
    inner_proj,
    state_proj,
    step_proj,
    conv_inner,
    bias_inner,
    conv_state,
    bias_state,
    step_bias,
    decay_log,
    skip_gain,
    gate_norm,
    out_proj,
):
    length, half = inputs.shape
    row_count = lax.axis_size("row")
    col_count = lax.axis_size("col")
    col_at = lax.axis_index("col")
    width = half * row_count
    share, nh, pc = gate_proj.shape
    inner = nh * pc
    state_width = state_proj.shape[1]
    ns = state_width // 2
    conv_rows = inner + state_width
    gate_at = conv_rows + STEP_ROWS
    out_at = gate_at + inner
    rows = out_at + inner
    q = BLOCK_LEN
    blocks = length // q

    def channel_rows(w):
        return jnp.transpose(w, (1, 2, 0)).reshape(inner, share)

    gathers = lax.axis_size("dp") == 4 and share % 128 == 0
    parts = [
        channel_rows(inner_proj),
        state_proj,
        step_proj.T,
        channel_rows(gate_proj),
        channel_rows(out_proj),
    ]
    if not gathers:
        step_rows = jnp.pad(step_proj.T, ((0, STEP_ROWS - nh), (0, 0)))
        parts = [state_proj.T, step_rows, parts[0], parts[3], parts[4]]
        stacked = jnp.concatenate(parts, axis=0).astype(BF16)
        parts = [lax.all_gather(stacked, "dp", axis=1, tiled=True)]
    gain_own = norm_gain[None, :]
    group = row_count * col_count

    units = UNITS
    slots = blocks * units
    cfg = types.SimpleNamespace(
        nh=nh,
        pc=pc,
        ns=ns,
        width=width,
        row_count=row_count,
        col_count=col_count,
        gathers=gathers,
        blocks=blocks,
        units=units,
        early_split=144,
        stops=STOPS,
    )
    plan = Plan(blocks, units, slots, *MODEL)

    def fold(i):
        return walk(i, blocks)[1]

    def whole(*shape):
        return pl.BlockSpec(shape, lambda i: (0,) * len(shape), pipeline_mode=pl.Buffered(1))

    sds, dma, vmem = jax.ShapeDtypeStruct, pltpu.SemaphoreType.DMA, pltpu.VMEM
    anywhere = pl.BlockSpec(memory_space=pl.ANY)
    token_block = pl.BlockSpec((q, half), lambda i: (fold(i), 0))
    ins = {
        "x_own": (inputs, token_block),
        "c_own": (cotangent, token_block),
        "x_any": (inputs, anywhere),
        "c_any": (cotangent, anywhere),
        "gain_in": (norm_gain, whole(half)),
        "seg": (segments, pl.BlockSpec((1, q), lambda i: (0, fold(i)))),
        "conv_in": (jnp.transpose(conv_inner, (1, 0, 2)), whole(nh, 4, pc)),
        "bias_in": (bias_inner, whole(nh, pc)),
        "gate_gain": (gate_norm, whole(nh, pc)),
        "conv_st": (conv_state, whole(4, state_width)),
        "bias_st": (bias_state[None], whole(1, state_width)),
        "step_bias": (step_bias[None], whole(1, nh)),
        "decay_log": (decay_log[None], whole(1, nh)),
        "skip_gain": (skip_gain[None], whole(1, nh)),
    }
    outs = {
        "out_total": (sds((length, half), BF16), anywhere),
        "dn_total": (sds((length, half), BF16), anywhere),
        "token_out": (sds((3 * blocks, q), F32), whole(3 * blocks, q)),
        "vec_out": (sds((8, conv_rows), F32), whole(8, conv_rows)),
    }
    scratch = {
        "acc_w": vmem((rows, width), F32),
        "x_scr": vmem((blocks, q, half), BF16),
        "c_scr": vmem((blocks, q, half), BF16),
        "gain_own": vmem((1, half), F32),
        "gain_sib": vmem((1, half), F32),
        "conv": vmem((conv_rows, 128), F32),
        "head": vmem((STEP_ROWS, 128), F32),
        "prev_seg": vmem((1, 128), F32),
        "pre": vmem((conv_rows, length + 128), F32),
        "step": vmem((STEP_ROWS, length), F32),
        "gate": vmem((inner, length), BF16),
        "mixed": vmem((inner, length), F32),
        "dng": vmem((inner, length), BF16),
        "aux": vmem((8, length), F32),
        "scale": vmem((q, 128), F32),
        "states": vmem((blocks, inner, ns), F32),
        "state": vmem((inner, ns), F32),
        "stats": vmem((group, 2 * blocks, q), F32),
        "work": vmem((inner, q), F32),
        "slope": vmem((conv_rows, q), F32),
        "low": vmem((out_at, q), BF16),
        "after": vmem((3, conv_rows, 128), F32),
        "acc_conv": vmem((5, conv_rows, 128), F32),
        "acc_chan": vmem((2, inner, 128), F32),
        "acc_head": vmem((2, STEP_ROWS, 128), F32),
        "acc_norm": vmem((2, 8, half), F32),
        "acc_dot": vmem((q, 128), F32),
        "group_vec": vmem((group, 24, 2 * ns), F32),
        "dp_vec": vmem((4, 8, conv_rows), F32),
        "ch_own": vmem((2 * units, q // units, half), BF16),
        "ch_sib": vmem((2 * units, q // units, half), BF16),
        "ch_first": vmem((slots, q // units, half), BF16),
        "ch_pair": vmem((slots, q // units, half), BF16),
        "ch_cross": vmem((slots, q // units, half), BF16),
        "cs_send": dma((3, slots)),
        "cs_recv": dma((3, slots)),
        "cs_out": dma((2, plan.total)),
        "cs_keep": dma((slots,)),
        "ch_free": pltpu.SemaphoreType.REGULAR((3,)),
        "swap_sems": dma((4, blocks + 1)),
        "stat_sems": dma((2, group - 1)),
        "group_sems": dma((2, group - 1)),
        "dp_sems": dma((2, 3)),
    }
    if gathers:
        for name, part in zip(("inner_w", "state_w", "step_w", "gate_w", "out_w"), parts):
            ins[name] = (part, whole(*part.shape) if name == "step_w" else anywhere)
        grad_shape = sds((inner, share), F32)
        outs["g_inner"] = (grad_shape, whole(inner, share))
        outs["g_gate"] = (grad_shape, whole(inner, share))
        outs["g_out"] = (grad_shape, whole(inner, share))
        outs["g_state"] = (sds((share, state_width), F32), whole(share, state_width))
        outs["g_step"] = (sds((STEP_ROWS, share), F32), whole(STEP_ROWS, share))
        pieces = (group, state_width // group, share)
        early_rows = state_width + STEP_ROWS
        late_half = (rows - early_rows) // 2
        scratch.update(
            weights=vmem((rows, width), BF16),
            gather_sems=dma((8, 4)),
            raw_sems=dma((4,)),
            ea_top=vmem((2, cfg.early_split, share), BF16),
            ea_low=vmem((2, early_rows - cfg.early_split, share), BF16),
            ea_top_last=vmem((cfg.early_split, share), BF16),
            ea_low_last=vmem((early_rows - cfg.early_split, share), BF16),
            ea_sems=dma((4, 3)),
            rs_top=vmem((2, late_half, share), BF16),
            rs_low=vmem((2, late_half, share), BF16),
            rs_top_last=vmem((late_half, share), BF16),
            rs_low_last=vmem((late_half, share), BF16),
            rs_sems=dma((4, 3)),
            step_swap=vmem((2, STEP_ROWS, share), F32),
            state_send=vmem(pieces, BF16),
            state_recv=vmem(pieces, BF16),
            state_all=vmem(pieces, BF16),
            state_sems=dma((4, group)),
        )
    else:
        ins["weights"] = (parts[0], whole(rows, width))
        outs["grad_w"] = (sds((rows, width), BF16), whole(rows, width))
    names = (*ins, *outs, *scratch)
    results = pl.pallas_call(
        functools.partial(layer_kernel, cfg, plan, names),
        name="layer",
        grid=(3 * blocks,),
        in_specs=[spec for _, spec in ins.values()],
        out_specs=[spec for _, spec in outs.values()],
        out_shape=[shape for shape, _ in outs.values()],
        scratch_shapes=list(scratch.values()),
        compiler_params=pltpu.CompilerParams(
            vmem_limit_bytes=VMEM_LIMIT, collective_id=1, has_side_effects=True
        ),
        cost_estimate=pl.CostEstimate(
            flops=6 * length * width * rows,
            bytes_accessed=60 << 20,
            transcendentals=2 * nh * length * q,
        ),
    )(*(array for array, _ in ins.values()))
    made = types.SimpleNamespace(**dict(zip(outs, results, strict=True)))
    if gathers:
        return finish(nh, blocks, made, inputs, cotangent, norm_gain, decay_log[None], ns)
    tokens = made.token_out.reshape(3, length)
    scale, pull, gate_scale = (tokens[k][:, None] for k in range(3))
    plain = inputs.astype(F32)
    output = (plain + gate_scale * made.out_total.astype(F32)).astype(BF16)
    weighted = made.dn_total.astype(F32) * gain_own
    grad_inputs = cotangent.astype(F32) + scale * weighted - plain * pull
    vectors = made.vec_out
    grads = lax.psum_scatter(made.grad_w, "dp", scatter_dimension=1, tiled=True)
    grads = grads.astype(F32)
    vectors = lax.psum(vectors, "dp")
    g_state = lax.psum(grads[0:state_width], ("row", "col")).T
    g_step = lax.psum(grads[state_width : state_width + STEP_ROWS], "row")
    g_inner = grads[state_width + STEP_ROWS : gate_at]
    g_gate = grads[gate_at:out_at]
    g_out = grads[out_at:]

    def feature_rows(w):
        return jnp.transpose(w.reshape(nh, pc, share), (2, 0, 1))

    channel_vecs = vectors[:, 0:inner].reshape(8, nh, pc)
    grad_norm = jnp.concatenate([vectors[6, inner:], vectors[7, : half - 2 * ns]])
    return (
        output,
        grad_inputs,
        grad_norm,
        feature_rows(g_gate),
        feature_rows(g_inner),
        g_state,
        g_step[:nh].T,
        channel_vecs[0:4],
        channel_vecs[4],
        vectors[0:4, inner:],
        vectors[4, inner:],
        vectors[5, inner : inner + nh],
        -vectors[5, inner + 128 : inner + 128 + nh] * jnp.exp(decay_log),
        jnp.sum(channel_vecs[6], axis=1),
        channel_vecs[5],
        feature_rows(g_out),
    )


def finish(nh, blocks, made, inputs, cotangent, gain_own, decay_log, ns):
    length, half = inputs.shape
    inner, share = made.g_inner.shape
    pc = inner // nh
    q = length // blocks
    steps = FINISH_STEPS
    sds = jax.ShapeDtypeStruct

    def whole(*shape):
        return pl.BlockSpec(shape, lambda i: (0,) * len(shape))

    tokens = pl.BlockSpec((length // steps, half), lambda i: (i, 0))
    rows = pl.BlockSpec((inner // steps, share), lambda i: (i, 0))
    state_rows = pl.BlockSpec((share // steps, 2 * ns), lambda i: (i, 0))
    grad = sds((inner, share), F32)
    (
        output,
        grad_inputs,
        g_inner,
        g_gate,
        g_out,
        g_state,
        g_step,
        norm,
        conv_inner,
        bias_inner,
        conv_state,
        bias_state,
        step_bias,
        decay,
        skip,
        gate_norm,
    ) = pl.pallas_call(
        functools.partial(finish_kernel, nh),
        name="finish",
        grid=(steps,),
        in_specs=[
            tokens,
            tokens,
            tokens,
            tokens,
            whole(3 * blocks, q),
            whole(half),
            whole(*made.vec_out.shape),
            whole(1, nh),
            rows,
            rows,
            rows,
            state_rows,
            whole(STEP_ROWS, share),
        ],
        out_specs=[
            tokens,
            tokens,
            rows,
            rows,
            rows,
            state_rows,
            whole(nh, share),
            whole(half),
            whole(nh, 4, pc),
            whole(nh, pc),
            whole(4, 2 * ns),
            whole(2 * ns),
            whole(nh),
            whole(nh),
            whole(nh),
            whole(nh, pc),
        ],
        out_shape=[
            sds((length, half), BF16),
            sds((length, half), F32),
            grad,
            grad,
            grad,
            sds((share, 2 * ns), F32),
            sds((nh, share), F32),
            sds((half,), F32),
            sds((nh, 4, pc), F32),
            sds((nh, pc), F32),
            sds((4, 2 * ns), F32),
            sds((2 * ns,), F32),
            sds((nh,), F32),
            sds((nh,), F32),
            sds((nh,), F32),
            sds((nh, pc), F32),
        ],
        compiler_params=pltpu.CompilerParams(vmem_limit_bytes=VMEM_LIMIT),
    )(
        inputs,
        cotangent,
        made.out_total,
        made.dn_total,
        made.token_out,
        gain_own,
        made.vec_out,
        decay_log,
        made.g_inner,
        made.g_gate,
        made.g_out,
        made.g_state,
        made.g_step,
    )

    def feature_rows(w):
        return jnp.transpose(w.reshape(nh, pc, share), (2, 0, 1))

    return (
        output,
        grad_inputs,
        norm,
        feature_rows(g_gate),
        feature_rows(g_inner),
        g_state,
        g_step.T,
        jnp.transpose(conv_inner, (1, 0, 2)),
        bias_inner,
        conv_state,
        bias_state,
        step_bias,
        decay,
        skip,
        gate_norm,
        feature_rows(g_out),
    )


def solution(mesh):
    return jax.shard_map(
        per_device,
        mesh=mesh,
        in_specs=(
            P("dp", "row"),
            P("dp", None),
            P("dp", "row"),
            P("row"),
            P("dp", "col", "row"),
            P("dp", "col", "row"),
            P("dp", None),
            P("dp", "col"),
            P(None, "col", "row"),
            P("col", "row"),
            P(),
            P(),
            P("col"),
            P("col"),
            P("col"),
            P("col", "row"),
            P("dp", "col", "row"),
        ),
        out_specs=(
            P("dp", "row"),
            P("dp", "row"),
            P("row"),
            P("dp", "col", "row"),
            P("dp", "col", "row"),
            P("dp", None),
            P("dp", "col"),
            P(None, "col", "row"),
            P("col", "row"),
            P(),
            P(),
            P("col"),
            P("col"),
            P("col"),
            P("col", "row"),
            P("dp", "col", "row"),
        ),
        check_vma=False,
    )
```

```python
import functools
import types

import jax
import jax.numpy as jnp
from jax import lax
from jax.experimental import pallas as pl
from jax.experimental.pallas import tpu as pltpu
from jax.sharding import PartitionSpec as P

H = 48
P_SIZE = 64
BLOCK_LEN = 256
EPSILON = 1e-05
NEG = -1e30
STEP_ROWS = 16
UNITS = 2
UP_AT = (0.45, None, None, None, None, None, None, 0.8)
DOWN_AT = (None, None, None, 0.22, 0.35, 0.5, 0.65, 0.78)
TURN_AT = (0.3, 0.6, 0.9)
AHEAD = 5
MODEL = (2.4, 3.7, 10.0, 8.2, 8.0, 0.5)
FORWARD_AT = (1, 3)
STOPS = (1, 1, 2, 3, 4, 7, 7, 8, 10)
DEPTH = 2
VMEM_LIMIT = 63 << 20
FINISH_STEPS = 2
F32 = jnp.float32
BF16 = jnp.bfloat16
HIGHEST = lax.Precision.HIGHEST


def dot_nn(left, right, precision=None):
    return lax.dot_general(
        left, right, (((1,), (0,)), ((), ())), preferred_element_type=F32, precision=precision
    )


def dot_nt(left, right, precision=None):
    return lax.dot_general(
        left, right, (((1,), (1,)), ((), ())), preferred_element_type=F32, precision=precision
    )


def dot_tn(left, right):
    return lax.dot_general(left, right, (((0,), (0,)), ((), ())), preferred_element_type=F32)


def sigmoid(values):
    return 0.5 * jnp.tanh(0.5 * values) + 0.5


def softplus(values):
    return jnp.maximum(values, 0.0) + jnp.log1p(jnp.exp(-jnp.abs(values)))


def lane_fold(values):
    total = values[:, :128]
    for at in range(128, values.shape[1], 128):
        total = total + values[:, at : at + 128]
    return total


def columns_of(rows):
    padded = jnp.concatenate([rows, jnp.zeros((128 - rows.shape[0], rows.shape[1]), F32)], axis=0)
    return padded.T


def rows_of(ref):
    lanes = lax.broadcasted_iota(jnp.int32, ref.shape[1:], 1)
    total = jnp.zeros(ref.shape[1:], F32)
    for at in range(ref.shape[0]):
        total = jnp.where(lanes == at, jnp.sum(ref[at], axis=1, keepdims=True), total)
    if total.shape[0] % 128:
        total = jnp.concatenate([total, jnp.zeros((128 - total.shape[0], 128), F32)], axis=0)
    return total.T[0:8]


def pad_lanes(rows):
    return jnp.concatenate([rows, jnp.zeros((rows.shape[0], 128 - rows.shape[1]), F32)], axis=1)


def load_columns(r):
    nh, taps, pc = r.conv_in.shape
    rows = []
    for h in range(nh):
        rows += [r.conv_in[h], r.bias_in[h : h + 1], r.gate_gain[h : h + 1]]
        rows += [jnp.zeros((2, pc), F32)]
    cols = columns_of(pad_lanes(jnp.concatenate(rows, axis=0)))[0:pc]
    for h in range(nh):
        turned = pltpu.roll(cols, 128 - 8 * h, axis=1) if h else cols
        r.conv[h * pc : (h + 1) * pc] = turned
    state_rows = jnp.concatenate([r.conv_st[...], r.bias_st[...]], axis=0)
    r.conv[nh * pc :] = columns_of(state_rows)
    head_rows = jnp.concatenate([r.step_bias[...], r.decay_log[...], r.skip_gain[...]], axis=0)
    heads = columns_of(pad_lanes(head_rows))[0:STEP_ROWS]
    lanes = lax.broadcasted_iota(jnp.int32, heads.shape, 1)
    r.head[...] = jnp.where(lanes == 1, -jnp.exp(heads), heads)


def block_rows(dims, step_pre, hrow, aux):
    q = step_pre.shape[1]
    step_arg = step_pre + hrow[:, 0:1]
    step = softplus(step_arg)
    log_decay = step * hrow[:, 1:2]
    source = lax.broadcasted_iota(jnp.int32, (q, q), 0)
    target = lax.broadcasted_iota(jnp.int32, (q, q), 1)
    upper = (source <= target).astype(F32)
    cumul = dot_nn(log_decay, upper, HIGHEST)
    last = cumul[:, q - 1 : q]
    cols = columns_of(jnp.concatenate([cumul, aux], axis=0))
    return step_arg, step, cumul, last, cols


MESH = pl.DeviceIdType.MESH


def send(src, dst, sems, at, **device):
    return pltpu.make_async_remote_copy(
        src_ref=src,
        dst_ref=dst,
        send_sem=sems[0].at[at],
        recv_sem=sems[1].at[at],
        device_id=device,
        device_id_type=MESH,
    )


def group_peers(row_count, col_count):
    row_at, col_at = lax.axis_index("row"), lax.axis_index("col")
    return [
        dict(row=lax.rem(row_at + j, row_count), col=lax.rem(col_at + k, col_count))
        for k in range(col_count)
        for j in range(row_count)
        if (j, k) != (0, 0)
    ]


def greet(peers):
    barrier = pltpu.get_barrier_semaphore()
    for peer in peers:
        pl.semaphore_signal(barrier, inc=1, device_id=peer, device_id_type=MESH)


def greeted(peers):
    pl.semaphore_wait(pltpu.get_barrier_semaphore(), len(peers))


def add_low(left, right):
    return left + right


class Chain:
    def __init__(self, r, total, turn, first_rows, second_rows):
        self.total, self.turn = total, turn
        self.own, self.sib = r.ch_own, r.ch_sib
        self.first, self.pair, self.cross = r.ch_first, r.ch_pair, r.ch_cross
        self.slots = self.first.shape[0]
        self.out_slots = self.own.shape[0]
        self.sems = [(r.cs_send.at[k], r.cs_recv.at[k]) for k in range(3)]
        self.sems.append((r.cs_out.at[0], r.cs_out.at[1]))
        self.keep_sems = r.cs_keep
        self.free = r.ch_free
        self.first_rows, self.second_rows = first_rows, second_rows
        self.row_at, self.col_at = lax.axis_index("row"), lax.axis_index("col")
        self.is_outer = (self.col_at == 0) | (self.col_at == 3)
        self.inward = 1 + lax.div(self.col_at, 2)
        self.outward = 3 * lax.div(self.col_at, 2)

    def slot(self, m):
        return lax.rem(m, self.slots)

    def out_slot(self, m):
        return lax.rem(m, self.out_slots)

    def exchange(self, m):
        return send(
            self.sib.at[self.out_slot(m)],
            self.first.at[self.slot(m)],
            self.sems[0],
            self.slot(m),
            row=1 - self.row_at,
        )

    def to_inner(self, m):
        at = self.slot(m)
        return send(self.first.at[at], self.pair.at[at], self.sems[1], at, col=self.inward)

    def across(self, m):
        at = self.slot(m)
        return send(self.pair.at[at], self.cross.at[at], self.sems[2], at, col=3 - self.col_at)

    def to_outer(self, m, rows):
        return send(self.cross.at[self.slot(m)], rows, self.sems[3], m, col=self.outward)

    def keep(self, m, rows):
        at = self.slot(m)
        return pltpu.make_async_copy(self.cross.at[at], rows, self.keep_sems.at[at])

    def credit(self, which, m, **device):
        @pl.when(m < self.total - self.slots)
        def _():
            pl.semaphore_signal(
                self.free.at[which], inc=1, device_id=device, device_id_type=MESH
            )

    def spend(self, which, m):
        @pl.when(m >= self.slots)
        def _():
            pl.semaphore_wait(self.free.at[which], 1)

    def begin(self, m, sib_part):
        @pl.when(m >= self.out_slots)
        def _():
            self.exchange(m - self.out_slots).wait_send()

        self.sib[self.out_slot(m)] = sib_part
        self.spend(0, m)
        self.exchange(m).start()

    def put_own(self, m, own_part):
        self.own[self.out_slot(m)] = own_part

    def stage_first(self, m):
        at = self.slot(m)
        self.exchange(m).wait_recv()
        self.first[at] = add_low(self.own[self.out_slot(m)], self.first[at])

        @pl.when(self.is_outer & (m < DEPTH))
        def _():
            self.to_inner(m).start()

    def stage_pair(self, m):
        at = self.slot(m)

        @pl.when(self.is_outer)
        def _():
            self.to_inner(m).wait_send()

            @pl.when(m + DEPTH < self.total)
            def _():
                self.spend(1, m + DEPTH)
                self.to_inner(m + DEPTH).start()

        @pl.when(~self.is_outer)
        def _():
            self.to_inner(m).wait_recv()
            self.pair[at] = add_low(self.first[at], self.pair[at])
            self.spend(2, m)
            self.across(m).start()

        self.credit(0, m, row=1 - self.row_at)

    def stage_cross(self, m):
        at = self.slot(m)

        @pl.when(~self.is_outer)
        def _():
            self.across(m).wait()
            self.cross[at] = add_low(self.pair[at], self.cross[at])
            self.credit(1, m, col=self.outward)

            @pl.when(m < self.turn)
            def _():
                self.keep(m, self.first_rows(m)).start()
                self.to_outer(m, self.first_rows(m)).start()

            @pl.when(m >= self.turn)
            def _():
                self.keep(m, self.second_rows(m)).start()
                self.to_outer(m, self.second_rows(m)).start()

    def stage_done(self, m):
        @pl.when(~self.is_outer)
        def _():
            rows = self.first_rows(0)
            self.keep(m, rows).wait()
            self.to_outer(m, rows).wait_send()
            self.credit(2, m, col=3 - self.col_at)

    def totals(self):
        @pl.when(self.is_outer)
        def _():
            def one(m, _):
                self.to_outer(m, self.first_rows(0)).wait_recv()
                return 0

            lax.fori_loop(0, self.total, one, 0)


class Plan:
    def __init__(self, blocks, units, slots, up_us, scan_us, gap, down_us, hop, lag):
        steps = 2 * blocks
        self.total = steps * units
        self.per_step = len(UP_AT)
        self.points = steps * self.per_step
        hop = hop / units
        mixed = blocks - AHEAD
        lengths = [up_us + scan_us] * mixed + [up_us] * AHEAD + [down_us] * blocks
        starts = [0.0]
        for step in range(1, steps):
            pause = gap if step == blocks else 0.0
            starts.append(starts[-1] + lengths[step - 1] + pause)
        times = []
        for step in range(steps):
            if step < blocks:
                times += [None if at is None else starts[step] + at * up_us for at in UP_AT]
            else:
                times += [
                    None if at is None else starts[step] + at * down_us for at in DOWN_AT
                ]
        for which, at in enumerate(TURN_AT):
            times[self.per_step * blocks + which] = starts[blocks] - gap * (1.0 - at)
        ends = [at + up_us for at in starts[:blocks]]
        ends += [at + down_us for at in starts[blocks:]]

        def point_after(when):
            fits = [p for p, at in enumerate(times) if at is not None and at >= when]
            return fits[0] if fits else self.points

        def exact(point, when):
            known = point < len(times) and times[point] is not None
            return times[point] if known else when

        self.pair, self.cross, self.done = [], [], []
        one = two = three = 0.0
        for m in range(self.total):
            ready = ends[m // units] + 2.0
            if m >= DEPTH:
                ready = max(ready, taken[m - DEPTH])
            else:
                taken = taken if m else []
            one = max(one, ready) + hop
            point = point_after(one + lag)
            if m + DEPTH < self.total:
                point = max(point, self.per_step * ((m + DEPTH) // units + 1))
            if m + slots < self.total:
                point = min(point, self.per_step * ((m + slots) // units + 1) - 1)
            point = min(point, self.points)
            self.pair.append(point)
            taken_at = exact(point, one + lag)
            taken.append(taken_at)
            two = max(two, taken_at) + hop
            point = max(point_after(two + lag), point)
            self.cross.append(point)
            three = max(three, exact(point, two + lag)) + hop
            self.done.append(point_after(three + lag))
        for m in range(self.total - slots):
            self.done[m] = max(min(self.done[m], self.pair[m + slots]), self.cross[m])
        self.end = three + lag

    def span(self, table, which, step, steps):
        first = count = 0
        for point in sorted(set(table)):
            on = point // self.per_step
            if on in steps and point % self.per_step == which:
                hit = (step == on).astype(jnp.int32)
                first = first + table.index(point) * hit
                count = count + table.count(point) * hit
        return first, first + count

    def left(self, table):
        return sum(1 for at in table if at < self.points)


class Gather:
    def __init__(self, whole, sems, groups):
        self.whole, self.groups = whole, groups
        self.sems = sems
        at = lax.axis_index("dp")
        self.at = at
        self.near = at + 1 - 2 * lax.rem(at, 2)
        self.far = lax.rem(at + 2, 4)
        self.share = whole.shape[1] // 4

    def part(self, shard, lo, hi):
        return self.whole.at[
            lo:hi, pl.ds(pl.multiple_of(shard * self.share, 128), self.share)
        ]

    def direct(self, g, to_near):
        lo, _, hi = self.groups[g]
        return send(
            self.part(self.at, lo, hi),
            self.part(self.at, lo, hi),
            self.sems[0 if to_near else 1],
            g,
            dp=self.near if to_near else self.far,
        )

    def onward(self, g, from_near):
        lo, mid, hi = self.groups[g]
        lo, hi = (lo, mid) if from_near else (mid, hi)
        part = self.part(self.near if from_near else self.far, lo, hi)
        return send(
            part,
            part,
            self.sems[2 if from_near else 3],
            g,
            dp=self.far if from_near else self.near,
        )

    def start(self, g):
        self.direct(g, True).start()
        self.direct(g, False).start()

    def forward(self, g):
        for which in (True, False):
            self.direct(g, which).wait_recv()
            self.onward(g, which).start()

    def take(self, g):
        self.onward(g, True).wait_recv()
        self.onward(g, False).wait_recv()

    def finish(self):
        for g in range(len(self.groups)):
            for which in (True, False):
                self.direct(g, which).wait_send()
                self.onward(g, which).wait_send()


class Reduce:
    def __init__(self, acc, stage, bounds, bufs, sems):
        self.acc, self.stage = acc, stage
        self.halves = (bounds[0:2], bounds[1:3])
        self.bufs, self.sems = bufs, sems
        at = lax.axis_index("dp")
        self.at = at
        self.near = at + 1 - 2 * lax.rem(at, 2)
        self.far = lax.rem(at + 2, 4)
        self.share = acc.shape[1] // 4

    def cols(self, shard):
        return pl.ds(pl.multiple_of(shard * self.share, 128), self.share)

    def first(self, half, slot):
        lo, hi = self.halves[half]
        to = (self.near, self.far)[half]
        shard = to if slot == 0 else 3 - self.at
        return send(
            self.stage.at[lo:hi, self.cols(shard)],
            self.bufs[half].at[slot],
            self.sems[half],
            slot,
            dp=to,
        )

    def second(self, half):
        return send(
            self.bufs[half].at[1],
            self.bufs[2 + half],
            self.sems[half],
            2,
            dp=(self.far, self.near)[half],
        )

    def start(self):
        for slot in (1, 0):
            for half in range(2):
                self.first(half, slot).start()

    def middle(self):
        for half in range(2):
            lo, hi = self.halves[half]
            other = (self.far, self.near)[half]
            self.first(half, 1).wait_recv()
            self.bufs[half][1] = (
                self.acc[lo:hi, self.cols(other)] + self.bufs[half][1].astype(F32)
            ).astype(BF16)
            self.second(half).start()

    def end(self):
        for half in range(2):
            lo, hi = self.halves[half]
            self.first(half, 0).wait_recv()
            self.second(half).wait_recv()
            mine = self.cols(self.at)
            self.acc[lo:hi, mine] = (
                self.acc[lo:hi, mine]
                + self.bufs[half][0].astype(F32)
                + self.bufs[2 + half][...].astype(F32)
            )

    def finish(self):
        for half in range(2):
            self.first(half, 0).wait_send()
            self.first(half, 1).wait_send()
            self.second(half).wait_send()


def layer_kernel(cfg, plan, names, *refs):
    r = types.SimpleNamespace(**dict(zip(names, refs, strict=True)))
    nh, pc, ns, width = cfg.nh, cfg.pc, cfg.ns, cfg.width
    gathers, blocks, units = cfg.gathers, cfg.blocks, cfg.units
    inner = nh * pc
    conv_rows = inner + 2 * ns
    step_row = 2 * ns
    inner_at = step_row + STEP_ROWS
    gate_at = inner_at + inner
    out_at = gate_at + inner
    rows = out_at + inner
    q, half = r.x_own.shape
    hq = q // 2
    unit_rows = q // units
    inner_width = H * P_SIZE
    step_at = pl.program_id(0)
    scans, block_at = walk(step_at, blocks)
    goes_down = step_at >= 2 * blocks
    chain_step = jnp.where(goes_down, step_at - blocks, block_at)
    row_at, col_at, dp_at = (lax.axis_index(name) for name in ("row", "col", "dp"))
    own_at = pl.multiple_of(row_at * half, 128)
    sib_at = pl.multiple_of((1 - row_at) * half, 128)
    own_cols, sib_cols = pl.ds(own_at, half), pl.ds(sib_at, half)
    group = cfg.row_count * cfg.col_count
    me = row_at * cfg.col_count + col_at
    peers = group_peers(cfg.row_count, cfg.col_count)
    friends = [dict(dp=lax.rem(dp_at + k, 4)) for k in range(1, 4)] if gathers else []
    weights = r.weights

    def out_rows(m):
        return r.out_total.at[pl.ds(pl.multiple_of(m * unit_rows, unit_rows), unit_rows)]

    def dn_rows(m):
        at = (2 * blocks - 1 - lax.div(m, units)) * q + lax.rem(m, units) * unit_rows
        return r.dn_total.at[pl.ds(pl.multiple_of(at, unit_rows), unit_rows)]

    chain = Chain(r, plan.total, blocks * units, out_rows, dn_rows)

    def send_parts(sib_part, own_part):
        for u in range(units):
            lo = u * unit_rows
            chain.begin(chain_step * units + u, sib_part[lo : lo + unit_rows])
        own = own_part()
        for u in range(units):
            lo = u * unit_rows
            chain.put_own(chain_step * units + u, own[lo : lo + unit_rows].astype(BF16))
        return own

    def progress(which, steps):
        if which == 0:

            @pl.when(chain_step > 0)
            def _():
                for u in range(units):
                    chain.stage_first((chain_step - 1) * units + u)

        for table, stage in (
            (plan.done, chain.stage_done),
            (plan.pair, chain.stage_pair),
            (plan.cross, chain.stage_cross),
        ):

            def one(m, _, stage=stage):
                stage(m)
                return 0

            lo, hi = plan.span(table, which, chain_step, steps)
            if lo is not hi:
                lax.fori_loop(lo, hi, one, 0)

    up_steps, down_steps = range(blocks), range(blocks, 2 * blocks)

    def token_rows(ref, b):
        return ref.at[pl.ds(pl.multiple_of(b * q, q), q)]

    def swap(which, b):
        src, dst = ((r.x_any, r.x_scr), (r.c_any, r.c_scr))[which]
        sems = (r.swap_sems.at[2 * which], r.swap_sems.at[2 * which + 1])
        return send(token_rows(src, b), dst.at[b], sems, b, row=1 - row_at)

    gain_swap = send(
        r.gain_own,
        r.gain_sib,
        (r.swap_sems.at[0], r.swap_sems.at[1]),
        blocks,
        row=1 - row_at,
    )

    def stat_copy(k):
        sems = (r.stat_sems.at[0], r.stat_sems.at[1])
        return send(r.stats.at[me], r.stats.at[me], sems, k, **peers[k])

    if gathers:
        bounds = (
            (0, cfg.early_split, inner_at),
            (inner_at, inner_at + inner // 2, gate_at),
            (gate_at, gate_at + inner // 2, out_at),
            (out_at, out_at + inner // 2, rows),
        )
        sems = [(r.gather_sems.at[2 * k], r.gather_sems.at[2 * k + 1]) for k in range(4)]
        gather = Gather(weights, sems, bounds)
        early = Reduce(
            r.acc_w,
            weights,
            (0, cfg.early_split, inner_at),
            (r.ea_top, r.ea_low, r.ea_top_last, r.ea_low_last),
            [(r.ea_sems.at[2 * k], r.ea_sems.at[2 * k + 1]) for k in range(2)],
        )
        late = Reduce(
            r.acc_w,
            weights,
            (inner_at, (inner_at + rows) // 2, rows),
            (r.rs_top, r.rs_low, r.rs_top_last, r.rs_low_last),
            [(r.rs_sems.at[2 * k], r.rs_sems.at[2 * k + 1]) for k in range(2)],
        )
        share = width // 4
        mine = early.cols(dp_at)
        raw = (
            (r.inner_w, 0, inner, 0, share),
            (r.state_w, 0, share, share, 2 * ns),
            (r.gate_w, inner, inner, 0, share),
            (r.out_w, 2 * inner, inner, 0, share),
        )

        def raw_copy(k):
            src, lo, count, at, size = raw[k]
            return pltpu.make_async_copy(
                src, r.acc_w.at[lo : lo + count, at : at + size], r.raw_sems.at[k]
            )

        def raw_value(k):
            _, lo, count, at, size = raw[k]
            return r.acc_w[lo : lo + count, at : at + size]

    @pl.when(step_at == 0)
    def _():
        greet(peers + friends)
        r.gain_own[...] = r.gain_in[...].reshape(1, half)
        if gathers:
            for k in range(len(raw)):
                raw_copy(k).start()
            for k in range(len(raw)):
                raw_copy(k).wait()
            step_rows = jnp.concatenate(
                [r.step_w[...], jnp.zeros((STEP_ROWS - nh, share), F32)], axis=0
            )
            weights[0:step_row, mine] = raw_value(1).T.astype(BF16)
            weights[step_row:inner_at, mine] = step_rows.astype(BF16)
            weights[inner_at:gate_at, mine] = raw_value(0).astype(BF16)
            weights[gate_at:out_at, mine] = raw_value(2).astype(BF16)
            weights[out_at:, mine] = raw_value(3).astype(BF16)
        greeted(peers + friends)
        if gathers:
            gather.start(0)
            gather.start(1)
        gain_swap.start()
        for b in range(blocks):
            swap(0, b).start()
            swap(1, b).start()
        load_columns(r)
        for ref in (r.acc_w, r.state, r.after, r.acc_conv, r.acc_chan, r.acc_head):
            ref[...] = jnp.zeros_like(ref)
        for ref in (r.acc_norm, r.acc_dot, r.scale):
            ref[...] = jnp.zeros_like(ref)
        r.pre[:, 0:128] = jnp.zeros((conv_rows, 128), F32)
        r.prev_seg[...] = jnp.full_like(r.prev_seg, -1.0)
        gain_swap.wait_recv()
        if gathers:
            gather.forward(0)
            gather.forward(1)
            gather.start(2)
            gather.start(3)
            gather.take(0)
            gather.take(1)

    def scan_step():
        b = block_at
        here = pl.ds(pl.multiple_of(b * q, q), q)
        swap(0, b).wait_recv()
        xo = r.x_own[...].astype(F32)
        xs = r.x_scr[b].astype(F32)
        squares = jnp.sum(xo * xo, axis=1, keepdims=True) + jnp.sum(
            xs * xs, axis=1, keepdims=True
        )
        scaling = lax.rsqrt(squares / width + EPSILON)
        lanes = lax.broadcasted_iota(jnp.int32, r.scale.shape, 1)
        r.scale[...] = jnp.where(lanes == b, scaling, r.scale[...])
        no = (xo * scaling * r.gain_own[...]).astype(BF16)
        nsib = (xs * scaling * r.gain_sib[...]).astype(BF16)
        pre = dot_nt(weights[0:gate_at, own_cols], no) + dot_nt(weights[0:gate_at, sib_cols], nsib)
        values = jnp.concatenate([pre[inner_at:gate_at], pre[0:step_row]], axis=0)
        step_pre = pre[step_row:inner_at]
        r.pre[:, pl.ds(pl.multiple_of(b * q + 128, 128), q)] = values
        r.step[:, here] = step_pre
        seg = r.seg[...].astype(F32)
        seg_before = r.prev_seg[...]
        seg_joined = jnp.concatenate([seg_before, seg], axis=1)
        before, final = seg_before[:, 127:128], seg[:, q - 1 : q]
        aux = jnp.concatenate(
            [
                (seg_joined[:, 128 - offset : 128 - offset + q] == seg).astype(F32)
                for offset in range(1, 4)
            ]
            + [
                seg,
                (seg == before).astype(F32),
                (seg == final).astype(F32),
                jnp.broadcast_to((before == final).astype(F32), (1, q)),
                jnp.zeros((1, q), F32),
            ],
            axis=0,
        )
        r.prev_seg[...] = seg[:, q - 128 :]
        r.aux[:, here] = aux
        conv = r.conv[...]
        head = r.head[...]
        arg = conv_args(r, conv, aux, b, q)
        act = arg * sigmoid(arg)
        r.work[...] = act[0:inner]
        in_low = act[inner : inner + ns].astype(BF16)
        out_low = act[inner + ns :].astype(BF16)

        _, step, cumul, last, cols = block_rows(None, step_pre, head, aux)
        source = lax.broadcasted_iota(jnp.int32, (q, q), 0)
        target = lax.broadcasted_iota(jnp.int32, (q, q), 1)
        seg_col = cols[:, STEP_ROWS + 3 : STEP_ROWS + 4]
        bias = jnp.where((source <= target) & (seg_col == aux[3:4]), 0.0, NEG)
        pairs = dot_tn(in_low, out_low)
        entering = r.state[...]
        r.states[b] = entering
        from_state = dot_nn(entering.astype(BF16), out_low)
        reach = aux[4:5] * jnp.exp(cumul)
        tails = aux[5:6] * jnp.exp(last - cumul)
        keep = aux[6:7, 0:1] * jnp.exp(last)
        tail_parts = []
        for h in range(nh):
            lo = h * pc
            x_h = r.work[lo : lo + pc]
            u_h = (x_h * step[h : h + 1]).astype(BF16)
            tail_parts.append((x_h * (step[h : h + 1] * tails[h : h + 1])).astype(BF16))
            col = cols[:, h : h + 1]
            row = cumul[h : h + 1]
            top = (jnp.exp((row - col[:hq]) + bias[:hq]) * pairs[:hq]).astype(BF16)
            low = jnp.exp((row[:, hq:] - col[hq:]) + bias[hq:, hq:]) * pairs[hq:, hq:]
            y_top = dot_nn(u_h[:, :hq], top)
            y_low = dot_nn(u_h[:, hq:], low.astype(BF16))
            y_h = jnp.concatenate([y_top[:, :hq], y_top[:, hq:] + y_low], axis=1)
            y_h = y_h + from_state[lo : lo + pc] * reach[h : h + 1]
            r.mixed[lo : lo + pc, here] = y_h + head[h : h + 1, 2:3] * x_h
        contrib = dot_nt(jnp.concatenate(tail_parts, axis=0), in_low)
        for h in range(nh):
            lo = h * pc
            r.state[lo : lo + pc] = keep[h : h + 1] * entering[lo : lo + pc] + contrib[lo : lo + pc]

    def out_step():
        b = block_at
        here = pl.ds(pl.multiple_of(b * q, q), q)
        gain = r.conv[0:inner, 5:6]
        if gathers:

            @pl.when(step_at == AHEAD)
            def _():
                gather.take(2)

        no, nsib, _ = normed_block(b)
        gate = dot_nt(weights[gate_at:out_at, own_cols], no) + dot_nt(
            weights[gate_at:out_at, sib_cols], nsib
        )
        r.gate[:, here] = gate.astype(BF16)
        progress(0, up_steps)
        gated = r.mixed[:, here] * (gate * sigmoid(gate))
        squares_row = jnp.sum(gated * gated, axis=0, keepdims=True)
        weighted = gated * gain
        low = weighted.astype(BF16)
        if gathers:

            @pl.when(step_at == AHEAD)
            def _():
                gather.take(3)

        send_parts(
            dot_tn(low, weights[out_at:, sib_cols]).astype(BF16),
            lambda: dot_tn(low, weights[out_at:, own_cols]),
        )
        progress(7, up_steps)
        swap(1, b).wait_recv()
        dng = dot_nt(weights[out_at:, own_cols], r.c_own[...]) + dot_nt(
            weights[out_at:, sib_cols], r.c_scr[b]
        )
        r.dng[:, here] = dng.astype(BF16)
        r.stats[me, pl.ds(b, 1)] = squares_row
        r.stats[me, pl.ds(blocks + b, 1)] = jnp.sum(dng * weighted, axis=0, keepdims=True)

    def normed_block(b):
        lanes = lax.broadcasted_iota(jnp.int32, r.scale.shape, 1)
        scaling = jnp.sum(jnp.where(lanes == b, r.scale[...], 0.0), axis=1, keepdims=True)
        no = (r.x_own[...].astype(F32) * scaling * r.gain_own[...]).astype(BF16)
        nsib = (r.x_scr[b].astype(F32) * scaling * r.gain_sib[...]).astype(BF16)
        return no, nsib, lanes

    def backward_step():
        b = block_at
        here = pl.ds(pl.multiple_of(b * q, q), q)
        aux = r.aux[:, here]
        conv = r.conv[...]
        gain = conv[0:inner, 5:6]
        head = r.head[...]
        no, nsib, lanes = normed_block(b)
        arg = conv_args(r, conv, aux, b, q)
        sig_arg = sigmoid(arg)
        act = arg * sig_arg
        r.slope[...] = sig_arg * (1.0 + arg * (1.0 - sig_arg))
        x_all = act[0:inner]
        in_low = act[inner : inner + ns].astype(BF16)
        out_low = act[inner + ns :].astype(BF16)
        step_arg, step, cumul, last, cols = block_rows(None, r.step[:, here], head, aux)
        gate = r.gate[:, here].astype(F32)
        sig = sigmoid(gate)
        silu = gate * sig
        mixed = r.mixed[:, here]
        gated = mixed * silu

        for which in range(len(TURN_AT)):
            progress(which, down_steps)

        @pl.when(step_at == 2 * blocks)
        def _():
            for k in range(group - 1):
                stat_copy(k).wait()

        square_sum, gate_dot = jnp.zeros((1, q), F32), jnp.zeros((1, q), F32)
        for k in range(group):
            square_sum = square_sum + r.stats[k, pl.ds(b, 1)]
            gate_dot = gate_dot + r.stats[k, pl.ds(blocks + b, 1)]
        gate_scale = lax.rsqrt(square_sum / inner_width + EPSILON)
        pull = gate_scale * gate_scale * gate_scale * gate_dot / inner_width
        dng_scaled = r.dng[:, here].astype(F32) * gate_scale
        d_gated = gain * dng_scaled - gated * pull
        r.acc_chan[0] += lane_fold(dng_scaled * gated)
        normed_gate = (gated * (gate_scale * gain)).astype(BF16)
        r.acc_w[out_at:, own_cols] += dot_nn(normed_gate, r.c_own[...])
        r.acc_w[out_at:, sib_cols] += dot_nn(normed_gate, r.c_scr[b])
        grad_mixed = d_gated * silu
        r.low[gate_at:out_at] = (d_gated * mixed * (sig * (1.0 + gate * (1.0 - sig)))).astype(BF16)
        progress(3, down_steps)

        t_at = lax.broadcasted_iota(jnp.int32, (q, q), 0)
        s_at = lax.broadcasted_iota(jnp.int32, (q, q), 1)
        seg_col = cols[:, STEP_ROWS + 3 : STEP_ROWS + 4]
        bias = jnp.where((s_at <= t_at) & (seg_col == aux[3:4]), 0.0, NEG)
        pairs = dot_tn(out_low, in_low)
        reach = aux[4:5] * jnp.exp(cumul)
        tails = aux[5:6] * jnp.exp(last - cumul)
        keep = aux[6:7, 0:1] * jnp.exp(last)
        entering = r.states[b]

        @pl.when(step_at == 2 * blocks)
        def _():
            r.state[...] = jnp.zeros_like(r.state)

        d_next = r.state[...]
        from_next = dot_nn(d_next.astype(BF16), in_low)
        r.acc_chan[1] += lane_fold(grad_mixed * x_all)
        d_pairs_top = jnp.zeros((hq, hq), F32)
        d_pairs_low = jnp.zeros((hq, q), F32)
        reach_parts, tail_parts = [], []
        row_sums, col_sums, x_sums, tail_sums, carry_sums = [], [], [], [], []
        for h in range(nh):
            lo = h * pc
            x_h = x_all[lo : lo + pc]
            u_h = x_h * step[h : h + 1]
            u_low = u_h.astype(BF16)
            g_h = grad_mixed[lo : lo + pc]
            g_low = g_h.astype(BF16)
            col = cols[:, h : h + 1]
            row = cumul[h : h + 1]
            reach_parts.append((g_h * reach[h : h + 1]).astype(BF16))
            tail_parts.append((u_h * tails[h : h + 1]).astype(BF16))
            e_top = jnp.exp((col[:hq] - row[:, :hq]) + bias[:hq, :hq])
            e_low = jnp.exp((col[hq:] - row) + bias[hq:])
            m_top = (e_top * pairs[:hq, :hq]).astype(BF16)
            m_low = (e_low * pairs[hq:]).astype(BF16)
            dm_top = dot_tn(g_low[:, :hq], u_low[:, :hq])
            dm_low = dot_tn(g_low[:, hq:], u_low)
            d_pairs_top = d_pairs_top + dm_top * e_top
            d_pairs_low = d_pairs_low + dm_low * e_low
            du_top = dot_nn(g_low[:, :hq], m_top)
            du_low = dot_nn(g_low[:, hq:], m_low)
            du_local = jnp.concatenate([du_top + du_low[:, :hq], du_low[:, hq:]], axis=1)
            du_next = from_next[lo : lo + pc] * tails[h : h + 1]
            du = du_local + du_next
            skip = head[h : h + 1, 2:3]
            r.work[lo : lo + pc] = du * step[h : h + 1] + skip * g_h
            u_round = u_low.astype(F32)
            y_h = mixed[lo : lo + pc] - skip * x_h
            row_sums.append(jnp.sum(g_low.astype(F32) * y_h, axis=0, keepdims=True))
            next_sum = jnp.sum(u_round * du_next, axis=0, keepdims=True)
            col_sums.append(jnp.sum(u_round * du_local, axis=0, keepdims=True) + next_sum)
            tail_sums.append(next_sum)
            x_sums.append(jnp.sum(x_h * du, axis=0, keepdims=True))
            carry_sums.append(
                jnp.sum(entering[lo : lo + pc] * d_next[lo : lo + pc], axis=0, keepdims=True)
            )
            if h in (nh // 3, 2 * nh // 3):
                progress(3 + h // (nh // 3), down_steps)
        progress(6, down_steps)
        pad_rows = [jnp.zeros((STEP_ROWS - nh, q), F32)]
        row_sum = jnp.concatenate(row_sums + pad_rows, axis=0)
        col_sum = jnp.concatenate(col_sums + pad_rows, axis=0)
        tail_sum = jnp.concatenate(tail_sums + pad_rows, axis=0)
        x_sum = jnp.concatenate(x_sums + pad_rows, axis=0)
        carry = jnp.concatenate(carry_sums + [jnp.zeros((STEP_ROWS - nh, ns), F32)], axis=0)
        d_last = jnp.sum(tail_sum, axis=1, keepdims=True) + keep * jnp.sum(
            carry, axis=1, keepdims=True
        )
        later = (t_at >= s_at).astype(F32)
        d_log = dot_nn(row_sum - col_sum, later, HIGHEST) + d_last
        d_step = x_sum + head[:, 1:2] * d_log
        d_step_arg = d_step * sigmoid(step_arg)
        r.acc_head[0] += lane_fold(d_step_arg)
        r.acc_head[1] += lane_fold(step * d_log)
        r.low[step_row:inner_at] = d_step_arg.astype(BF16)

        g_reach = jnp.concatenate(reach_parts, axis=0)
        u_tail = jnp.concatenate(tail_parts, axis=0)
        d_top_low = d_pairs_top.astype(BF16)
        d_low_low = d_pairs_low.astype(BF16)
        d_out = dot_tn(entering.astype(BF16), g_reach)
        d_out = d_out + jnp.concatenate(
            [dot_nt(in_low[:, :hq], d_top_low), dot_nt(in_low, d_low_low)], axis=1
        )
        d_in = dot_tn(d_next.astype(BF16), u_tail) + dot_nn(out_low[:, hq:], d_low_low)
        d_in_top = dot_nn(out_low[:, :hq], d_top_low)
        d_in = jnp.concatenate([d_in[:, :hq] + d_in_top, d_in[:, hq:]], axis=1)
        d_enter = dot_nt(g_reach, out_low)
        for h in range(nh):
            lo = h * pc
            r.state[lo : lo + pc] = keep[h : h + 1] * d_next[lo : lo + pc] + d_enter[lo : lo + pc]

        err = jnp.concatenate([r.work[...], d_in, d_out], axis=0) * r.slope[...]
        values = r.pre[:, pl.ds(pl.multiple_of(b * q + 128, 128), q)]
        d_pre = conv[:, 3:4] * err
        r.acc_conv[3] += lane_fold(err * values)
        r.acc_conv[4] += lane_fold(err)
        for offset in range(1, 4):
            masked = err * aux[offset - 1 : offset]
            joined = jnp.concatenate([masked, r.after[offset - 1]], axis=1)
            shifted = joined[:, offset : offset + q]
            r.after[offset - 1] = masked[:, :128]
            d_pre = d_pre + conv[:, 3 - offset : 4 - offset] * shifted
            r.acc_conv[3 - offset] += lane_fold(shifted * values)
        r.low[inner_at:gate_at] = d_pre[0:inner].astype(BF16)
        r.low[0:step_row] = d_pre[inner:].astype(BF16)
        progress(7, down_steps)
        low = r.low[...]
        dn_sib = dot_tn(low, weights[0:out_at, sib_cols])
        dn_own = send_parts(
            dn_sib.astype(BF16), lambda: dot_tn(low, weights[0:out_at, own_cols])
        )
        token_dot = jnp.zeros((q, 1), F32)
        for which, (part, seen) in enumerate(((dn_own, no), (dn_sib, nsib))):
            product = part * seen.astype(F32)
            token_dot = token_dot + jnp.sum(product, axis=1, keepdims=True)
            r.acc_norm[which] += jnp.sum(product.reshape(q // 8, 8, half), axis=0)
        r.acc_dot[...] = jnp.where(lanes == b, token_dot, r.acc_dot[...])
        r.acc_w[0:out_at, own_cols] += dot_nn(low, no)
        r.acc_w[0:out_at, sib_cols] += dot_nn(low, nsib)

    def ending():
        lane = 2 * ns
        if gathers:
            weights[0:inner_at] = r.acc_w[0:inner_at].astype(BF16)
            early.start()
        else:
            r.grad_w[...] = r.acc_w[...].astype(BF16)
        for u in range(units):
            chain.stage_first((2 * blocks - 1) * units + u)
        zeros = jnp.zeros((1, 128), F32)
        conv_vec, chan_vec, head_vec = (
            rows_of(ref) for ref in (r.acc_conv, r.acc_chan, r.acc_head)
        )
        norm_vec = [jnp.sum(r.acc_norm[which], axis=0, keepdims=True) for which in range(2)]
        skip = chan_vec[1:2]
        r.group_vec[me] = jnp.concatenate(
            [
                conv_vec[0:5, inner:],
                skip[:, 0:lane],
                jnp.concatenate([skip[:, lane:], head_vec[0:1]], axis=1),
                jnp.concatenate([head_vec[1:2], zeros], axis=1),
                r.acc_dot[...].T[0:blocks],
            ]
            + [vec[:, at : at + lane] for vec in norm_vec for at in range(0, half, lane)]
            + [jnp.zeros((2, lane), F32)],
            axis=0,
        )

        def group_copy(k):
            sems = (r.group_sems.at[0], r.group_sems.at[1])
            return send(r.group_vec.at[me], r.group_vec.at[me], sems, k, **peers[k])

        for k in range(group - 1):
            group_copy(k).start()

        n_pair, n_cross, n_done = (
            plan.left(table) for table in (plan.pair, plan.cross, plan.done)
        )

        def late_cross(m, _):
            chain.stage_cross(m)
            return 0

        lax.fori_loop(n_cross, max(n_cross, n_pair - 1), late_cross, 0)
        n_cross = max(n_cross, n_pair - 1)
        drained = [n_pair]

        def drain(count=None):
            lo = drained[0]
            hi = plan.total + 1 if count is None else min(plan.total, n_pair + count)
            drained[0] = max(lo, hi)

            def one(m, _):
                @pl.when((m - chain.slots >= n_done) & (m < plan.total))
                def _():
                    chain.stage_done(m - chain.slots)

                @pl.when(m < plan.total)
                def _():
                    chain.stage_pair(m)

                @pl.when(m - 1 >= n_cross)
                def _():
                    chain.stage_cross(m - 1)

                return 0

            lax.fori_loop(lo, max(lo, hi), one, 0)

        if gathers:
            middle = (inner_at + rows) // 2
            for at, (lo, hi) in enumerate(((inner_at, middle), (middle, rows))):
                drain(cfg.stops[at])
                weights[lo:hi] = r.acc_w[lo:hi].astype(BF16)
            drain(cfg.stops[2])
            early.middle()
            late.start()
            drain(cfg.stops[3])
            early.end()
            slice_rows = 2 * ns // group
            for k in range(group):
                lo = k * slice_rows
                r.state_send[k] = r.acc_w[lo : lo + slice_rows, mine].astype(BF16)
            r.step_swap[0] = r.acc_w[step_row:inner_at, mine]

            def state_copy(phase, k):
                peer = peers[k]
                sems = (r.state_sems.at[2 * phase], r.state_sems.at[2 * phase + 1])
                to = peer["row"] * cfg.col_count + peer["col"]
                if phase == 0:
                    return send(r.state_send.at[to], r.state_recv.at[me], sems, k, **peer)
                return send(r.state_all.at[me], r.state_all.at[me], sems, k, **peer)

            step_copy = send(
                r.step_swap.at[0],
                r.step_swap.at[1],
                (r.state_sems.at[0], r.state_sems.at[1]),
                group - 1,
                row=1 - row_at,
            )
            for k in range(group - 1):
                state_copy(0, k).start()
            step_copy.start()
            r.state_recv[me] = r.state_send[me]
        drain(cfg.stops[4])

        for k in range(group - 1):
            group_copy(k).wait()
        shared = r.group_vec[0]
        for k in range(1, group):
            shared = shared + r.group_vec[k]
        by_row, by_head = jnp.zeros((3, lane), F32), jnp.zeros((3, lane), F32)
        for k in range(group):
            one = r.group_vec[k]
            same_row, same_col = (k // cfg.col_count) == row_at, (k % cfg.col_count) == col_at
            by_row = by_row + jnp.where(same_row, one[16:19], one[19:22])
            by_head = by_head + jnp.where(same_col, one[5:8], 0.0)
        scale = r.scale[...].T[0:blocks]
        square_sum = r.stats[0, 0:blocks]
        for k in range(1, group):
            square_sum = square_sum + r.stats[k, 0:blocks]
        gate_scale = lax.rsqrt(square_sum / inner_width + EPSILON)
        r.token_out[...] = jnp.concatenate(
            [scale, shared[8:16] * scale * scale / width, gate_scale], axis=0
        )
        norm_sum = jnp.concatenate([by_row[at : at + 1] for at in range(half // lane)], axis=1)
        norm_sum = norm_sum / r.gain_own[...]
        skip_sum = jnp.concatenate([by_head[0:1], by_head[1:2, 0:128]], axis=1)
        r.dp_vec[0] = jnp.concatenate(
            [
                jnp.concatenate([conv_vec[0:5, 0:inner], shared[0:5]], axis=1),
                jnp.concatenate([chan_vec[0:1], by_head[1:2, 128:], by_head[2:3, 0:128]], axis=1),
                jnp.concatenate([skip_sum, norm_sum[:, 0:lane]], axis=1),
                jnp.concatenate([norm_sum[:, lane:], zeros], axis=1),
            ],
            axis=0,
        )

        def dp_copy(k):
            sems = (r.dp_sems.at[0], r.dp_sems.at[1])
            return send(r.dp_vec.at[0], r.dp_vec.at[k], sems, k - 1, **friends[k - 1])

        if not gathers:
            r.vec_out[...] = r.dp_vec[0]
            drain()
        else:
            for k in range(1, 4):
                dp_copy(k).start()
            drain(cfg.stops[5])
            for k in range(group - 1):
                state_copy(0, k).wait()
            summed = r.state_recv[0].astype(F32)
            for k in range(1, group):
                summed = summed + r.state_recv[k].astype(F32)
            r.state_all[me] = summed.astype(BF16)
            for k in range(group - 1):
                state_copy(1, k).start()
            step_copy.wait()
            r.g_step[...] = r.step_swap[0] + r.step_swap[1]
            drain(cfg.stops[6])
            late.middle()
            drain(cfg.stops[7])
            for k in range(1, 4):
                dp_copy(k).wait()
            ordered = [lax.rem(dp_at - k + 4, 4) for k in range(4)]
            total = r.dp_vec[ordered[0]]
            for k in range(1, 4):
                total = total + r.dp_vec[ordered[k]]
            r.vec_out[...] = total
            drain(cfg.stops[8])
            late.end()
            r.g_inner[...] = r.acc_w[inner_at:gate_at, mine]
            r.g_gate[...] = r.acc_w[gate_at:out_at, mine]
            r.g_out[...] = r.acc_w[out_at:, mine]
            drain()
            for k in range(group - 1):
                state_copy(1, k).wait()
            whole_state = [r.state_all[k].astype(F32) for k in range(group)]
            r.g_state[...] = jnp.concatenate(whole_state, axis=0).T
            early.finish()
            late.finish()
        last_done = max(n_done, plan.total - chain.slots)

        def settle(m, _):
            chain.stage_done(m)
            return 0

        lax.fori_loop(last_done, plan.total, settle, 0)
        chain.totals()
        for m in range(plan.total - chain.out_slots, plan.total):
            chain.exchange(m).wait_send()

    @pl.when(scans == 1)
    def _():
        scan_step()

    if gathers:
        for g, at in ((2, FORWARD_AT[0]), (3, FORWARD_AT[1])):

            @pl.when(step_at == at)
            def _(g=g):
                gather.forward(g)

    @pl.when((scans == 0) & ~goes_down)
    def _():
        out_step()

    @pl.when(step_at == 2 * blocks - 1)
    def _():
        for k in range(group - 1):
            stat_copy(k).start()
        gain_swap.wait_send()
        for b in range(blocks):
            swap(0, b).wait_send()
            swap(1, b).wait_send()
        if gathers:
            gather.finish()

    @pl.when(step_at >= 2 * blocks)
    def _():
        backward_step()

    @pl.when(step_at == 3 * blocks - 1)
    def _():
        ending()


def walk(step, blocks):
    def flag(test):
        return test.astype(jnp.int32)

    mixed = blocks - AHEAD
    at = step - AHEAD
    early = flag(at < 0)
    late = flag(at >= 2 * mixed)
    down = flag(step >= 2 * blocks)
    turn = (1 - early) * (1 - late)
    ahead = at + early * AHEAD
    odd = turn * lax.rem(ahead, 2)
    pair = lax.div(ahead, 2)
    block = (
        early * step
        + turn * (pair + odd * AHEAD)
        + late * (1 - down) * (step - blocks)
        + down * (3 * blocks - 1 - step)
    )
    return early + odd, block


def conv_args(r, conv, aux, b, q):
    rows = conv.shape[0]
    joined = r.pre[:, pl.ds(pl.multiple_of(b * q, q), q + 128)]
    arg = conv[:, 4:5] + conv[:, 3:4] * joined[:, 128:]
    for offset in range(1, 4):
        arg = arg + conv[:, 3 - offset : 4 - offset] * (
            aux[offset - 1 : offset] * joined[:, 128 - offset : 128 - offset + q]
        )
    return arg


def finish_kernel(
    nh,
    x_ref,
    c_ref,
    out_total,
    dn_total,
    tokens,
    gain_own,
    vectors,
    decay_log,
    g_inner,
    g_gate,
    g_out,
    g_state,
    g_step,
    output,
    grad_inputs,
    inner_grad,
    gate_grad,
    out_grad,
    state_grad,
    step_grad,
    norm_grad,
    conv_inner,
    bias_inner,
    conv_state,
    bias_state,
    step_bias,
    decay_grad,
    skip_grad,
    gate_norm,
):
    at = pl.program_id(0)
    blocks = tokens.shape[0] // 3
    steps = pl.num_programs(0)
    cols = []
    for part in range(blocks // steps):
        b = at * (blocks // steps) + part
        rows = [tokens[pl.ds(k * blocks + b, 1)] for k in range(3)]
        cols.append(columns_of(jnp.concatenate(rows, axis=0)))
    cols = jnp.concatenate(cols, axis=0)
    scale, pull, gate_scale = (cols[:, k : k + 1] for k in range(3))
    plain = x_ref[...].astype(F32)
    output[...] = (plain + gate_scale * out_total[...].astype(F32)).astype(BF16)
    weighted = dn_total[...].astype(F32) * gain_own[...].reshape(1, -1)
    grad_inputs[...] = c_ref[...].astype(F32) + scale * weighted - plain * pull
    inner_grad[...] = g_inner[...]
    gate_grad[...] = g_gate[...]
    out_grad[...] = g_out[...]
    state_grad[...] = g_state[...]

    @pl.when(at == 0)
    def _():
        inner = g_inner.shape[0] * steps
        pc = inner // nh
        lane = vectors.shape[1] - inner
        half = gain_own.shape[0]
        vec = vectors[...]
        step_grad[...] = g_step[0:nh]
        norm_grad[...] = jnp.concatenate([vec[6:7, inner:], vec[7:8, 0 : half - lane]], axis=1)[0]
        conv_state[...] = vec[0:4, inner:]
        bias_state[...] = vec[4, inner:]
        skips = []
        for h in range(nh):
            part = vec[:, h * pc : (h + 1) * pc]
            conv_inner[h] = part[0:4]
            bias_inner[h : h + 1] = part[4:5]
            gate_norm[h : h + 1] = part[5:6]
            skips.append(jnp.sum(part[6:7], axis=1, keepdims=True))
        decay = -vec[5:6, inner + 128 : inner + 128 + nh] * jnp.exp(decay_log[...])
        step_bias[...] = vec[5, inner : inner + nh]
        decay_grad[...] = decay[0]
        skip_grad[...] = jnp.concatenate(skips, axis=1)[0]


def per_device(
    inputs,
    segments,
    cotangent,
    norm_gain,
    gate_proj,
    inner_proj,
    state_proj,
    step_proj,
    conv_inner,
    bias_inner,
    conv_state,
    bias_state,
    step_bias,
    decay_log,
    skip_gain,
    gate_norm,
    out_proj,
):
    length, half = inputs.shape
    row_count = lax.axis_size("row")
    col_count = lax.axis_size("col")
    col_at = lax.axis_index("col")
    width = half * row_count
    share, nh, pc = gate_proj.shape
    inner = nh * pc
    state_width = state_proj.shape[1]
    ns = state_width // 2
    conv_rows = inner + state_width
    gate_at = conv_rows + STEP_ROWS
    out_at = gate_at + inner
    rows = out_at + inner
    q = BLOCK_LEN
    blocks = length // q

    def channel_rows(w):
        return jnp.transpose(w, (1, 2, 0)).reshape(inner, share)

    gathers = lax.axis_size("dp") == 4 and share % 128 == 0
    parts = [
        channel_rows(inner_proj),
        state_proj,
        step_proj.T,
        channel_rows(gate_proj),
        channel_rows(out_proj),
    ]
    if not gathers:
        step_rows = jnp.pad(step_proj.T, ((0, STEP_ROWS - nh), (0, 0)))
        parts = [state_proj.T, step_rows, parts[0], parts[3], parts[4]]
        stacked = jnp.concatenate(parts, axis=0).astype(BF16)
        parts = [lax.all_gather(stacked, "dp", axis=1, tiled=True)]
    gain_own = norm_gain[None, :]
    group = row_count * col_count

    units = UNITS
    slots = blocks * units
    cfg = types.SimpleNamespace(
        nh=nh,
        pc=pc,
        ns=ns,
        width=width,
        row_count=row_count,
        col_count=col_count,
        gathers=gathers,
        blocks=blocks,
        units=units,
        early_split=144,
        stops=STOPS,
    )
    plan = Plan(blocks, units, slots, *MODEL)

    def fold(i):
        return walk(i, blocks)[1]

    def whole(*shape):
        return pl.BlockSpec(shape, lambda i: (0,) * len(shape), pipeline_mode=pl.Buffered(1))

    sds, dma, vmem = jax.ShapeDtypeStruct, pltpu.SemaphoreType.DMA, pltpu.VMEM
    anywhere = pl.BlockSpec(memory_space=pl.ANY)
    token_block = pl.BlockSpec((q, half), lambda i: (fold(i), 0))
    ins = {
        "x_own": (inputs, token_block),
        "c_own": (cotangent, token_block),
        "x_any": (inputs, anywhere),
        "c_any": (cotangent, anywhere),
        "gain_in": (norm_gain, whole(half)),
        "seg": (segments, pl.BlockSpec((1, q), lambda i: (0, fold(i)))),
        "conv_in": (jnp.transpose(conv_inner, (1, 0, 2)), whole(nh, 4, pc)),
        "bias_in": (bias_inner, whole(nh, pc)),
        "gate_gain": (gate_norm, whole(nh, pc)),
        "conv_st": (conv_state, whole(4, state_width)),
        "bias_st": (bias_state[None], whole(1, state_width)),
        "step_bias": (step_bias[None], whole(1, nh)),
        "decay_log": (decay_log[None], whole(1, nh)),
        "skip_gain": (skip_gain[None], whole(1, nh)),
    }
    outs = {
        "out_total": (sds((length, half), BF16), anywhere),
        "dn_total": (sds((length, half), BF16), anywhere),
        "token_out": (sds((3 * blocks, q), F32), whole(3 * blocks, q)),
        "vec_out": (sds((8, conv_rows), F32), whole(8, conv_rows)),
    }
    scratch = {
        "acc_w": vmem((rows, width), F32),
        "x_scr": vmem((blocks, q, half), BF16),
        "c_scr": vmem((blocks, q, half), BF16),
        "gain_own": vmem((1, half), F32),
        "gain_sib": vmem((1, half), F32),
        "conv": vmem((conv_rows, 128), F32),
        "head": vmem((STEP_ROWS, 128), F32),
        "prev_seg": vmem((1, 128), F32),
        "pre": vmem((conv_rows, length + 128), F32),
        "step": vmem((STEP_ROWS, length), F32),
        "gate": vmem((inner, length), BF16),
        "mixed": vmem((inner, length), F32),
        "dng": vmem((inner, length), BF16),
        "aux": vmem((8, length), F32),
        "scale": vmem((q, 128), F32),
        "states": vmem((blocks, inner, ns), F32),
        "state": vmem((inner, ns), F32),
        "stats": vmem((group, 2 * blocks, q), F32),
        "work": vmem((inner, q), F32),
        "slope": vmem((conv_rows, q), F32),
        "low": vmem((out_at, q), BF16),
        "after": vmem((3, conv_rows, 128), F32),
        "acc_conv": vmem((5, conv_rows, 128), F32),
        "acc_chan": vmem((2, inner, 128), F32),
        "acc_head": vmem((2, STEP_ROWS, 128), F32),
        "acc_norm": vmem((2, 8, half), F32),
        "acc_dot": vmem((q, 128), F32),
        "group_vec": vmem((group, 24, 2 * ns), F32),
        "dp_vec": vmem((4, 8, conv_rows), F32),
        "ch_own": vmem((2 * units, q // units, half), BF16),
        "ch_sib": vmem((2 * units, q // units, half), BF16),
        "ch_first": vmem((slots, q // units, half), BF16),
        "ch_pair": vmem((slots, q // units, half), BF16),
        "ch_cross": vmem((slots, q // units, half), BF16),
        "cs_send": dma((3, slots)),
        "cs_recv": dma((3, slots)),
        "cs_out": dma((2, plan.total)),
        "cs_keep": dma((slots,)),
        "ch_free": pltpu.SemaphoreType.REGULAR((3,)),
        "swap_sems": dma((4, blocks + 1)),
        "stat_sems": dma((2, group - 1)),
        "group_sems": dma((2, group - 1)),
        "dp_sems": dma((2, 3)),
    }
    if gathers:
        for name, part in zip(("inner_w", "state_w", "step_w", "gate_w", "out_w"), parts):
            ins[name] = (part, whole(*part.shape) if name == "step_w" else anywhere)
        grad_shape = sds((inner, share), F32)
        outs["g_inner"] = (grad_shape, whole(inner, share))
        outs["g_gate"] = (grad_shape, whole(inner, share))
        outs["g_out"] = (grad_shape, whole(inner, share))
        outs["g_state"] = (sds((share, state_width), F32), whole(share, state_width))
        outs["g_step"] = (sds((STEP_ROWS, share), F32), whole(STEP_ROWS, share))
        pieces = (group, state_width // group, share)
        early_rows = state_width + STEP_ROWS
        late_half = (rows - early_rows) // 2
        scratch.update(
            weights=vmem((rows, width), BF16),
            gather_sems=dma((8, 4)),
            raw_sems=dma((4,)),
            ea_top=vmem((2, cfg.early_split, share), BF16),
            ea_low=vmem((2, early_rows - cfg.early_split, share), BF16),
            ea_top_last=vmem((cfg.early_split, share), BF16),
            ea_low_last=vmem((early_rows - cfg.early_split, share), BF16),
            ea_sems=dma((4, 3)),
            rs_top=vmem((2, late_half, share), BF16),
            rs_low=vmem((2, late_half, share), BF16),
            rs_top_last=vmem((late_half, share), BF16),
            rs_low_last=vmem((late_half, share), BF16),
            rs_sems=dma((4, 3)),
            step_swap=vmem((2, STEP_ROWS, share), F32),
            state_send=vmem(pieces, BF16),
            state_recv=vmem(pieces, BF16),
            state_all=vmem(pieces, BF16),
            state_sems=dma((4, group)),
        )
    else:
        ins["weights"] = (parts[0], whole(rows, width))
        outs["grad_w"] = (sds((rows, width), BF16), whole(rows, width))
    names = (*ins, *outs, *scratch)
    results = pl.pallas_call(
        functools.partial(layer_kernel, cfg, plan, names),
        name="layer",
        grid=(3 * blocks,),
        in_specs=[spec for _, spec in ins.values()],
        out_specs=[spec for _, spec in outs.values()],
        out_shape=[shape for shape, _ in outs.values()],
        scratch_shapes=list(scratch.values()),
        compiler_params=pltpu.CompilerParams(
            vmem_limit_bytes=VMEM_LIMIT, collective_id=1, has_side_effects=True
        ),
        cost_estimate=pl.CostEstimate(
            flops=6 * length * width * rows,
            bytes_accessed=60 << 20,
            transcendentals=2 * nh * length * q,
        ),
    )(*(array for array, _ in ins.values()))
    made = types.SimpleNamespace(**dict(zip(outs, results, strict=True)))
    if gathers:
        return finish(nh, blocks, made, inputs, cotangent, norm_gain, decay_log[None], ns)
    tokens = made.token_out.reshape(3, length)
    scale, pull, gate_scale = (tokens[k][:, None] for k in range(3))
    plain = inputs.astype(F32)
    output = (plain + gate_scale * made.out_total.astype(F32)).astype(BF16)
    weighted = made.dn_total.astype(F32) * gain_own
    grad_inputs = cotangent.astype(F32) + scale * weighted - plain * pull
    vectors = made.vec_out
    grads = lax.psum_scatter(made.grad_w, "dp", scatter_dimension=1, tiled=True)
    grads = grads.astype(F32)
    vectors = lax.psum(vectors, "dp")
    g_state = lax.psum(grads[0:state_width], ("row", "col")).T
    g_step = lax.psum(grads[state_width : state_width + STEP_ROWS], "row")
    g_inner = grads[state_width + STEP_ROWS : gate_at]
    g_gate = grads[gate_at:out_at]
    g_out = grads[out_at:]

    def feature_rows(w):
        return jnp.transpose(w.reshape(nh, pc, share), (2, 0, 1))

    channel_vecs = vectors[:, 0:inner].reshape(8, nh, pc)
    grad_norm = jnp.concatenate([vectors[6, inner:], vectors[7, : half - 2 * ns]])
    return (
        output,
        grad_inputs,
        grad_norm,
        feature_rows(g_gate),
        feature_rows(g_inner),
        g_state,
        g_step[:nh].T,
        channel_vecs[0:4],
        channel_vecs[4],
        vectors[0:4, inner:],
        vectors[4, inner:],
        vectors[5, inner : inner + nh],
        -vectors[5, inner + 128 : inner + 128 + nh] * jnp.exp(decay_log),
        jnp.sum(channel_vecs[6], axis=1),
        channel_vecs[5],
        feature_rows(g_out),
    )


def finish(nh, blocks, made, inputs, cotangent, gain_own, decay_log, ns):
    length, half = inputs.shape
    inner, share = made.g_inner.shape
    pc = inner // nh
    q = length // blocks
    steps = FINISH_STEPS
    sds = jax.ShapeDtypeStruct

    def whole(*shape):
        return pl.BlockSpec(shape, lambda i: (0,) * len(shape))

    tokens = pl.BlockSpec((length // steps, half), lambda i: (i, 0))
    rows = pl.BlockSpec((inner // steps, share), lambda i: (i, 0))
    state_rows = pl.BlockSpec((share // steps, 2 * ns), lambda i: (i, 0))
    grad = sds((inner, share), F32)
    (
        output,
        grad_inputs,
        g_inner,
        g_gate,
        g_out,
        g_state,
        g_step,
        norm,
        conv_inner,
        bias_inner,
        conv_state,
        bias_state,
        step_bias,
        decay,
        skip,
        gate_norm,
    ) = pl.pallas_call(
        functools.partial(finish_kernel, nh),
        name="finish",
        grid=(steps,),
        in_specs=[
            tokens,
            tokens,
            tokens,
            tokens,
            whole(3 * blocks, q),
            whole(half),
            whole(*made.vec_out.shape),
            whole(1, nh),
            rows,
            rows,
            rows,
            state_rows,
            whole(STEP_ROWS, share),
        ],
        out_specs=[
            tokens,
            tokens,
            rows,
            rows,
            rows,
            state_rows,
            whole(nh, share),
            whole(half),
            whole(nh, 4, pc),
            whole(nh, pc),
            whole(4, 2 * ns),
            whole(2 * ns),
            whole(nh),
            whole(nh),
            whole(nh),
            whole(nh, pc),
        ],
        out_shape=[
            sds((length, half), BF16),
            sds((length, half), F32),
            grad,
            grad,
            grad,
            sds((share, 2 * ns), F32),
            sds((nh, share), F32),
            sds((half,), F32),
            sds((nh, 4, pc), F32),
            sds((nh, pc), F32),
            sds((4, 2 * ns), F32),
            sds((2 * ns,), F32),
            sds((nh,), F32),
            sds((nh,), F32),
            sds((nh,), F32),
            sds((nh, pc), F32),
        ],
        compiler_params=pltpu.CompilerParams(vmem_limit_bytes=VMEM_LIMIT),
    )(
        inputs,
        cotangent,
        made.out_total,
        made.dn_total,
        made.token_out,
        gain_own,
        made.vec_out,
        decay_log,
        made.g_inner,
        made.g_gate,
        made.g_out,
        made.g_state,
        made.g_step,
    )

    def feature_rows(w):
        return jnp.transpose(w.reshape(nh, pc, share), (2, 0, 1))

    return (
        output,
        grad_inputs,
        norm,
        feature_rows(g_gate),
        feature_rows(g_inner),
        g_state,
        g_step.T,
        jnp.transpose(conv_inner, (1, 0, 2)),
        bias_inner,
        conv_state,
        bias_state,
        step_bias,
        decay,
        skip,
        gate_norm,
        feature_rows(g_out),
    )


def solution(mesh):
    return jax.shard_map(
        per_device,
        mesh=mesh,
        in_specs=(
            P("dp", "row"),
            P("dp", None),
            P("dp", "row"),
            P("row"),
            P("dp", "col", "row"),
            P("dp", "col", "row"),
            P("dp", None),
            P("dp", "col"),
            P(None, "col", "row"),
            P("col", "row"),
            P(),
            P(),
            P("col"),
            P("col"),
            P("col"),
            P("col", "row"),
            P("dp", "col", "row"),
        ),
        out_specs=(
            P("dp", "row"),
            P("dp", "row"),
            P("row"),
            P("dp", "col", "row"),
            P("dp", "col", "row"),
            P("dp", None),
            P("dp", "col"),
            P(None, "col", "row"),
            P("col", "row"),
            P(),
            P(),
            P("col"),
            P("col"),
            P("col"),
            P("col", "row"),
            P("dp", "col", "row"),
        ),
        check_vma=False,
    )
```
